32 devices in a mesh: dp: 8 (over y, x, core), mp: 4 (over z).
Axes of the slice: x: 2, y: 2, z: 4, core: 2. Of those that a mesh axis runs over, the one named last changes fastest.
Arguments:
- text_tokens: bfloat16 [64, 128, 768], P(('dp', 'mp')), may hold values from -6 to 6
- image_regions: bfloat16 [64, 36, 1024], P(('dp', 'mp')), may hold values from -6 to 6
- lengths: int32 [64], P(('dp', 'mp')), may hold values from 8 to 128
- region_counts: int32 [64], P(('dp', 'mp')), may hold values from 10 to 36
- text_cross: bfloat16 [3, 768, 1024], P(None, None, 'mp'), may hold values from -0.21875 to 0.21875
- image_cross: bfloat16 [3, 1024, 1024], P(None, None, 'mp'), may hold values from -0.1875 to 0.1875
- text_cross_out: bfloat16 [1024, 768], P('mp'), may hold values from -0.5 to 0.5
- image_cross_out: bfloat16 [1024, 1024], P('mp'), may hold values from -0.5 to 0.5
- text_up: bfloat16 [768, 3072], P(None, 'mp'), may hold values from -0.21875 to 0.21875
- text_down: bfloat16 [3072, 768], P('mp'), may hold values from -0.15625 to 0.15625
- image_up: bfloat16 [1024, 1024], P(None, 'mp'), may hold values from -0.1875 to 0.1875
- image_down: bfloat16 [1024, 1024], P('mp'), may hold values from -0.25 to 0.25
- text_self: bfloat16 [3, 768, 768], P(None, None, 'mp'), may hold values from -0.21875 to 0.21875
- text_self_out: bfloat16 [768, 768], P('mp'), may hold values from -0.625 to 0.625
- image_self: bfloat16 [3, 1024, 1024], P(None, None, 'mp'), may hold values from -0.1875 to 0.1875
- image_self_out: bfloat16 [1024, 1024], P('mp'), may hold values from -0.5 to 0.5
- text_gains: float32 [3, 768], replicated, may hold values from 0.5 to 1.5
- text_shifts: float32 [3, 768], replicated, may hold values from -1.75 to 1.75
- image_gains: float32 [3, 1024], replicated, may hold values from 0.5 to 1.5
- image_shifts: float32 [3, 1024], replicated, may hold values from -1.75 to 1.75
- text_cotangent: bfloat16 [64, 128, 768], P(('dp', 'mp')), may hold values from -6 to 6
- image_cotangent: bfloat16 [64, 36, 1024], P(('dp', 'mp')), may hold values from -6 to 6
Outputs:
- text_output: float32 [64, 128, 768], P(('dp', 'mp'))
- image_output: float32 [64, 36, 1024], P(('dp', 'mp'))
- text_grad: float32 [64, 128, 768], P(('dp', 'mp'))
- image_grad: float32 [64, 36, 1024], P(('dp', 'mp'))
- text_cross_grad: float32 [3, 768, 1024], P(None, 'dp', 'mp')
- image_cross_grad: float32 [3, 1024, 1024], P(None, 'dp', 'mp')
- text_cross_out_grad: float32 [1024, 768], P('mp', 'dp')
- image_cross_out_grad: float32 [1024, 1024], P('mp', 'dp')
- text_up_grad: float32 [768, 3072], P('dp', 'mp')
- text_down_grad: float32 [3072, 768], P('mp', 'dp')
- image_up_grad: float32 [1024, 1024], P('dp', 'mp')
- image_down_grad: float32 [1024, 1024], P('mp', 'dp')
- text_self_grad: float32 [3, 768, 768], P(None, 'dp', 'mp')
- text_self_out_grad: float32 [768, 768], P('mp', 'dp')
- image_self_grad: float32 [3, 1024, 1024], P(None, 'dp', 'mp')
- image_self_out_grad: float32 [1024, 1024], P('mp', 'dp')
- text_gains_grad: float32 [3, 768], replicated
- text_shifts_grad: float32 [3, 768], replicated
- image_gains_grad: float32 [3, 1024], replicated
- image_shifts_grad: float32 [3, 1024], replicated
The draws below stay inside these ranges and needn't reach their ends.
Inputs may be any that keep to these rules, and one draw needn't show every extreme that they name: `lengths`: text slots at or beyond a pair's length are padding and are never attended to. `region_counts`: image regions at or beyond a pair's count are padding and are never attended to.
All inputs are finite; a program needn't handle non-finite values.
Results may differ from the reference program's by a relative error of at most 0.039.
Values may be sent and summed in bfloat16 or wider, within the bound.
A program may use at most 192 MiB of HBM per device.

```python
import math
import jax
import jax.numpy as jnp
from jax import lax

DT = 768
DV = 1024
INNER = 1024
FT = 3072
FV = 1024
TEXT_HEAD = 64
CROSS_HEAD = 128
IMAGE_HEAD = 128
SLOTS = 128
REGIONS = 36
PAIRS = 64


def set_ends(result, rng, smallest, largest):
    shape = result.shape
    place = [jax.random.randint(jax.random.fold_in(rng, axis), (), 0, shape[axis]) for axis in range(len(shape))]
    result = result.at[tuple(place)].set(smallest)
    longest = shape.index(max(shape))
    place[longest] = (place[longest] + 1) % shape[longest]
    return result.at[tuple(place)].set(largest)


def block_scale(own_key, extent, cuts, low, largest):
    loudness, own = 1.0, jax.random.fold_in(own_key, 6)
    for dim, parts in cuts:
        steps = jnp.exp(jax.random.uniform(jax.random.fold_in(own, dim), (parts,), jnp.float32, low / len(cuts), largest / len(cuts)))
        loudness = loudness * jnp.repeat(steps, extent[dim] // parts).reshape([-1 if axis == dim else 1 for axis in range(len(extent))])
    return loudness


def bell_draw(own_key, dims, scale, most, shards=(), held_as=jnp.bfloat16):
    factor_of = block_scale(own_key, dims, shards, -0.22, 0.18) if shards else 1.0
    values = jax.random.normal(own_key, dims, jnp.float32) * scale * factor_of
    return jnp.minimum(jnp.maximum(values, -most), most).astype(held_as)


def setup_inputs(seed: int = 0) -> dict:
    keys = jax.random.split(jax.random.key(seed), 23)
    text_tokens = bell_draw(keys[0], (PAIRS, SLOTS, DT), 1.0, 6.0, ((0, 32),))
    image_regions = bell_draw(keys[1], (PAIRS, REGIONS, DV), 1.0, 6.0, ((0, 32),))
    lengths = set_ends(jax.random.randint(keys[2], (PAIRS,), max(1, SLOTS // 16), SLOTS + 1), jax.random.fold_in(keys[2], 1), max(1, SLOTS // 16), SLOTS).astype(jnp.int32)
    region_counts = set_ends(jax.random.randint(keys[3], (PAIRS,), max(1, REGIONS * 5 // 18), REGIONS + 1), jax.random.fold_in(keys[3], 1), max(1, REGIONS * 5 // 18), REGIONS).astype(jnp.int32)
    text_cross = bell_draw(keys[4], (3, DT, INNER), DT ** -0.5, 0.21875, ((2, 4),))
    image_cross = bell_draw(keys[5], (3, DV, INNER), DV ** -0.5, 0.1875, ((2, 4),))
    text_cross_out = bell_draw(keys[6], (INNER, DT), (INNER // 8) ** -0.5, 0.5, ((0, 4),))
    image_cross_out = bell_draw(keys[7], (INNER, DV), (INNER // 8) ** -0.5, 0.5, ((0, 4),))
    text_up = bell_draw(keys[8], (DT, FT), DT ** -0.5, 0.21875, ((1, 4),))
    text_down = bell_draw(keys[9], (FT, DT), (FT // 2) ** -0.5, 0.15625, ((0, 4),))
    image_up = bell_draw(keys[10], (DV, FV), DV ** -0.5, 0.1875, ((1, 4),))
    image_down = bell_draw(keys[11], (FV, DV), (FV // 2) ** -0.5, 0.25, ((0, 4),))
    text_self = bell_draw(keys[12], (3, DT, DT), DT ** -0.5, 0.21875, ((2, 4),))
    text_self_out = bell_draw(keys[13], (DT, DT), (DT // 8) ** -0.5, 0.625, ((0, 4),))
    image_self = bell_draw(keys[14], (3, DV, DV), DV ** -0.5, 0.1875, ((2, 4),))
    image_self_out = bell_draw(keys[15], (DV, DV), (DV // 8) ** -0.5, 0.5, ((0, 4),))
    text_gains = jnp.clip(1.0 + 0.1 * jax.random.normal(keys[16], (3, DT), jnp.float32), 0.5, 1.5)
    text_shifts = bell_draw(keys[17], (3, DT), 0.3, 1.75, (), jnp.float32)
    image_gains = jnp.clip(1.0 + 0.1 * jax.random.normal(keys[18], (3, DV), jnp.float32), 0.5, 1.5)
    image_shifts = bell_draw(keys[19], (3, DV), 0.3, 1.75, (), jnp.float32)
    text_cotangent = bell_draw(keys[20], (PAIRS, SLOTS, DT), 1.0, 6.0, ((0, 32),))
    image_cotangent = bell_draw(keys[21], (PAIRS, REGIONS, DV), 1.0, 6.0, ((0, 32),))
    return dict(text_tokens=text_tokens, image_regions=image_regions, lengths=lengths, region_counts=region_counts, text_cross=text_cross, image_cross=image_cross, text_cross_out=text_cross_out, image_cross_out=image_cross_out, text_up=text_up, text_down=text_down, image_up=image_up, image_down=image_down, text_self=text_self, text_self_out=text_self_out, image_self=image_self, image_self_out=image_self_out, text_gains=text_gains, text_shifts=text_shifts, image_gains=image_gains, image_shifts=image_shifts, text_cotangent=text_cotangent, image_cotangent=image_cotangent)


EPSILON = 1e-05
MASKED = -1e+30
HIGHEST = lax.Precision.HIGHEST

@jax.custom_vjp
def low(v):
    return lax.optimization_barrier(v.astype(jnp.bfloat16)).astype(jnp.float32)

@jax.custom_vjp
def low_back(v):
    return v

def low_keep(v):
    return (low(v), None)

def low_pass(kept, grad):
    return (grad,)

def back_keep(v):
    return (v, None)

def back_low(kept, grad):
    return (low(grad),)
low.defvjp(low_keep, low_pass)
low_back.defvjp(back_keep, back_low)

def rounded(value):
    return low_back(low(value))

def project(inputs, weight):
    return jnp.matmul(inputs, weight, precision=HIGHEST)

def layer_norm(hidden, scales, offsets):
    average = lax.optimization_barrier(jnp.mean(hidden, -1, keepdims=True))
    centred = hidden - average
    spread = lax.optimization_barrier(jnp.mean(centred * centred, -1, keepdims=True))
    return centred * lax.rsqrt(spread + EPSILON) * scales + offsets

def attend(queries, key_rows, value_rows, visible, head_size):
    pair_count, query_count, inner_width = queries.shape
    key_count = key_rows.shape[1]
    head_count = inner_width // head_size
    query_heads = rounded(queries).reshape(pair_count, query_count, head_count, head_size)
    key_heads = rounded(key_rows).reshape(pair_count, key_count, head_count, head_size)
    value_heads = rounded(value_rows).reshape(pair_count, key_count, head_count, head_size)
    scores = jnp.einsum('plhe,pmhe->phlm', query_heads, key_heads, precision=HIGHEST) / math.sqrt(head_size)
    scores = low_back(jnp.where(visible[:, None, None, :], scores, MASKED))
    probs = jax.nn.softmax(scores, axis=-1)
    context = jnp.einsum('phlm,pmhe->plhe', low(probs), value_heads, precision=HIGHEST)
    return rounded(context.reshape(pair_count, query_count, inner_width))

def ffn_block(inputs, up_weight, down_weight, scales, offsets):
    upper = low_back(project(low(inputs), up_weight))
    branch = low_back(project(low(jax.nn.gelu(upper, approximate=False)), down_weight))
    return layer_norm(inputs + branch, scales, offsets)

def self_block(inputs, weights, out_weight, visible, head_size, scales, offsets):
    lowered = low(inputs)
    context = attend(project(lowered, weights[0]), project(lowered, weights[1]), project(lowered, weights[2]), visible, head_size)
    branch = low_back(project(context, out_weight))
    return layer_norm(inputs + branch, scales, offsets)

def layer(text_state, image_state, params, text_seen, image_seen):
    text_cross, image_cross, text_cross_out, image_cross_out, text_up, text_down, image_up, image_down, text_self, text_self_out, image_self, image_self_out, text_gains, text_shifts, image_gains, image_shifts = params
    text_low = low(text_state)
    image_low = low(image_state)
    text_query = project(text_low, text_cross[0])
    text_key = project(text_low, text_cross[1])
    text_value = project(text_low, text_cross[2])
    image_query = project(image_low, image_cross[0])
    image_key = project(image_low, image_cross[1])
    image_value = project(image_low, image_cross[2])
    text_context = attend(text_query, image_key, image_value, image_seen, CROSS_HEAD)
    image_context = attend(image_query, text_key, text_value, text_seen, CROSS_HEAD)
    text_mid = layer_norm(text_state + low_back(project(text_context, text_cross_out)), text_gains[0], text_shifts[0])
    image_mid = layer_norm(image_state + low_back(project(image_context, image_cross_out)), image_gains[0], image_shifts[0])
    text_mixed = ffn_block(text_mid, text_up, text_down, text_gains[1], text_shifts[1])
    image_mixed = ffn_block(image_mid, image_up, image_down, image_gains[1], image_shifts[1])
    text_final = self_block(text_mixed, text_self, text_self_out, text_seen, TEXT_HEAD, text_gains[2], text_shifts[2])
    image_final = self_block(image_mixed, image_self, image_self_out, image_seen, IMAGE_HEAD, image_gains[2], image_shifts[2])
    return (text_final, image_final)

def reference(text_tokens, image_regions, lengths, region_counts, text_cross, image_cross, text_cross_out, image_cross_out, text_up, text_down, image_up, image_down, text_self, text_self_out, image_self, image_self_out, text_gains, text_shifts, image_gains, image_shifts, text_cotangent, image_cotangent):
    params = tuple((weight.astype(jnp.float32) for weight in (text_cross, image_cross, text_cross_out, image_cross_out, text_up, text_down, image_up, image_down, text_self, text_self_out, image_self, image_self_out, text_gains, text_shifts, image_gains, image_shifts)))
    group_size = math.gcd(PAIRS, 16)
    group_count = PAIRS // group_size

    def blocks(array):
        return array.reshape((group_count, group_size) + array.shape[1:])

    def flatten(array):
        return array.reshape((PAIRS,) + array.shape[2:])

    def one_group(totals, carried):
        text_state, image_state, text_length, image_length, text_back, image_back = carried
        text_seen = jnp.arange(SLOTS, dtype=jnp.int32)[None, :] < text_length[:, None]
        image_seen = jnp.arange(REGIONS, dtype=jnp.int32)[None, :] < image_length[:, None]

        def forward(text_arg, image_arg, weights):
            return layer(text_arg, image_arg, weights, text_seen, image_seen)
        outputs, pullback = jax.vjp(forward, text_state, image_state, params)
        text_grad, image_grad, weight_grads = pullback((text_back, image_back))
        totals = jax.tree.map(jnp.add, totals, weight_grads)
        return (totals, (outputs[0], outputs[1], text_grad, image_grad))
    initial = jax.tree.map(jnp.zeros_like, params)
    totals, results = lax.scan(one_group, initial, (blocks(text_tokens.astype(jnp.float32)), blocks(image_regions.astype(jnp.float32)), blocks(lengths), blocks(region_counts), blocks(text_cotangent.astype(jnp.float32)), blocks(image_cotangent.astype(jnp.float32))))
    return (flatten(results[0]), flatten(results[1]), flatten(results[2]), flatten(results[3]), totals[0], totals[1], totals[2], totals[3], totals[4], totals[5], totals[6], totals[7], totals[8], totals[9], totals[10], totals[11], totals[12], totals[13], totals[14], totals[15])
```

```python
import functools
import math

import jax
import jax.numpy as jnp
from jax import lax
from jax.experimental import pallas as pl
from jax.experimental.pallas import tpu as pltpu
from jax.sharding import PartitionSpec as P

TEXT_HEAD = 64
CROSS_HEAD = 128
IMAGE_HEAD = 128


EPSILON = 1e-05
MASKED = -1e30


def project(inputs, weight):
    return jnp.dot(inputs, weight, preferred_element_type=jnp.float32)


def project_back(gradient, weight):
    return lax.dot_general(
        gradient,
        weight,
        (((gradient.ndim - 1,), (1,)), ((), ())),
        preferred_element_type=jnp.float32,
    )


def layer_norm(hidden, scales, offsets):
    average = jnp.mean(hidden, -1, keepdims=True)
    centred = hidden - average
    spread = jnp.mean(centred * centred, -1, keepdims=True)
    return centred * lax.rsqrt(spread + EPSILON) * scales + offsets


def norm_back(hidden, scales, offsets, gradient):
    unused, pullback = jax.vjp(layer_norm, hidden, scales, offsets)
    return pullback(gradient)


def gelu_exact(values):
    return jax.nn.gelu(values, approximate=False)


def split_heads(rows, head_size):
    return rows.reshape(rows.shape[0], rows.shape[1], rows.shape[2] // head_size, head_size)


def scores_of(query_heads, key_heads, visible, head_size):
    scores = jnp.einsum(
        "plhe,pmhe->phlm", query_heads, key_heads, preferred_element_type=jnp.float32
    ) / math.sqrt(head_size)
    return jnp.where(visible[:, None, None, :], scores, MASKED)


def attend(queries, key_rows, value_rows, visible, head_size):
    scores = scores_of(
        split_heads(queries, head_size), split_heads(key_rows, head_size), visible, head_size
    )
    highest = jnp.max(scores, -1, keepdims=True)
    log_total = highest + jnp.log(jnp.sum(jnp.exp(scores - highest), -1, keepdims=True))
    probs = jnp.exp(scores - log_total).astype(jnp.bfloat16)
    context = jnp.einsum(
        "phlm,pmhe->plhe",
        probs,
        split_heads(value_rows, head_size),
        preferred_element_type=jnp.float32,
    )
    return (context.reshape(queries.shape).astype(jnp.bfloat16), log_total)


def attend_back(queries, key_rows, value_rows, visible, head_size, log_total, context_grad):
    query_heads = split_heads(queries, head_size)
    key_heads = split_heads(key_rows, head_size)
    value_heads = split_heads(value_rows, head_size)
    grad_heads = split_heads(context_grad, head_size)
    probs = jnp.exp(scores_of(query_heads, key_heads, visible, head_size) - log_total)
    value_grad = jnp.einsum(
        "phlm,plhe->pmhe",
        probs.astype(jnp.bfloat16),
        grad_heads,
        preferred_element_type=jnp.float32,
    )
    prob_grad = jnp.einsum(
        "plhe,pmhe->phlm", grad_heads, value_heads, preferred_element_type=jnp.float32
    )
    inner = jnp.sum(probs * prob_grad, -1, keepdims=True)
    score_grad = (probs * (prob_grad - inner)).astype(jnp.bfloat16)
    query_grad = jnp.einsum(
        "phlm,pmhe->plhe", score_grad, key_heads, preferred_element_type=jnp.float32
    ) / math.sqrt(head_size)
    key_grad = jnp.einsum(
        "phlm,plhe->pmhe", score_grad, query_heads, preferred_element_type=jnp.float32
    ) / math.sqrt(head_size)
    return (
        query_grad.reshape(queries.shape).astype(jnp.bfloat16),
        key_grad.reshape(key_rows.shape).astype(jnp.bfloat16),
        value_grad.reshape(value_rows.shape).astype(jnp.bfloat16),
    )


def project_three(group_rows, weights):
    return tuple((project(group_rows, weights[number]).astype(jnp.bfloat16) for number in range(3)))


def input_part(grads, weights):
    return (
        project_back(grads[0], weights[0])
        + project_back(grads[1], weights[1])
        + project_back(grads[2], weights[2])
    )


def cross_forward(text_group, image_group, text_cross, image_cross, text_mask, image_mask):
    text_proj = project_three(text_group, text_cross)
    image_proj = project_three(image_group, image_cross)
    text_context, text_total = attend(
        text_proj[0], image_proj[1], image_proj[2], image_mask, CROSS_HEAD
    )
    image_context, image_total = attend(
        image_proj[0], text_proj[1], text_proj[2], text_mask, CROSS_HEAD
    )
    return (text_proj, image_proj, (text_context, image_context), (text_total, image_total))


def ffn_forward(group_rows, up_weight, down_weight):
    upper = project(group_rows, up_weight)
    middle = gelu_exact(upper).astype(jnp.bfloat16)
    return (upper, middle, project(middle, down_weight))


def ffn_back(upper, up_weight, down_weight, coming):
    middle_grad = project_back(coming, down_weight)
    unused, pullback = jax.vjp(gelu_exact, upper)
    upper_grad = pullback(middle_grad)[0].astype(jnp.bfloat16)
    return (upper_grad, project_back(upper_grad, up_weight))


def self_forward(group_rows, weights, out_weight, visible, head_size):
    proj = project_three(group_rows, weights)
    context, log_total = attend(proj[0], proj[1], proj[2], visible, head_size)
    return (proj, context, log_total, project(context, out_weight))


def self_back(saved, weights, out_weight, visible, head_size, coming):
    proj, context, log_total = (saved[0], saved[1], saved[2])
    context_grad = project_back(coming, out_weight).astype(jnp.bfloat16)
    grads = attend_back(proj[0], proj[1], proj[2], visible, head_size, log_total, context_grad)
    return (grads, input_part(grads, weights))


MESH_ID = pl.DeviceIdType.MESH


def flip(index, step):
    return index + step * (1 - 2 * ((index // step) % 2))


def position():
    data, model = lax.axis_index("dp"), lax.axis_index("mp")
    return data, model, data % 2, (data // 2) % 2, (data // 4) % 2


def greet(data, model):
    barrier = pltpu.get_barrier_semaphore()
    partners = [(flip(data, step), model) for step in (1, 2, 4)]
    partners += [(data, flip(model, step)) for step in (1, 2)]
    for partner in partners:
        pl.semaphore_signal(barrier, inc=1, device_id=partner, device_id_type=MESH_ID)
    pl.semaphore_wait(barrier, len(partners))


def view_of(ref, kind, shard, width, y, x, c):
    if kind == "col3":
        columns = pl.ds(pl.multiple_of(shard * width, 128), width)
        return ref.at[:, y, x, c, :, columns]
    if kind == "col":
        columns = pl.ds(pl.multiple_of(shard * width, 128), width)
        return ref.at[y, x, c, :, columns]
    if kind == "row":
        return ref.at[shard, y, x, c]
    return ref.at[shard, :, y, x, c]


def local_of(ref, kind, y, x, c):
    if kind in ("col3", "split3"):
        return ref.at[:, y, x, c]
    return ref.at[y, x, c]


def gather_kernel(kinds, widths, streams, *refs):
    count = len(kinds)
    ins, outs = refs[:count], refs[count : 2 * count]
    own_sem, send_sem, recv_sem = refs[2 * count :]
    data, model, c, x, y = position()
    every = slice(None)
    near, far = flip(model, 1), flip(model, 2)
    corner = flip(near, 2)
    owns = []
    for k in range(count):
        own = pltpu.make_async_copy(
            ins[k], view_of(outs[k], kinds[k], model, widths[k], every, every, every), own_sem.at[k]
        )
        own.start()
        owns.append(own)
    greet(data, model)

    def send(k, slot, source, target, partner):
        copy = pltpu.make_async_remote_copy(
            src_ref=source,
            dst_ref=target,
            send_sem=send_sem.at[k, slot],
            recv_sem=recv_sem.at[k, slot],
            device_id=partner,
            device_id_type=MESH_ID,
        )
        copy.start()
        return copy

    def piece(k, shard, y, x, c):
        return view_of(outs[k], kinds[k], shard, widths[k], y, x, c)

    copies = {}
    for k in range(count):
        mine = local_of(ins[k], kinds[k], y, x, c)
        copies[k, 0] = send(k, 0, mine, piece(k, model, y, x, c), (data, far))

    def pair_up(k):
        mine = local_of(ins[k], kinds[k], y, x, c)
        copies[k, 1] = send(k, 1, mine, piece(k, model, y, x, c), (data, near))
        copies[k, 0].wait_recv()
        block = piece(k, far, y, x, c)
        copies[k, 2] = send(k, 2, block, block, (data, near))

    def spread(k, stage):
        first_x = streams[k] == (stage == 0)
        if stage == 2:
            where, partner = (every, every, c), (flip(data, 1), model)
        elif stage == 0:
            where = (y, x, c)
            partner = (flip(data, 2 if first_x else 4), model)
        else:
            where = (y, every, c) if streams[k] else (every, x, c)
            partner = (flip(data, 2 if first_x else 4), model)
        base = 3 + 3 * stage
        for number, shard in enumerate((far, near, corner)):
            if stage == 0:
                if number > 0:
                    copies[k, number].wait_recv()
            else:
                copies[k, base - 3 + number].wait_recv()
            block = piece(k, shard, *where)
            copies[k, base + number] = send(k, base + number, block, block, partner)

    for step in range(count + 3):
        if step < count:
            pair_up(step)
        for stage in range(3):
            k = step - 1 - stage
            if 0 <= k < count:
                spread(k, stage)
    for k in range(count):
        for number in range(3):
            copies[k, 9 + number].wait_recv()
        owns[k].wait()
        for slot in range(12):
            copies[k, slot].wait_send()


def gather_all(arrays, kinds, streams, mp):
    ins, outs, widths, finals = [], [], [], []
    for array, kind in zip(arrays, kinds):
        widths.append(array.shape[-1])
        rows, width = array.shape[-2] // 8, array.shape[-1]
        if kind in ("col3", "split3"):
            ins.append(array.reshape(array.shape[0], 2, 2, 2, rows, width))
        else:
            ins.append(array.reshape(2, 2, 2, rows, width))
        if kind == "col3":
            shape, final = (array.shape[0], 2, 2, 2, rows, mp * width), (array.shape[0], 8 * rows, mp * width)
        elif kind == "col":
            shape, final = (2, 2, 2, rows, mp * width), (8 * rows, mp * width)
        elif kind == "row":
            shape, final = (mp, 2, 2, 2, rows, width), (mp * 8 * rows, width)
        else:
            shape = (mp, array.shape[0], 2, 2, 2, rows, width)
            final = (mp, array.shape[0], 8 * rows, width)
        outs.append(jax.ShapeDtypeStruct(shape, array.dtype))
        finals.append(final)
    count = len(arrays)
    results = pl.pallas_call(
        functools.partial(gather_kernel, tuple(kinds), tuple(widths), tuple(streams)),
        out_shape=outs,
        in_specs=[pl.BlockSpec(memory_space=pltpu.VMEM)] * count,
        out_specs=[pl.BlockSpec(memory_space=pl.ANY)] * count,
        scratch_shapes=[
            pltpu.SemaphoreType.DMA((count,)),
            pltpu.SemaphoreType.DMA((count, 12)),
            pltpu.SemaphoreType.DMA((count, 12)),
        ],
        compiler_params=pltpu.CompilerParams(
            collective_id=0, has_side_effects=True, vmem_limit_bytes=32 * 1024 * 1024
        ),
        name="gather_weights",
    )(*ins)
    return [result.reshape(final) for result, final in zip(results, finals)]


def steps_up(k, marks):
    total = 0
    for mark in marks:
        total = total + jnp.where(k >= mark, 1, 0)
    return total


TEXT_MARKS = (3, 4, 7, 10)
IMAGE_MARKS = (3, 4, 5, 6, 9)


def reduce_kernel(
    text_left, text_right, text_extra, image_left, image_right, norms,
    text_out, image_out, norm_out,
    text_send, image_send,
    text_r0, text_r1, text_r2, text_r3, text_r4,
    image_r0, image_r1, image_r2, image_r3, image_r4,
    norm_buf,
    text_ss, text_rs, image_ss, image_rs, norm_ss, norm_rs,
):
    data, model, c, x, y = position()
    low, high = model % 2, (model // 2) % 2
    f32, bf16 = jnp.float32, jnp.bfloat16
    core = (flip(data, 1), model)
    along_x = (flip(data, 2), model)
    along_y = (flip(data, 4), model)
    near = (data, flip(model, 1))
    far = (data, flip(model, 2))
    greet(data, model)

    def stream(left, right, extra, out, outgoing, bufs, send_sem, recv_sem, marks, x_first):
        r0, r1, r2, r3, r4 = bufs
        total = right.shape[0]
        rows = left.shape[-2]

        def copy(k, stage):
            if stage == 0:
                pair = (outgoing.at[k % 2], r0.at[k], core)
            elif stage == 1:
                source = r0.at[k, :, 1 - x] if x_first else r0.at[k, 1 - y]
                pair = (source, r1.at[k], along_x if x_first else along_y)
            elif stage == 2:
                source = r1.at[k, 1 - y] if x_first else r1.at[k, 1 - x]
                pair = (source, r2.at[k], along_y if x_first else along_x)
            elif stage == 3:
                pair = (r2.at[k, :, 1 - low], r3.at[k], near)
            else:
                pair = (r3.at[k, 1 - high], r4.at[k], far)
            return pltpu.make_async_remote_copy(
                src_ref=pair[0], dst_ref=pair[1],
                send_sem=send_sem.at[k, stage], recv_sem=recv_sem.at[k, stage],
                device_id=pair[2], device_id_type=MESH_ID,
            )

        def products(k, half, put):
            lhs = left[half, steps_up(k, marks)].reshape(4 * rows, left.shape[-1])

            def plain():
                for z in range(4):
                    value = jnp.dot(lhs, right[k, z], preferred_element_type=f32)
                    put(z, value.reshape(2, 2, rows, 256))

            if extra is None:
                plain()
                return
            pl.when(k != total - 1)(plain)

            @pl.when(k == total - 1)
            def _():
                more = left[half, 5].reshape(4 * rows, left.shape[-1])
                for z in range(4):
                    value = jnp.dot(lhs, right[k, z], preferred_element_type=f32)
                    value += jnp.dot(more, extra[z], preferred_element_type=f32)
                    put(z, value.reshape(2, 2, rows, 256))

        def begin(k):
            @pl.when(k >= 2)
            def _():
                copy(k - 2, 0).wait_send()

            def put(z, value):
                outgoing[k % 2, :, :, z // 2, z % 2] = value.astype(bf16)

            products(k, 1 - c, put)
            copy(k, 0).start()

        def join(k):
            copy(k, 0).wait_recv()

            def put(z, value):
                held = r0[k, :, :, z // 2, z % 2].astype(f32)
                r0[k, :, :, z // 2, z % 2] = (held + value).astype(bf16)

            products(k, c, put)
            copy(k, 1).start()

        def add_into(target, k, kept):
            target[k] = (target[k].astype(f32) + kept.astype(f32)).astype(bf16)

        def second(k):
            copy(k, 1).wait_recv()
            add_into(r1, k, r0[k, :, x] if x_first else r0[k, y])
            copy(k, 2).start()

        def third(k):
            copy(k, 2).wait_recv()
            add_into(r2, k, r1[k, y] if x_first else r1[k, x])
            copy(k, 3).start()

        def fourth(k):
            copy(k, 3).wait_recv()
            add_into(r3, k, r2[k, :, low])
            copy(k, 4).start()

        def last(k):
            copy(k, 4).wait_recv()
            out[k] = r4[k].astype(f32) + r3[k, high].astype(f32)

        def finish():
            def body(k, carry):
                for stage in range(1, 5):
                    copy(k, stage).wait_send()
                return carry

            lax.fori_loop(0, total, body, 0)
            copy(total - 2, 0).wait_send()
            copy(total - 1, 0).wait_send()

        return total, (begin, join, second, third, fourth, last), finish

    text_total, text_stages, text_finish = stream(
        text_left, text_right, text_extra, text_out, text_send,
        (text_r0, text_r1, text_r2, text_r3, text_r4), text_ss, text_rs, TEXT_MARKS, True,
    )
    image_total, image_stages, image_finish = stream(
        image_left, image_right, None, image_out, image_send,
        (image_r0, image_r1, image_r2, image_r3, image_r4), image_ss, image_rs, IMAGE_MARKS, False,
    )
    lags = (0, 1, 3, 5, 6, 7)
    partners = (core, along_x, along_y, near, far)

    def norm_copy(stage):
        return pltpu.make_async_remote_copy(
            src_ref=norms if stage == 0 else norm_buf.at[stage - 1],
            dst_ref=norm_buf.at[stage],
            send_sem=norm_ss.at[stage], recv_sem=norm_rs.at[stage],
            device_id=partners[stage], device_id_type=MESH_ID,
        )

    def turn(t, carry):
        for lag, text_stage, image_stage in zip(lags, text_stages, image_stages):
            k = t - lag
            pl.when((k >= 0) & (k < text_total))(functools.partial(text_stage, k))
            pl.when((k >= 0) & (k < image_total))(functools.partial(image_stage, k))
        for stage in range(6):

            @pl.when(t == 2 * stage)
            def _(stage=stage):
                if stage > 0:
                    norm_copy(stage - 1).wait_recv()
                    held = norms[...] if stage == 1 else norm_buf[stage - 2]
                    if stage < 5:
                        norm_buf[stage - 1] += held
                    else:
                        norm_out[...] = norm_buf[stage - 1] + held
                if stage < 5:
                    norm_copy(stage).start()

        return carry

    lax.fori_loop(0, max(text_total, image_total) + lags[-1], turn, 0)
    text_finish()
    image_finish()
    for stage in range(5):
        norm_copy(stage).wait_send()


def reduce_all(text_left, text_right, text_extra, image_left, image_right, norms):
    bf16, f32 = jnp.bfloat16, jnp.float32

    def buffers(right, left):
        total, rows = right.shape[0], left.shape[-2]
        tail = (rows, 256)
        return [
            pltpu.VMEM((total, 2, 2, 2, 2) + tail, bf16),
            pltpu.VMEM((total, 2, 2, 2) + tail, bf16),
            pltpu.VMEM((total, 2, 2) + tail, bf16),
            pltpu.VMEM((total, 2) + tail, bf16),
            pltpu.VMEM((total,) + tail, bf16),
        ]

    def outgoing(left):
        return pltpu.VMEM((2, 2, 2, 2, 2, left.shape[-2], 256), bf16)

    texts, images = text_right.shape[0], image_right.shape[0]
    sems = []
    for total in (texts, images):
        sems += [pltpu.SemaphoreType.DMA((total, 5))] * 2
    sems += [pltpu.SemaphoreType.DMA((5,))] * 2
    return pl.pallas_call(
        reduce_kernel,
        out_shape=[
            jax.ShapeDtypeStruct((texts, text_left.shape[-2], 256), f32),
            jax.ShapeDtypeStruct((images, image_left.shape[-2], 256), f32),
            jax.ShapeDtypeStruct(norms.shape, f32),
        ],
        in_specs=[pl.BlockSpec(memory_space=pltpu.VMEM)] * 6,
        out_specs=[pl.BlockSpec(memory_space=pltpu.VMEM)] * 3,
        scratch_shapes=[outgoing(text_left), outgoing(image_left)]
        + buffers(text_right, text_left)
        + buffers(image_right, image_left)
        + [pltpu.VMEM((5,) + norms.shape, f32)]
        + sems,
        compiler_params=pltpu.CompilerParams(
            collective_id=1, has_side_effects=True, vmem_limit_bytes=67043328
        ),
        name="reduce_gradients",
    )(text_left, text_right, text_extra, image_left, image_right, norms)


def weight_kinds():
    return (
        ("col3", True), ("col3", False), ("row", True), ("row", False), ("col", True), ("row", True),
        ("col", False), ("row", False), ("split3", True), ("row", True), ("col3", False), ("row", False),
    )


def shards(
    text_tokens, image_regions, lengths, region_counts, text_cross, image_cross, text_cross_out,
    image_cross_out, text_up, text_down, image_up, image_down, text_self, text_self_out, image_self,
    image_self_out, text_gains, text_shifts, image_gains, image_shifts, text_cotangent, image_cotangent,
):
    mp, dp = lax.axis_size("mp"), lax.axis_size("dp")
    bf16, f32 = jnp.bfloat16, jnp.float32
    kinds = [kind for kind, unused in weight_kinds()]
    streams = [by_x for unused, by_x in weight_kinds()]
    (
        text_cross, image_cross, text_cross_out, image_cross_out, text_up, text_down, image_up,
        image_down, text_self, text_self_out, image_self, image_self_out,
    ) = gather_all(
        (
            text_cross, image_cross, text_cross_out, image_cross_out, text_up, text_down, image_up,
            image_down, text_self, text_self_out, image_self, image_self_out,
        ),
        kinds, streams, mp,
    )
    text_self = text_self.transpose(1, 2, 0, 3).reshape(3, text_self.shape[2], -1)
    slot_count = text_tokens.shape[1]
    region_total = image_regions.shape[1]
    text_mask = jnp.arange(slot_count, dtype=jnp.int32)[None, :] < lengths[:, None]
    image_mask = jnp.arange(region_total, dtype=jnp.int32)[None, :] < region_counts[:, None]
    text_input = text_tokens.astype(f32)
    image_input = image_regions.astype(f32)
    text_proj, image_proj, contexts, totals = cross_forward(
        text_tokens, image_regions, text_cross, image_cross, text_mask, image_mask
    )
    text_hidden_a = text_input + project(contexts[0], text_cross_out)
    image_hidden_a = image_input + project(contexts[1], image_cross_out)
    text_mid = layer_norm(text_hidden_a, text_gains[0], text_shifts[0])
    image_mid = layer_norm(image_hidden_a, image_gains[0], image_shifts[0])
    text_second, image_second = text_mid.astype(bf16), image_mid.astype(bf16)
    text_upper, text_middle, text_part = ffn_forward(text_second, text_up, text_down)
    image_upper, image_middle, image_part = ffn_forward(image_second, image_up, image_down)
    text_hidden_b = text_mid + text_part
    image_hidden_b = image_mid + image_part
    text_mixed = layer_norm(text_hidden_b, text_gains[1], text_shifts[1])
    image_mixed = layer_norm(image_hidden_b, image_gains[1], image_shifts[1])
    text_third, image_third = text_mixed.astype(bf16), image_mixed.astype(bf16)
    text_saved = self_forward(text_third, text_self, text_self_out, text_mask, TEXT_HEAD)
    image_saved = self_forward(image_third, image_self, image_self_out, image_mask, IMAGE_HEAD)
    text_hidden_c = text_mixed + text_saved[3]
    image_hidden_c = image_mixed + image_saved[3]
    text_result = layer_norm(text_hidden_c, text_gains[2], text_shifts[2])
    image_result = layer_norm(image_hidden_c, image_gains[2], image_shifts[2])
    text_grad_c, text_gain_c, text_shift_c = norm_back(
        text_hidden_c, text_gains[2], text_shifts[2], text_cotangent.astype(f32)
    )
    image_grad_c, image_gain_c, image_shift_c = norm_back(
        image_hidden_c, image_gains[2], image_shifts[2], image_cotangent.astype(f32)
    )
    text_coming_c, image_coming_c = text_grad_c.astype(bf16), image_grad_c.astype(bf16)
    text_self_grads, text_part = self_back(
        text_saved, text_self, text_self_out, text_mask, TEXT_HEAD, text_coming_c
    )
    image_self_grads, image_part = self_back(
        image_saved, image_self, image_self_out, image_mask, IMAGE_HEAD, image_coming_c
    )
    text_grad_b, text_gain_b, text_shift_b = norm_back(
        text_hidden_b, text_gains[1], text_shifts[1], text_grad_c + text_part
    )
    image_grad_b, image_gain_b, image_shift_b = norm_back(
        image_hidden_b, image_gains[1], image_shifts[1], image_grad_c + image_part
    )
    text_coming_b, image_coming_b = text_grad_b.astype(bf16), image_grad_b.astype(bf16)
    text_upper_grad, text_part = ffn_back(text_upper, text_up, text_down, text_coming_b)
    image_upper_grad, image_part = ffn_back(image_upper, image_up, image_down, image_coming_b)
    text_grad_a, text_gain_a, text_shift_a = norm_back(
        text_hidden_a, text_gains[0], text_shifts[0], text_grad_b + text_part
    )
    image_grad_a, image_gain_a, image_shift_a = norm_back(
        image_hidden_a, image_gains[0], image_shifts[0], image_grad_b + image_part
    )
    text_coming_a, image_coming_a = text_grad_a.astype(bf16), image_grad_a.astype(bf16)
    text_ctx_grad = project_back(text_coming_a, text_cross_out).astype(bf16)
    image_ctx_grad = project_back(image_coming_a, image_cross_out).astype(bf16)
    text_query_grad, image_key_grad, image_value_grad = attend_back(
        text_proj[0], image_proj[1], image_proj[2], image_mask, CROSS_HEAD, totals[0], text_ctx_grad
    )
    image_query_grad, text_key_grad, text_value_grad = attend_back(
        image_proj[0], text_proj[1], text_proj[2], text_mask, CROSS_HEAD, totals[1], image_ctx_grad
    )
    text_cross_grads = (text_query_grad, text_key_grad, text_value_grad)
    image_cross_grads = (image_query_grad, image_key_grad, image_value_grad)
    text_input_grad = text_grad_a + input_part(text_cross_grads, text_cross)
    image_input_grad = image_grad_a + input_part(image_cross_grads, image_cross)

    more = dp // 8

    def lefts(arrays, pad):
        tiles = []
        for array in arrays:
            flat = array.reshape(-1, array.shape[-1])
            flat = jnp.pad(flat, ((0, pad), (0, 0))).T
            rows = flat.shape[0] // dp
            parts = flat.reshape(more, 2, 2, 2, rows, flat.shape[1]).transpose(3, 1, 2, 0, 4, 5)
            tiles.append(parts.reshape(2, 2, 2, more * rows, flat.shape[1]))
        return jnp.stack(tiles, 1)

    def cut(arrays, pad):
        tiles = []
        for array in arrays:
            flat = jnp.pad(array.reshape(-1, array.shape[-1]), ((0, pad), (0, 0)))
            tiles.append(flat.reshape(flat.shape[0], mp, -1))
        joined = jnp.concatenate(tiles, -1)
        chunked = joined.reshape(joined.shape[0], mp, -1, 256)
        return chunked.transpose(2, 1, 0, 3)

    text_left = lefts(
        (text_tokens, text_coming_a, text_second, text_coming_b, text_third, text_coming_c), 0
    )
    text_context = text_saved[1]
    text_right = cut(
        text_cross_grads + (contexts[0], text_upper_grad, text_middle) + text_self_grads
        + (jnp.zeros_like(text_context),), 0
    )
    extra = text_context.reshape(-1, mp, text_context.shape[-1] // mp)
    text_extra = jnp.pad(extra, ((0, 0), (0, 0), (256 - extra.shape[-1], 0))).transpose(1, 0, 2)
    image_rows = image_regions.shape[0] * region_total
    pad = 128 * math.ceil(image_rows / 128) - image_rows
    image_left = lefts(
        (image_regions, image_coming_a, image_second, image_coming_b, image_third, image_coming_c), pad
    )
    image_right = cut(
        image_cross_grads + (contexts[1], image_upper_grad, image_middle) + image_self_grads
        + (image_saved[1],), pad
    )
    norms = jnp.concatenate(
        [
            text_gain_a, text_gain_b, text_gain_c, text_shift_a, text_shift_b, text_shift_c,
            image_gain_a, image_gain_b, image_gain_c, image_shift_a, image_shift_b, image_shift_c,
        ]
    ).reshape(-1, 128)
    text_sums, image_sums, norm_sums = reduce_all(
        text_left, text_right, text_extra, image_left, image_right, norms
    )
    if more > 1:
        norm_sums = lax.psum(norm_sums, "dp") / 8
        text_sums, image_sums = outer_sum(text_sums, more), outer_sum(image_sums, more)
    text_sums = text_sums.transpose(1, 0, 2).reshape(text_sums.shape[1], -1)
    image_sums = image_sums.transpose(1, 0, 2).reshape(image_sums.shape[1], -1)

    def columns(sums, widths):
        parts, start = [], 0
        for width in widths:
            parts.append(sums[:, start : start + width])
            start += width
        return parts

    def triple(parts):
        return jnp.stack(parts[:3])

    text_widths = [array.shape[-1] // mp for array in text_cross_grads + (contexts[0],)]
    text_widths += [text_upper_grad.shape[-1] // mp, text_middle.shape[-1] // mp]
    text_widths += [array.shape[-1] // mp for array in text_self_grads + (text_context,)]
    image_widths = [array.shape[-1] // mp for array in image_cross_grads + (contexts[1],)]
    image_widths += [image_upper_grad.shape[-1] // mp, image_middle.shape[-1] // mp]
    image_widths += [array.shape[-1] // mp for array in image_self_grads + (image_saved[1],)]
    text_parts = columns(text_sums, text_widths)
    image_parts = columns(image_sums, image_widths)
    flat_norms = norm_sums.reshape(-1)
    text_size, image_size = text_gains.size, image_gains.size
    text_end = 2 * text_size
    return (
        text_result,
        image_result,
        text_input_grad,
        image_input_grad,
        triple(text_parts[:3]),
        triple(image_parts[:3]),
        text_parts[3].T,
        image_parts[3].T,
        text_parts[4],
        text_parts[5].T,
        image_parts[4],
        image_parts[5].T,
        triple(text_parts[6:9]),
        text_parts[9].T,
        triple(image_parts[6:9]),
        image_parts[9].T,
        flat_norms[:text_size].reshape(text_gains.shape),
        flat_norms[text_size:text_end].reshape(text_shifts.shape),
        flat_norms[text_end : text_end + image_size].reshape(image_gains.shape),
        flat_norms[text_end + image_size :].reshape(image_shifts.shape),
    )


def outer_sum(sums, more):
    chunks, rows, width = sums.shape
    apart = sums.reshape(chunks, more, rows // more, width)
    low = lax.axis_index("dp") % 8
    spread = jnp.zeros((chunks, more, 8, rows // more, width), sums.dtype)
    spread = lax.dynamic_update_slice(spread, apart[:, :, None], (0, 0, low, 0, 0))
    spread = spread.reshape(chunks, more * 8 * (rows // more), width)
    return lax.psum_scatter(spread, "dp", scatter_dimension=1, tiled=True)


def solution(mesh):
    in_specs = (
        P(("dp", "mp"), None, None),
        P(("dp", "mp"), None, None),
        P(("dp", "mp")),
        P(("dp", "mp")),
        P(None, None, "mp"),
        P(None, None, "mp"),
        P("mp", None),
        P("mp", None),
        P(None, "mp"),
        P("mp", None),
        P(None, "mp"),
        P("mp", None),
        P(None, None, "mp"),
        P("mp", None),
        P(None, None, "mp"),
        P("mp", None),
        P(),
        P(),
        P(),
        P(),
        P(("dp", "mp"), None, None),
        P(("dp", "mp"), None, None),
    )
    out_specs = (
        P(("dp", "mp"), None, None),
        P(("dp", "mp"), None, None),
        P(("dp", "mp"), None, None),
        P(("dp", "mp"), None, None),
        P(None, "dp", "mp"),
        P(None, "dp", "mp"),
        P("mp", "dp"),
        P("mp", "dp"),
        P("dp", "mp"),
        P("mp", "dp"),
        P("dp", "mp"),
        P("mp", "dp"),
        P(None, "dp", "mp"),
        P("mp", "dp"),
        P(None, "dp", "mp"),
        P("mp", "dp"),
        P(),
        P(),
        P(),
        P(),
    )
    return jax.shard_map(shards, mesh=mesh, in_specs=in_specs, out_specs=out_specs, check_vma=False)
```

```python
import functools
import math

import jax
import jax.numpy as jnp
from jax import lax
from jax.experimental import pallas as pl
from jax.experimental.pallas import tpu as pltpu
from jax.sharding import PartitionSpec as P

TEXT_HEAD = 64
CROSS_HEAD = 128
IMAGE_HEAD = 128


EPSILON = 1e-05
MASKED = -1e30
MESH_ID = pl.DeviceIdType.MESH


def flip(index, step):
    return index + step * (1 - 2 * ((index // step) % 2))


def position(unit):
    data, model = lax.axis_index("dp"), lax.axis_index("mp")
    return data, model, (data // unit) % 2, (data // (2 * unit)) % 2, (data // (4 * unit)) % 2


def greet(data, model, unit):
    barrier = pltpu.get_barrier_semaphore()
    partners = [(flip(data, step * unit), model) for step in (1, 2, 4)]
    partners += [(data, flip(model, step)) for step in (1, 2)]
    for partner in partners:
        pl.semaphore_signal(barrier, inc=1, device_id=partner, device_id_type=MESH_ID)
    pl.semaphore_wait(barrier, len(partners))


def view_of(ref, kind, shard, width, y, x, c):
    if kind == "col3":
        columns = pl.ds(pl.multiple_of(shard * width, 128), width)
        return ref.at[:, y, x, c, :, columns]
    if kind == "col":
        columns = pl.ds(pl.multiple_of(shard * width, 128), width)
        return ref.at[y, x, c, :, columns]
    if kind == "row":
        return ref.at[shard, y, x, c]
    return ref.at[shard, :, y, x, c]


def local_of(ref, kind, y, x, c):
    if kind in ("col3", "split3"):
        return ref.at[:, y, x, c]
    return ref.at[y, x, c]


def gather_kernel(unit, kinds, widths, streams, *refs):
    count = len(kinds)
    ins, outs = refs[:count], refs[count : 2 * count]
    own_sem, send_sem, recv_sem = refs[2 * count :]
    data, model, c, x, y = position(unit)
    every = slice(None)
    near, far = flip(model, 1), flip(model, 2)
    corner = flip(near, 2)
    owns = []
    for k in range(count):
        own = pltpu.make_async_copy(
            ins[k], view_of(outs[k], kinds[k], model, widths[k], every, every, every), own_sem.at[k]
        )
        own.start()
        owns.append(own)
    greet(data, model, unit)

    def send(k, slot, source, target, partner):
        copy = pltpu.make_async_remote_copy(
            src_ref=source,
            dst_ref=target,
            send_sem=send_sem.at[k, slot],
            recv_sem=recv_sem.at[k, slot],
            device_id=partner,
            device_id_type=MESH_ID,
        )
        copy.start()
        return copy

    def piece(k, shard, y, x, c):
        return view_of(outs[k], kinds[k], shard, widths[k], y, x, c)

    copies = {}
    for k in range(count):
        mine = local_of(ins[k], kinds[k], y, x, c)
        copies[k, 0] = send(k, 0, mine, piece(k, model, y, x, c), (data, far))

    def pair_up(k):
        mine = local_of(ins[k], kinds[k], y, x, c)
        copies[k, 1] = send(k, 1, mine, piece(k, model, y, x, c), (data, near))
        copies[k, 0].wait_recv()
        block = piece(k, far, y, x, c)
        copies[k, 2] = send(k, 2, block, block, (data, near))

    def spread(k, stage):
        first_x = streams[k] == (stage == 0)
        if stage == 2:
            where, partner = (every, every, c), (flip(data, unit), model)
        elif stage == 0:
            where = (y, x, c)
            partner = (flip(data, (2 if first_x else 4) * unit), model)
        else:
            where = (y, every, c) if streams[k] else (every, x, c)
            partner = (flip(data, (2 if first_x else 4) * unit), model)
        base = 3 + 3 * stage
        for number, shard in enumerate((far, near, corner)):
            if stage == 0:
                if number > 0:
                    copies[k, number].wait_recv()
            else:
                copies[k, base - 3 + number].wait_recv()
            block = piece(k, shard, *where)
            copies[k, base + number] = send(k, base + number, block, block, partner)

    for step in range(count + 3):
        if step < count:
            pair_up(step)
        for stage in range(3):
            k = step - 1 - stage
            if 0 <= k < count:
                spread(k, stage)
    for k in range(count):
        for number in range(3):
            copies[k, 9 + number].wait_recv()
        owns[k].wait()
        for slot in range(12):
            copies[k, slot].wait_send()


def gather_all(arrays, kinds, streams, mp, unit):
    ins, outs, widths, finals = [], [], [], []
    for array, kind in zip(arrays, kinds):
        widths.append(array.shape[-1])
        rows, width = array.shape[-2] // 8, array.shape[-1]
        if kind in ("col3", "split3"):
            ins.append(array.reshape(array.shape[0], 2, 2, 2, rows, width))
        else:
            ins.append(array.reshape(2, 2, 2, rows, width))
        if kind == "col3":
            shape, final = (array.shape[0], 2, 2, 2, rows, mp * width), (array.shape[0], 8 * rows, mp * width)
        elif kind == "col":
            shape, final = (2, 2, 2, rows, mp * width), (8 * rows, mp * width)
        elif kind == "row":
            shape, final = (mp, 2, 2, 2, rows, width), (mp * 8 * rows, width)
        else:
            shape = (mp, array.shape[0], 2, 2, 2, rows, width)
            final = (mp, array.shape[0], 8 * rows, width)
        outs.append(jax.ShapeDtypeStruct(shape, array.dtype))
        finals.append(final)
    count = len(arrays)
    results = pl.pallas_call(
        functools.partial(gather_kernel, unit, tuple(kinds), tuple(widths), tuple(streams)),
        out_shape=outs,
        in_specs=[pl.BlockSpec(memory_space=pltpu.VMEM)] * count,
        out_specs=[pl.BlockSpec(memory_space=pl.ANY)] * count,
        scratch_shapes=[
            pltpu.SemaphoreType.DMA((count,)),
            pltpu.SemaphoreType.DMA((count, 12)),
            pltpu.SemaphoreType.DMA((count, 12)),
        ],
        compiler_params=pltpu.CompilerParams(
            collective_id=0, has_side_effects=True, vmem_limit_bytes=32 * 1024 * 1024
        ),
        name="gather_weights",
    )(*ins)
    return [result.reshape(final) for result, final in zip(results, finals)]


def steps_up(k, marks):
    total = 0
    for mark in marks:
        total = total + jnp.where(k >= mark, 1, 0)
    return total


TEXT_MARKS = (3, 4, 7, 10)
IMAGE_MARKS = (3, 4, 5, 6, 9)


def reduce_kernel(
    unit,
    text_left, text_right, text_extra, image_left, image_right, norms,
    text_out, image_out, norm_out,
    text_send, image_send,
    text_r0, text_r1, text_r2, text_r3, text_r4,
    image_r0, image_r1, image_r2, image_r3, image_r4,
    norm_buf,
    text_ss, text_rs, image_ss, image_rs, norm_ss, norm_rs,
):
    data, model, c, x, y = position(unit)
    low, high = model % 2, (model // 2) % 2
    f32, bf16 = jnp.float32, jnp.bfloat16
    core = (flip(data, unit), model)
    along_x = (flip(data, 2 * unit), model)
    along_y = (flip(data, 4 * unit), model)
    near = (data, flip(model, 1))
    far = (data, flip(model, 2))
    greet(data, model, unit)

    def stream(left, right, extra, out, outgoing, bufs, send_sem, recv_sem, marks, x_first):
        r0, r1, r2, r3, r4 = bufs
        total = right.shape[0]
        rows = left.shape[-2]

        def copy(k, stage):
            if stage == 0:
                pair = (outgoing.at[k % 2], r0.at[k], core)
            elif stage == 1:
                source = r0.at[k, :, 1 - x] if x_first else r0.at[k, 1 - y]
                pair = (source, r1.at[k], along_x if x_first else along_y)
            elif stage == 2:
                source = r1.at[k, 1 - y] if x_first else r1.at[k, 1 - x]
                pair = (source, r2.at[k], along_y if x_first else along_x)
            elif stage == 3:
                pair = (r2.at[k, :, 1 - low], r3.at[k], near)
            else:
                pair = (r3.at[k, 1 - high], r4.at[k], far)
            return pltpu.make_async_remote_copy(
                src_ref=pair[0], dst_ref=pair[1],
                send_sem=send_sem.at[k, stage], recv_sem=recv_sem.at[k, stage],
                device_id=pair[2], device_id_type=MESH_ID,
            )

        def products(k, half, put):
            lhs = left[half, steps_up(k, marks)].reshape(4 * rows, left.shape[-1])

            def plain():
                for z in range(4):
                    value = jnp.dot(lhs, right[k, z], preferred_element_type=f32)
                    put(z, value.reshape(2, 2, rows, 256))

            if extra is None:
                plain()
                return
            pl.when(k != total - 1)(plain)

            @pl.when(k == total - 1)
            def _():
                more = left[half, 5].reshape(4 * rows, left.shape[-1])
                for z in range(4):
                    value = jnp.dot(lhs, right[k, z], preferred_element_type=f32)
                    value += jnp.dot(more, extra[z], preferred_element_type=f32)
                    put(z, value.reshape(2, 2, rows, 256))

        def begin(k):
            @pl.when(k >= 2)
            def _():
                copy(k - 2, 0).wait_send()

            def put(z, value):
                outgoing[k % 2, :, :, z // 2, z % 2] = value.astype(bf16)

            products(k, 1 - c, put)
            copy(k, 0).start()

        def join(k):
            copy(k, 0).wait_recv()

            def put(z, value):
                held = r0[k, :, :, z // 2, z % 2].astype(f32)
                r0[k, :, :, z // 2, z % 2] = (held + value).astype(bf16)

            products(k, c, put)
            copy(k, 1).start()

        def add_into(target, k, kept):
            target[k] = (target[k].astype(f32) + kept.astype(f32)).astype(bf16)

        def second(k):
            copy(k, 1).wait_recv()
            add_into(r1, k, r0[k, :, x] if x_first else r0[k, y])
            copy(k, 2).start()

        def third(k):
            copy(k, 2).wait_recv()
            add_into(r2, k, r1[k, y] if x_first else r1[k, x])
            copy(k, 3).start()

        def fourth(k):
            copy(k, 3).wait_recv()
            add_into(r3, k, r2[k, :, low])
            copy(k, 4).start()

        def last(k):
            copy(k, 4).wait_recv()
            out[k] = r4[k].astype(f32) + r3[k, high].astype(f32)

        def finish():
            def body(k, carry):
                for stage in range(1, 5):
                    copy(k, stage).wait_send()
                return carry

            lax.fori_loop(0, total, body, 0)
            copy(total - 2, 0).wait_send()
            copy(total - 1, 0).wait_send()

        return total, (begin, join, second, third, fourth, last), finish

    text_total, text_stages, text_finish = stream(
        text_left, text_right, text_extra, text_out, text_send,
        (text_r0, text_r1, text_r2, text_r3, text_r4), text_ss, text_rs, TEXT_MARKS, True,
    )
    image_total, image_stages, image_finish = stream(
        image_left, image_right, None, image_out, image_send,
        (image_r0, image_r1, image_r2, image_r3, image_r4), image_ss, image_rs, IMAGE_MARKS, False,
    )
    lags = (0, 1, 3, 5, 6, 7)
    partners = (core, along_x, along_y, near, far)

    def norm_copy(stage):
        return pltpu.make_async_remote_copy(
            src_ref=norms if stage == 0 else norm_buf.at[stage - 1],
            dst_ref=norm_buf.at[stage],
            send_sem=norm_ss.at[stage], recv_sem=norm_rs.at[stage],
            device_id=partners[stage], device_id_type=MESH_ID,
        )

    def turn(t, carry):
        for lag, text_stage, image_stage in zip(lags, text_stages, image_stages):
            k = t - lag
            pl.when((k >= 0) & (k < text_total))(functools.partial(text_stage, k))
            pl.when((k >= 0) & (k < image_total))(functools.partial(image_stage, k))
        for stage in range(6):

            @pl.when(t == 2 * stage)
            def _(stage=stage):
                if stage > 0:
                    norm_copy(stage - 1).wait_recv()
                    held = norms[...] if stage == 1 else norm_buf[stage - 2]
                    if stage < 5:
                        norm_buf[stage - 1] += held
                    else:
                        norm_out[...] = norm_buf[stage - 1] + held
                if stage < 5:
                    norm_copy(stage).start()

        return carry

    lax.fori_loop(0, max(text_total, image_total) + lags[-1], turn, 0)
    text_finish()
    image_finish()
    for stage in range(5):
        norm_copy(stage).wait_send()


def reduce_all(text_left, text_right, text_extra, image_left, image_right, norms, unit):
    bf16, f32 = jnp.bfloat16, jnp.float32

    def buffers(right, left):
        total, rows = right.shape[0], left.shape[-2]
        tail = (rows, 256)
        return [
            pltpu.VMEM((total, 2, 2, 2, 2) + tail, bf16),
            pltpu.VMEM((total, 2, 2, 2) + tail, bf16),
            pltpu.VMEM((total, 2, 2) + tail, bf16),
            pltpu.VMEM((total, 2) + tail, bf16),
            pltpu.VMEM((total,) + tail, bf16),
        ]

    def outgoing(left):
        return pltpu.VMEM((2, 2, 2, 2, 2, left.shape[-2], 256), bf16)

    texts, images = text_right.shape[0], image_right.shape[0]
    sems = []
    for total in (texts, images):
        sems += [pltpu.SemaphoreType.DMA((total, 5))] * 2
    sems += [pltpu.SemaphoreType.DMA((5,))] * 2
    return pl.pallas_call(
        functools.partial(reduce_kernel, unit),
        out_shape=[
            jax.ShapeDtypeStruct((texts, text_left.shape[-2], 256), f32),
            jax.ShapeDtypeStruct((images, image_left.shape[-2], 256), f32),
            jax.ShapeDtypeStruct(norms.shape, f32),
        ],
        in_specs=[pl.BlockSpec(memory_space=pltpu.VMEM)] * 6,
        out_specs=[pl.BlockSpec(memory_space=pltpu.VMEM)] * 3,
        scratch_shapes=[outgoing(text_left), outgoing(image_left)]
        + buffers(text_right, text_left)
        + buffers(image_right, image_left)
        + [pltpu.VMEM((5,) + norms.shape, f32)]
        + sems,
        compiler_params=pltpu.CompilerParams(
            collective_id=1, has_side_effects=True, vmem_limit_bytes=67043328
        ),
        name="reduce_gradients",
    )(text_left, text_right, text_extra, image_left, image_right, norms)


ROOT_HALF = math.sqrt(0.5)
DENSITY = 1.0 / math.sqrt(2.0 * math.pi)
TILE = 256
BLOCK = 32


def dot_nn(a, b):
    return jnp.dot(a, b, preferred_element_type=jnp.float32)


def dot_nt(a, b):
    return lax.dot_general(a, b, (((1,), (1,)), ((), ())), preferred_element_type=jnp.float32)


def dot_tn(a, b):
    return lax.dot_general(a, b, (((0,), (0,)), ((), ())), preferred_element_type=jnp.float32)


def row_blocks(rows, body):
    def step(i, carry):
        body(pl.ds(pl.multiple_of(i * BLOCK, BLOCK), BLOCK))
        return carry

    lax.fori_loop(0, rows // BLOCK, step, 0)


def tile_at(j):
    return pl.ds(pl.multiple_of(j * TILE, TILE), TILE)


def probabilities(query, keys, mask, head_size):
    scores = dot_nt(query, keys) * (1.0 / math.sqrt(head_size))
    scores = jnp.where(mask > 0.5, scores, MASKED)
    lifted = jnp.exp(scores - jnp.max(scores, -1, keepdims=True))
    return lifted / jnp.sum(lifted, -1, keepdims=True)


def head_forward(query, keys, values, mask, head_size):
    probs = probabilities(query, keys, mask, head_size)
    return dot_nn(probs.astype(jnp.bfloat16), values).astype(jnp.bfloat16)


def head_back(query, keys, values, mask, head_size, context_grad):
    bf16 = jnp.bfloat16
    probs = probabilities(query, keys, mask, head_size)
    value_grad = dot_tn(probs.astype(bf16), context_grad)
    prob_grad = dot_nt(context_grad, values)
    inner = jnp.sum(probs * prob_grad, -1, keepdims=True)
    score_grad = (probs * (prob_grad - inner)).astype(bf16)
    scale = 1.0 / math.sqrt(head_size)
    query_grad = dot_nn(score_grad, keys) * scale
    key_grad = dot_tn(score_grad, query) * scale
    return query_grad.astype(bf16), key_grad.astype(bf16), value_grad.astype(bf16)


def norm_forward(number, res, acc, xhat, rstd, gains, shifts, lows):
    def block(rows):
        hidden = res[rows, :] + acc[rows, :]
        centred = hidden - jnp.mean(hidden, -1, keepdims=True)
        scale = lax.rsqrt(jnp.mean(centred * centred, -1, keepdims=True) + EPSILON)
        unit = centred * scale
        xhat[number, rows, :] = unit
        rstd[number, rows, :] = jnp.broadcast_to(scale, (BLOCK, 128))
        out = unit * gains[number : number + 1, :] + shifts[number : number + 1, :]
        res[rows, :] = out
        if lows is not None:
            lows[rows, :] = out.astype(jnp.bfloat16)

    row_blocks(res.shape[0], block)


def norm_backward(number, grad, acc, xhat, rstd, gains, low, norms):
    count = gains.shape[0]
    width = grad.shape[1]

    def step(i, carry):
        gain_sum, shift_sum = carry
        rows = pl.ds(pl.multiple_of(i * BLOCK, BLOCK), BLOCK)
        coming = grad[rows, :] if acc is None else grad[rows, :] + acc[rows, :]
        unit = xhat[number, rows, :]
        gain_sum += jnp.sum(coming * unit, 0, keepdims=True)
        shift_sum += jnp.sum(coming, 0, keepdims=True)
        scaled = coming * gains[number : number + 1, :]
        mean = jnp.mean(scaled, -1, keepdims=True)
        slope = jnp.mean(scaled * unit, -1, keepdims=True)
        out = (scaled - mean - unit * slope) * rstd[number, rows, 0:1]
        grad[rows, :] = out
        low[rows, :] = out.astype(jnp.bfloat16)
        return gain_sum, shift_sum

    zero = jnp.zeros((1, width), jnp.float32)
    gain_sum, shift_sum = lax.fori_loop(0, grad.shape[0] // BLOCK, step, (zero, zero))
    norms[number : number + 1, :] = gain_sum
    norms[count + number : count + number + 1, :] = shift_sum


def turn_over(left, tokens, rows):
    part = left.shape[4]
    for number, source in enumerate((tokens, rows.at[2], rows.at[0], rows.at[3], rows.at[1], rows.at[4])):
        turned = source[...].T
        for y in range(2):
            for x in range(2):
                for c in range(2):
                    first = (4 * y + 2 * x + c) * part
                    left[c, number, y, x] = turned[first : first + part]


def layer_kernel(
    lengths, counts, text_tokens, image_tokens, text_cot, image_cot,
    text_gains, text_shifts, image_gains, image_shifts,
    text_cross, image_cross, text_cross_out, image_cross_out, text_up, text_down,
    image_up, image_down, text_self, image_self, image_self_out,
    text_output, image_output, text_grad, image_grad,
    text_left, image_left, text_right, text_extra, image_right, text_norms, image_norms,
    slot, load_sem, text_acc, image_acc, text_xhat, image_xhat, text_rstd, image_rstd,
    text_slope, image_slope, text_qkv, image_qkv, text_sqkv, image_sqkv,
    mask_ti, mask_it, mask_tt, mask_ii, text_rows, image_rows,
):
    f32, bf16 = jnp.float32, jnp.bfloat16
    rows_t, rows_i = text_tokens.shape[0], image_tokens.shape[0]
    width_t, width_i = text_tokens.shape[1], image_tokens.shape[1]
    pairs = lengths.shape[0]
    per_t, per_i = rows_t // pairs, rows_i // pairs
    zs = text_right.shape[1]
    inner = zs * TILE
    ups = text_up.shape[1] // (zs * TILE)

    def whole(ref, row):
        flat = ref
        return [(flat, slice(None), row, ref.shape[-2], ref.shape[-1])]

    def three(ref):
        return [(ref.at[n], slice(None), n * ref.shape[1], ref.shape[1], ref.shape[2]) for n in range(ref.shape[0])]

    wide = slot.shape[2]
    loads = {
        "tc": three(text_cross),
        "ic": three(image_cross),
        "out": whole(text_cross_out, 0) + whole(image_cross_out, inner),
        "tu": [
            (text_up, pl.ds(n * wide, wide), n * width_t, width_t, wide)
            for n in range(text_up.shape[1] // wide)
        ],
        "td": whole(text_down, 0),
        "if": whole(image_up, 0) + whole(image_down, width_i),
        "ts": three(text_self),
        "is": three(image_self),
        "io": whole(image_self_out, 0),
    }
    order = ["tc", "ic", "out", "tu", "td", "if", "ts", "is", "io"]
    order += ["td", "if", "tu", "out", "tc", "ic"]
    slots = [0, 1, 2, 0, 1, 2, 0, 1, 2, 2, 0, 1, 2, 0, 1]

    def copies(number):
        where = slots[number]
        return [
            pltpu.make_async_copy(
                ref.at[:, cols] if isinstance(cols, slice) is False else ref,
                slot.at[where, pl.ds(row, rows), pl.ds(0, width)],
                load_sem.at[number, part],
            )
            for part, (ref, cols, row, rows, width) in enumerate(loads[order[number]])
        ]

    def start(number):
        for copy in copies(number):
            copy.start()

    def ready(number):
        for copy in copies(number):
            copy.wait()
        return slot.at[slots[number]]

    for number in range(3):
        start(number)

    def set_mask(ref, query_per, key_per, limits):
        query = lax.broadcasted_iota(jnp.int32, ref.shape, 0)
        key = lax.broadcasted_iota(jnp.int32, ref.shape, 1)
        seen = jnp.zeros(ref.shape, f32)
        for pair in range(pairs):
            inside = (query >= pair * query_per) & (query < (pair + 1) * query_per)
            inside &= (key >= pair * key_per) & (key < pair * key_per + limits[pair])
            seen = jnp.where(inside, 1.0, seen)
        ref[...] = seen

    set_mask(mask_ti, per_t, per_i, counts)
    set_mask(mask_it, per_i, per_t, lengths)
    set_mask(mask_tt, per_t, per_t, lengths)
    set_mask(mask_ii, per_i, per_i, counts)
    text_output[...] = text_tokens[...].astype(f32)
    image_output[...] = image_tokens[...].astype(f32)

    def clear():
        text_acc[...] = jnp.zeros(text_acc.shape, f32)
        image_acc[...] = jnp.zeros(image_acc.shape, f32)

    clear()

    def project_tiles(rows_ref, weights, width, kept):
        def body(z, carry):
            for n in range(3):
                tile = dot_nn(rows_ref[...], weights[n * width : (n + 1) * width, tile_at(z)])
                kept[n, :, tile_at(z)] = tile.astype(bf16)
            return carry

        lax.fori_loop(0, zs, body, 0)

    def halves(tile):
        return tile[:, :128], tile[:, 128:]

    def pair_heads(fn, count, *tiles):
        size = TILE // count if count == 2 else 64
        results = []
        for h in range(count):
            results.append(fn(*[tile[:, h * size : (h + 1) * size] for tile in tiles]))
        return results

    project_tiles(text_tokens, ready(0), width_t, text_qkv)
    project_tiles(image_tokens, ready(1), width_i, image_qkv)
    start(3)
    start(4)
    outs = ready(2)

    def cross_forward_tile(z, carry):
        tq, tk, tv = [text_qkv[n, :, tile_at(z)] for n in range(3)]
        iq, ik, iv = [image_qkv[n, :, tile_at(z)] for n in range(3)]
        text_heads = pair_heads(
            lambda q, k, v: head_forward(q, k, v, mask_ti[...], CROSS_HEAD), 2, tq, ik, iv
        )
        image_heads = pair_heads(
            lambda q, k, v: head_forward(q, k, v, mask_it[...], CROSS_HEAD), 2, iq, tk, tv
        )
        text_context = jnp.concatenate(text_heads, -1)
        image_context = jnp.concatenate(image_heads, -1)
        text_right[3, z] = text_context
        image_right[3, z] = image_context
        text_acc[...] += dot_nn(text_context, outs[tile_at(z), 0:width_t])
        offset = pl.ds(pl.multiple_of(inner + z * TILE, TILE), TILE)
        image_acc[...] += dot_nn(image_context, outs[offset, 0:width_i])
        return carry

    lax.fori_loop(0, zs, cross_forward_tile, 0)
    start(5)
    norm_forward(0, text_output, text_acc, text_xhat, text_rstd, text_gains, text_shifts, text_rows.at[0])
    norm_forward(0, image_output, image_acc, image_xhat, image_rstd, image_gains, image_shifts, image_rows.at[0])

    def gelu_tile(upper):
        normal = 0.5 * (1.0 + lax.erf(upper * ROOT_HALF))
        slope = normal + upper * (DENSITY * jnp.exp(-0.5 * upper * upper))
        return (upper * normal).astype(bf16), slope

    up_t = ready(3)
    per_wide = wide // TILE

    def text_up_tile(j, carry):
        rows = pl.ds(pl.multiple_of((j // per_wide) * width_t, 8), width_t)
        upper = dot_nn(text_rows[0], up_t[rows, tile_at(j % per_wide)])
        middle, slope = gelu_tile(upper)
        text_slope[j] = slope
        text_right[7 + j % ups, j // ups] = middle
        return carry

    lax.fori_loop(0, zs * ups, text_up_tile, 0)
    start(6)
    down_t = ready(4)
    clear()

    def text_down_tile(j, carry):
        text_acc[...] += dot_nn(text_right[7 + j % ups, j // ups], down_t[tile_at(j), 0:width_t])
        return carry

    lax.fori_loop(0, zs * ups, text_down_tile, 0)
    start(7)
    both_i = ready(5)

    def image_up_tile(z, carry):
        middle, slope = gelu_tile(dot_nn(image_rows[0], both_i[0:width_i, tile_at(z)]))
        image_slope[z] = slope
        image_right[5, z] = middle
        offset = pl.ds(pl.multiple_of(width_i + z * TILE, TILE), TILE)
        image_acc[...] += dot_nn(middle, both_i[offset, 0:width_i])
        return carry

    lax.fori_loop(0, zs, image_up_tile, 0)
    start(8)
    norm_forward(1, text_output, text_acc, text_xhat, text_rstd, text_gains, text_shifts, text_rows.at[1])
    norm_forward(1, image_output, image_acc, image_xhat, image_rstd, image_gains, image_shifts, image_rows.at[1])

    clear()
    self_t = ready(6)
    project_tiles(text_rows.at[1], self_t, width_t, text_sqkv)
    self_i = ready(7)
    project_tiles(image_rows.at[1], self_i, width_i, image_sqkv)
    out_i = ready(8)
    share = TILE - TEXT_HEAD
    heads_t = share // TEXT_HEAD

    def self_forward_tile(z, carry):
        text_tiles = [text_sqkv[n, :, tile_at(z)] for n in range(3)]
        heads = pair_heads(
            lambda q, k, v: head_forward(q, k, v, mask_tt[...], TEXT_HEAD), heads_t, *text_tiles
        )
        blank = jnp.zeros((rows_t, TEXT_HEAD), bf16)
        text_extra[z] = jnp.concatenate([blank] + heads, -1)
        context = jnp.concatenate(heads + [blank], -1)
        text_acc[...] += dot_nt(context, self_t[3 * width_t : 4 * width_t, tile_at(z)])
        image_tiles = [image_sqkv[n, :, tile_at(z)] for n in range(3)]
        image_heads = pair_heads(
            lambda q, k, v: head_forward(q, k, v, mask_ii[...], IMAGE_HEAD), 2, *image_tiles
        )
        image_context = jnp.concatenate(image_heads, -1)
        image_right[9, z] = image_context
        image_acc[...] += dot_nn(image_context, out_i[tile_at(z), 0:width_i])
        return carry

    lax.fori_loop(0, zs, self_forward_tile, 0)
    norm_forward(2, text_output, text_acc, text_xhat, text_rstd, text_gains, text_shifts, None)
    norm_forward(2, image_output, image_acc, image_xhat, image_rstd, image_gains, image_shifts, None)

    text_grad[...] = text_cot[...].astype(f32)
    image_grad[...] = image_cot[...].astype(f32)
    norm_backward(2, text_grad, None, text_xhat, text_rstd, text_gains, text_rows.at[4], text_norms)
    norm_backward(2, image_grad, None, image_xhat, image_rstd, image_gains, image_rows.at[4], image_norms)
    clear()

    def self_back_tile(z, carry):
        text_tiles = [text_sqkv[n, :, tile_at(z)] for n in range(3)]
        context_grad = dot_nt_rows(text_rows[4], self_t, z)
        grads = pair_heads(
            lambda q, k, v, d: head_back(q, k, v, mask_tt[...], TEXT_HEAD, d),
            heads_t, *text_tiles, context_grad,
        )
        blank = jnp.zeros((rows_t, TEXT_HEAD), bf16)
        dq, dk, dv = [[grads[h][n] for h in range(heads_t)] for n in range(3)]
        pieces = dq + dk + dv
        text_right[10, z] = jnp.concatenate(pieces[0:4], -1)
        text_right[11, z] = jnp.concatenate(pieces[4:8], -1)
        text_right[12, z] = jnp.concatenate(pieces[8:9] + [blank] * 3, -1)
        total = jnp.zeros((rows_t, width_t), f32)
        for n, parts in enumerate((dq, dk, dv)):
            joined = jnp.concatenate(parts + [blank], -1)
            total += dot_nt(joined, self_t[n * width_t : (n + 1) * width_t, tile_at(z)])
        text_acc[...] += total
        return carry

    def dot_nt_rows(coming, weights, z):
        return dot_nn(coming, weights[3 * width_t : 4 * width_t, tile_at(z)]).astype(bf16)

    def self_back_image(z, carry):
        image_tiles = [image_sqkv[n, :, tile_at(z)] for n in range(3)]
        context_grad = dot_nt(image_rows[4], out_i[tile_at(z), 0:width_i]).astype(bf16)
        grads = pair_heads(
            lambda q, k, v, d: head_back(q, k, v, mask_ii[...], IMAGE_HEAD, d),
            2, *image_tiles, context_grad,
        )
        total = jnp.zeros((rows_i, width_i), f32)
        for n in range(3):
            joined = jnp.concatenate([grads[0][n], grads[1][n]], -1)
            image_right[6 + n, z] = joined
            total += dot_nt(joined, self_i[n * width_i : (n + 1) * width_i, tile_at(z)])
        image_acc[...] += total
        return carry

    lax.fori_loop(0, zs, self_back_image, 0)
    start(9)
    lax.fori_loop(0, zs, self_back_tile, 0)
    start(10)
    start(11)
    norm_backward(1, text_grad, text_acc, text_xhat, text_rstd, text_gains, text_rows.at[3], text_norms)
    norm_backward(1, image_grad, image_acc, image_xhat, image_rstd, image_gains, image_rows.at[3], image_norms)
    clear()

    back_down = ready(9)

    def text_down_back(j, carry):
        middle_grad = dot_nt(text_rows[3], back_down[tile_at(j), 0:width_t])
        text_right[4 + j % ups, j // ups] = (middle_grad * text_slope[j]).astype(bf16)
        return carry

    lax.fori_loop(0, zs * ups, text_down_back, 0)
    start(12)
    back_i = ready(10)

    def image_ffn_back(z, carry):
        offset = pl.ds(pl.multiple_of(width_i + z * TILE, TILE), TILE)
        middle_grad = dot_nt(image_rows[3], back_i[offset, 0:width_i])
        upper_grad = (middle_grad * image_slope[z]).astype(bf16)
        image_right[4, z] = upper_grad
        image_acc[...] += dot_nt(upper_grad, back_i[0:width_i, tile_at(z)])
        return carry

    lax.fori_loop(0, zs, image_ffn_back, 0)
    start(13)
    back_up = ready(11)

    def text_up_back(j, carry):
        rows = pl.ds(pl.multiple_of((j // per_wide) * width_t, 8), width_t)
        text_acc[...] += dot_nt(text_right[4 + j % ups, j // ups], back_up[rows, tile_at(j % per_wide)])
        return carry

    lax.fori_loop(0, zs * ups, text_up_back, 0)
    start(14)
    norm_backward(0, text_grad, text_acc, text_xhat, text_rstd, text_gains, text_rows.at[2], text_norms)
    norm_backward(0, image_grad, image_acc, image_xhat, image_rstd, image_gains, image_rows.at[2], image_norms)
    clear()

    back_out = ready(12)
    cross_t = ready(13)
    cross_i = ready(14)

    def cross_back_tile(z, carry):
        tq, tk, tv = [text_qkv[n, :, tile_at(z)] for n in range(3)]
        iq, ik, iv = [image_qkv[n, :, tile_at(z)] for n in range(3)]
        text_ctx_grad = dot_nt(text_rows[2], back_out[tile_at(z), 0:width_t]).astype(bf16)
        offset = pl.ds(pl.multiple_of(inner + z * TILE, TILE), TILE)
        image_ctx_grad = dot_nt(image_rows[2], back_out[offset, 0:width_i]).astype(bf16)
        text_side = pair_heads(
            lambda q, k, v, d: head_back(q, k, v, mask_ti[...], CROSS_HEAD, d), 2, tq, ik, iv, text_ctx_grad
        )
        image_side = pair_heads(
            lambda q, k, v, d: head_back(q, k, v, mask_it[...], CROSS_HEAD, d), 2, iq, tk, tv, image_ctx_grad
        )

        def joined(side, n):
            return jnp.concatenate([side[0][n], side[1][n]], -1)

        text_parts = (joined(text_side, 0), joined(image_side, 1), joined(image_side, 2))
        image_parts = (joined(image_side, 0), joined(text_side, 1), joined(text_side, 2))
        total_t = jnp.zeros((rows_t, width_t), f32)
        total_i = jnp.zeros((rows_i, width_i), f32)
        for n in range(3):
            text_right[n, z] = text_parts[n]
            image_right[n, z] = image_parts[n]
            total_t += dot_nt(text_parts[n], cross_t[n * width_t : (n + 1) * width_t, tile_at(z)])
            total_i += dot_nt(image_parts[n], cross_i[n * width_i : (n + 1) * width_i, tile_at(z)])
        text_acc[...] += total_t
        image_acc[...] += total_i
        return carry

    lax.fori_loop(0, zs, cross_back_tile, 0)
    text_grad[...] += text_acc[...]
    image_grad[...] += image_acc[...]
    turn_over(text_left, text_tokens, text_rows)
    turn_over(image_left, image_tokens, image_rows)


def layer(lengths, counts, rows, params, weights, mp):
    f32, bf16 = jnp.float32, jnp.bfloat16
    text_tokens, image_tokens = rows[0], rows[1]
    rows_t, width_t = text_tokens.shape
    rows_i, width_i = image_tokens.shape
    text_up = weights[4]
    text_tiles = text_up.shape[1] // TILE
    inner = mp * TILE

    vmem = pl.BlockSpec(memory_space=pltpu.VMEM)
    out_shape = [
        jax.ShapeDtypeStruct((rows_t, width_t), f32),
        jax.ShapeDtypeStruct((rows_i, width_i), f32),
        jax.ShapeDtypeStruct((rows_t, width_t), f32),
        jax.ShapeDtypeStruct((rows_i, width_i), f32),
        jax.ShapeDtypeStruct((2, 6, 2, 2, width_t // 8, rows_t), bf16),
        jax.ShapeDtypeStruct((2, 6, 2, 2, width_i // 8, rows_i), bf16),
        jax.ShapeDtypeStruct((13, mp, rows_t, TILE), bf16),
        jax.ShapeDtypeStruct((mp, rows_t, TILE), bf16),
        jax.ShapeDtypeStruct((10, mp, rows_i, TILE), bf16),
        jax.ShapeDtypeStruct((2 * params[0].shape[0], width_t), f32),
        jax.ShapeDtypeStruct((2 * params[0].shape[0], width_i), f32),
    ]
    return pl.pallas_call(
        layer_kernel,
        out_shape=out_shape,
        in_specs=[pl.BlockSpec(memory_space=pltpu.SMEM)] * 2
        + [vmem] * 8
        + [pl.BlockSpec(memory_space=pl.ANY)] * len(weights),
        out_specs=[vmem] * len(out_shape),
        scratch_shapes=[
            pltpu.VMEM((3, 3 * width_i, inner), bf16),
            pltpu.SemaphoreType.DMA((15, 4)),
            pltpu.VMEM((rows_t, width_t), f32),
            pltpu.VMEM((rows_i, width_i), f32),
            pltpu.VMEM((3, rows_t, width_t), f32),
            pltpu.VMEM((3, rows_i, width_i), f32),
            pltpu.VMEM((3, rows_t, 128), f32),
            pltpu.VMEM((3, rows_i, 128), f32),
            pltpu.VMEM((text_tiles, rows_t, TILE), f32),
            pltpu.VMEM((mp, rows_i, TILE), f32),
            pltpu.VMEM((3, rows_t, inner), bf16),
            pltpu.VMEM((3, rows_i, inner), bf16),
            pltpu.VMEM((3, rows_t, inner), bf16),
            pltpu.VMEM((3, rows_i, inner), bf16),
            pltpu.VMEM((rows_t, rows_i), f32),
            pltpu.VMEM((rows_i, rows_t), f32),
            pltpu.VMEM((rows_t, rows_t), f32),
            pltpu.VMEM((rows_i, rows_i), f32),
            pltpu.VMEM((5, rows_t, width_t), bf16),
            pltpu.VMEM((5, rows_i, width_i), bf16),
        ],
        compiler_params=pltpu.CompilerParams(vmem_limit_bytes=67043328),
        name="layer",
    )(lengths, counts, *rows, *params, *weights)


def weight_kinds():
    return (
        ("col3", True), ("col3", False), ("row", True), ("row", False), ("col", True), ("row", True),
        ("col", False), ("row", False), ("col3", True), ("col3", False), ("row", False),
    )


def shards(
    text_tokens, image_regions, lengths, region_counts, text_cross, image_cross, text_cross_out,
    image_cross_out, text_up, text_down, image_up, image_down, text_self, text_self_out, image_self,
    image_self_out, text_gains, text_shifts, image_gains, image_shifts, text_cotangent, image_cotangent,
):
    mp, dp = lax.axis_size("mp"), lax.axis_size("dp")
    more = dp // 8
    text_out_turned = text_self_out.T[None]
    text_four = jnp.concatenate([text_self, text_out_turned])
    spare = 256 - text_four.shape[-1]
    text_four = jnp.pad(text_four, ((0, 0), (0, 0), (0, spare)))
    kinds = [kind for kind, unused in weight_kinds()]
    streams = [by_x for unused, by_x in weight_kinds()]
    weights = gather_all(
        (
            text_cross, image_cross, text_cross_out, image_cross_out, text_up, text_down, image_up,
            image_down, text_four, image_self, image_self_out,
        ),
        kinds, streams, mp, more,
    )
    pairs, regions = image_regions.shape[0], image_regions.shape[1]
    padding = (-regions) % 16

    def pad_regions(array):
        return jnp.pad(array, ((0, 0), (0, padding), (0, 0))).reshape(-1, array.shape[-1])

    def flat(array):
        return array.reshape(-1, array.shape[-1])

    (
        text_result, image_result, text_input_grad, image_input_grad,
        text_left, image_left, text_right, text_extra, image_right, text_norms, image_norms,
    ) = layer(
        lengths, region_counts,
        (flat(text_tokens), pad_regions(image_regions), flat(text_cotangent), pad_regions(image_cotangent)),
        (text_gains, text_shifts, image_gains, image_shifts),
        weights, mp,
    )
    text_result, text_input_grad = [
        array.reshape(text_tokens.shape) for array in (text_result, text_input_grad)
    ]
    image_result, image_input_grad = [
        array.reshape(pairs, regions + padding, -1)[:, :regions]
        for array in (image_result, image_input_grad)
    ]
    norms = jnp.concatenate([text_norms.reshape(-1, 128), image_norms.reshape(-1, 128)])
    text_sums, image_sums, norm_sums = reduce_all(
        text_left, text_right, text_extra, image_left, image_right, norms, more
    )
    if more > 1:
        norm_sums = lax.psum(norm_sums, "dp") / 8
        text_sums, image_sums = outer_sum(text_sums, more), outer_sum(image_sums, more)
    text_sums = text_sums.transpose(1, 0, 2).reshape(text_sums.shape[1], -1)
    image_sums = image_sums.transpose(1, 0, 2).reshape(image_sums.shape[1], -1)

    def columns(sums, widths):
        parts, start = [], 0
        for width in widths:
            parts.append(sums[:, start : start + width])
            start += width
        return parts

    def triple(parts):
        return jnp.stack(parts[:3])

    text_widths = [text_cross.shape[-1]] * 3 + [text_cross_out.shape[0]]
    text_widths += [text_up.shape[-1], text_down.shape[0]]
    text_widths += [text_self.shape[-1]] * 3 + [text_self_out.shape[0]]
    image_widths = [image_cross.shape[-1]] * 3 + [image_cross_out.shape[0]]
    image_widths += [image_up.shape[-1], image_down.shape[0]]
    image_widths += [image_self.shape[-1]] * 3 + [image_self_out.shape[0]]
    text_parts = columns(text_sums, text_widths)
    image_parts = columns(image_sums, image_widths)
    flat_norms = norm_sums.reshape(-1)
    text_size, image_size = text_gains.size, image_gains.size
    text_end = 2 * text_size
    return (
        text_result,
        image_result,
        text_input_grad,
        image_input_grad,
        triple(text_parts[:3]),
        triple(image_parts[:3]),
        text_parts[3].T,
        image_parts[3].T,
        text_parts[4],
        text_parts[5].T,
        image_parts[4],
        image_parts[5].T,
        triple(text_parts[6:9]),
        text_parts[9].T,
        triple(image_parts[6:9]),
        image_parts[9].T,
        flat_norms[:text_size].reshape(text_gains.shape),
        flat_norms[text_size:text_end].reshape(text_shifts.shape),
        flat_norms[text_end : text_end + image_size].reshape(image_gains.shape),
        flat_norms[text_end + image_size :].reshape(image_shifts.shape),
    )


def outer_sum(sums, more):
    chunks, rows, width = sums.shape
    apart = sums.reshape(chunks, 1, more, rows // more, width)
    low = lax.axis_index("dp") // more
    spread = jnp.zeros((chunks, 8, more, rows // more, width), sums.dtype)
    spread = lax.dynamic_update_slice(spread, apart, (0, low, 0, 0, 0))
    spread = spread.reshape(chunks, 8 * rows, width)
    return lax.psum_scatter(spread, "dp", scatter_dimension=1, tiled=True)


def solution(mesh):
    in_specs = (
        P(("dp", "mp"), None, None),
        P(("dp", "mp"), None, None),
        P(("dp", "mp")),
        P(("dp", "mp")),
        P(None, None, "mp"),
        P(None, None, "mp"),
        P("mp", None),
        P("mp", None),
        P(None, "mp"),
        P("mp", None),
        P(None, "mp"),
        P("mp", None),
        P(None, None, "mp"),
        P("mp", None),
        P(None, None, "mp"),
        P("mp", None),
        P(),
        P(),
        P(),
        P(),
        P(("dp", "mp"), None, None),
        P(("dp", "mp"), None, None),
    )
    out_specs = (
        P(("dp", "mp"), None, None),
        P(("dp", "mp"), None, None),
        P(("dp", "mp"), None, None),
        P(("dp", "mp"), None, None),
        P(None, "dp", "mp"),
        P(None, "dp", "mp"),
        P("mp", "dp"),
        P("mp", "dp"),
        P("dp", "mp"),
        P("mp", "dp"),
        P("dp", "mp"),
        P("mp", "dp"),
        P(None, "dp", "mp"),
        P("mp", "dp"),
        P(None, "dp", "mp"),
        P("mp", "dp"),
        P(),
        P(),
        P(),
        P(),
    )
    return jax.shard_map(shards, mesh=mesh, in_specs=in_specs, out_specs=out_specs, check_vma=False)
```

```python
import functools
import math

import jax
import jax.numpy as jnp
from jax import lax
from jax.experimental import pallas as pl
from jax.experimental.pallas import tpu as pltpu
from jax.sharding import PartitionSpec as P

TEXT_HEAD = 64
CROSS_HEAD = 128
IMAGE_HEAD = 128


EPSILON = 1e-05
MASKED = -1e30
MESH_ID = pl.DeviceIdType.MESH


def flip(index, step):
    return index + step * (1 - 2 * ((index // step) % 2))


def position(unit):
    data, model = lax.axis_index("dp"), lax.axis_index("mp")
    return data, model, (data // unit) % 2, (data // (2 * unit)) % 2, (data // (4 * unit)) % 2


def greet(data, model, unit):
    barrier = pltpu.get_barrier_semaphore()
    partners = [(flip(data, step * unit), model) for step in (1, 2, 4)]
    partners += [(data, flip(model, step)) for step in (1, 2)]
    for partner in partners:
        pl.semaphore_signal(barrier, inc=1, device_id=partner, device_id_type=MESH_ID)
    pl.semaphore_wait(barrier, len(partners))


def view_of(ref, matrix, shard, width, y, x, c):
    if matrix is None:
        return ref.at[shard, y, x, c]
    return ref.at[matrix, y, x, c, :, pl.ds(pl.multiple_of(shard * width, 128), width)]


LEAD = 2
LAGS = (0, 2, 4, 6, 8)


def gather_kernel(unit, kinds, widths, chunks, *refs):
    count = len(kinds)
    ins, outs = refs[:count], refs[count : 2 * count]
    own_sem, send_sem, recv_sem = refs[2 * count :]
    data, model, c, x, y = position(unit)
    every = slice(None)
    near, far = flip(model, 1), flip(model, 2)
    corner = flip(near, 2)
    owns = []
    for k in range(count):
        for matrix in range(ins[k].shape[0]) if kinds[k] == "cols" else (None,):
            source = ins[k] if matrix is None else ins[k].at[matrix]
            target = view_of(outs[k], matrix, model, widths[k], every, every, every)
            own = pltpu.make_async_copy(source, target, own_sem.at[len(owns)])
            own.start()
            owns.append(own)
    greet(data, model, unit)
    copies = {}

    def send(n, slot, source, target, partner):
        copies[n, slot] = pltpu.make_async_remote_copy(
            src_ref=source,
            dst_ref=target,
            send_sem=send_sem.at[n, slot],
            recv_sem=recv_sem.at[n, slot],
            device_id=partner,
            device_id_type=MESH_ID,
        )
        copies[n, slot].start()

    def piece(n, shard, where):
        k, matrix, unused, unused = chunks[n]
        return view_of(outs[k], matrix, shard, widths[k], *where)

    def mine(n, where):
        k, matrix, unused, unused = chunks[n]
        return ins[k].at[where] if matrix is None else ins[k].at[(matrix,) + where]

    x_side = (flip(data, 2 * unit), model)
    y_side = (flip(data, 4 * unit), model)
    z_side = (data, near)
    single = (y, x, c)

    def relay(n, slot, shard, where, partner):
        block = piece(n, shard, where)
        send(n, slot, block, block, partner)

    def advance(n, stage):
        x_first, early = chunks[n][2:]
        first, second = (x_side, y_side) if x_first else (y_side, x_side)
        double = (y, every, c) if x_first else (every, x, c)
        if stage == 0:
            send(n, 0, mine(n, single), piece(n, model, single), (data, far))
        elif stage == 1 and not early:
            send(n, 1, mine(n, single), piece(n, model, single), z_side)
            copies[n, 0].wait_recv()
            relay(n, 2, far, single, z_side)
        elif stage == 2 and not early:
            relay(n, 3, far, single, first)
            copies[n, 1].wait_recv()
            relay(n, 4, near, single, first)
            copies[n, 2].wait_recv()
            relay(n, 5, corner, single, first)
        elif stage == 1:
            copies[n, 0].wait_recv()
            relay(n, 3, far, single, first)
        elif stage == 2:
            send(n, 1, mine(n, double), piece(n, model, double), z_side)
            copies[n, 3].wait_recv()
            relay(n, 2, far, double, z_side)
        elif stage == 3:
            before = (None, 1, 2) if early else (3, 4, 5)
            for number, shard in enumerate((far, near, corner)):
                if before[number] is not None:
                    copies[n, before[number]].wait_recv()
                relay(n, 6 + number, shard, double, second)
        else:
            for number, shard in enumerate((far, near, corner)):
                copies[n, 6 + number].wait_recv()
                relay(n, 9 + number, shard, (every, every, c), (flip(data, unit), model))

    total = len(chunks)
    for step in range(total + LAGS[-1]):
        for stage, lag in enumerate(LAGS):
            if 0 <= step - lag < total:
                advance(step - lag, stage)
    for n in range(total):
        for slot in range(9, 12):
            copies[n, slot].wait_recv()
    for own in owns:
        own.wait()
    for copy in copies.values():
        copy.wait_send()


def gather_all(arrays, kinds, chunks, mp, unit):
    ins, outs, widths, finals, owned = [], [], [], [], 0
    for array, kind in zip(arrays, kinds):
        rows, width = array.shape[-2] // 8, array.shape[-1]
        widths.append(width)
        if kind == "cols":
            lead = array.size // (8 * rows * width)
            ins.append(array.reshape(lead, 2, 2, 2, rows, width))
            shape = (lead, 2, 2, 2, rows, mp * width)
            finals.append(array.shape[:-1] + (mp * width,))
            owned += lead
        else:
            ins.append(array.reshape(2, 2, 2, rows, width))
            shape = (mp, 2, 2, 2, rows, width)
            finals.append((mp * 8 * rows, width))
            owned += 1
        outs.append(jax.ShapeDtypeStruct(shape, array.dtype))
    count = len(arrays)
    results = pl.pallas_call(
        functools.partial(gather_kernel, unit, tuple(kinds), tuple(widths), tuple(chunks)),
        out_shape=outs,
        in_specs=[pl.BlockSpec(memory_space=pltpu.VMEM)] * count,
        out_specs=[pl.BlockSpec(memory_space=pl.ANY)] * count,
        scratch_shapes=[
            pltpu.SemaphoreType.DMA((owned,)),
            pltpu.SemaphoreType.DMA((len(chunks), 12)),
            pltpu.SemaphoreType.DMA((len(chunks), 12)),
        ],
        compiler_params=pltpu.CompilerParams(
            collective_id=0, has_side_effects=True, vmem_limit_bytes=32 * 1024 * 1024
        ),
        name="gather_weights",
    )(*ins)
    return [result.reshape(final) for result, final in zip(results, finals)]


KINDS = ("cols", "cols", "rows", "rows", "cols", "rows", "cols", "rows", "cols", "cols", "rows")
SEQUENCE = (
    (0, 0), (1, 0), (0, 1), (1, 1), (0, 2), (1, 2), (2, None), (3, None), (4, 0), (6, 0), (5, None), (7, None),
    (8, 0), (9, 0), (8, 1), (9, 1), (8, 2), (9, 2), (8, 3), (10, None),
)


def chunk_plan():
    return tuple(
        (k, matrix, n % 4 in (0, 3), n % 2 == 1) for n, (k, matrix) in enumerate(SEQUENCE)
    )


def steps_up(k, marks):
    total = 0
    for mark in marks:
        total = total + jnp.where(k >= mark, 1, 0)
    return total


STAGE_LAGS = (0, 2, 4, 6, 8, 10)
TEXT_MARKS = (3, 4, 7, 10)
IMAGE_MARKS = (3, 4, 5, 6, 9)


def reduce_kernel(
    unit,
    text_left, text_right, text_extra, image_left, image_right, norms,
    text_out, image_out, norm_out,
    text_send, image_send,
    text_r0, text_r1, text_r2, text_r3, text_r4,
    image_r0, image_r1, image_r2, image_r3, image_r4,
    norm_buf,
    text_ss, text_rs, image_ss, image_rs, norm_ss, norm_rs,
):
    data, model, c, x, y = position(unit)
    low, high = model % 2, (model // 2) % 2
    f32, bf16 = jnp.float32, jnp.bfloat16
    core = (flip(data, unit), model)
    along_x = (flip(data, 2 * unit), model)
    along_y = (flip(data, 4 * unit), model)
    near = (data, flip(model, 1))
    far = (data, flip(model, 2))
    greet(data, model, unit)

    def stream(left, right, extra, out, outgoing, bufs, send_sem, recv_sem, marks, turn_first):
        r0, r1, r2, r3, r4 = bufs
        total = right.shape[0]
        rows = left.shape[-2]

        def order(k):
            by_y = (k + turn_first) % 2
            by_x = 1 - by_y
            first, second = x * by_x + y * by_y, y * by_x + x * by_y
            return by_x, first, second

        def copy(k, stage):
            by_x, first, second = order(k)
            if stage == 0:
                pair = (outgoing.at[k % 2], r0.at[k], core)
            elif stage == 1:
                pair = (r0.at[k, 1 - first], r1.at[k], (flip(data, (4 - 2 * by_x) * unit), model))
            elif stage == 2:
                pair = (r1.at[k, :, :, 1 - low], r2.at[k], near)
            elif stage == 3:
                pair = (r2.at[k, 1 - second], r3.at[k], (flip(data, (2 + 2 * by_x) * unit), model))
            else:
                pair = (r3.at[k, 1 - high], r4.at[k], far)
            return pltpu.make_async_remote_copy(
                src_ref=pair[0], dst_ref=pair[1],
                send_sem=send_sem.at[k, stage], recv_sem=recv_sem.at[k, stage],
                device_id=pair[2], device_id_type=MESH_ID,
            )

        def products(k, half, put):
            lhs = left[half, steps_up(k, marks)].reshape(4 * rows, left.shape[-1])

            def plain():
                for z in range(4):
                    value = jnp.dot(lhs, right[k, z], preferred_element_type=f32)
                    put(z, value.reshape(2, 2, rows, 256))

            if extra is None:
                plain()
                return
            pl.when(k != total - 1)(plain)

            @pl.when(k == total - 1)
            def _():
                more = left[half, 5].reshape(4 * rows, left.shape[-1])
                for z in range(4):
                    value = jnp.dot(lhs, right[k, z], preferred_element_type=f32)
                    value += jnp.dot(more, extra[z], preferred_element_type=f32)
                    put(z, value.reshape(2, 2, rows, 256))

        def places(k):
            by_x, unused, unused = order(k)
            for y_side in range(2):
                for x_side in range(2):
                    first = x_side * by_x + y_side * (1 - by_x)
                    yield y_side, x_side, first, y_side + x_side - first

        def begin(k):
            @pl.when(k >= 2)
            def _():
                copy(k - 2, 0).wait_send()

            def put(z, value):
                for y_side, x_side, first, second in places(k):
                    outgoing[k % 2, first, second, z // 2, z % 2] = value[y_side, x_side].astype(bf16)

            products(k, 1 - c, put)
            copy(k, 0).start()

        def join(k):
            copy(k, 0).wait_recv()

            def put(z, value):
                for y_side, x_side, first, second in places(k):
                    held = r0[k, first, second, z // 2, z % 2].astype(f32)
                    r0[k, first, second, z // 2, z % 2] = (held + value[y_side, x_side]).astype(bf16)

            products(k, c, put)
            copy(k, 1).start()

        def add_into(target, k, kept):
            target[k] = (target[k].astype(f32) + kept.astype(f32)).astype(bf16)

        def second(k):
            copy(k, 1).wait_recv()
            add_into(r1, k, r0[k, order(k)[1]])
            copy(k, 2).start()

        def third(k):
            copy(k, 2).wait_recv()
            add_into(r2, k, r1[k, :, :, low])
            copy(k, 3).start()

        def fourth(k):
            copy(k, 3).wait_recv()
            add_into(r3, k, r2[k, order(k)[2]])
            copy(k, 4).start()

        def last(k):
            copy(k, 4).wait_recv()
            out[k] = r4[k].astype(f32) + r3[k, high].astype(f32)

        def finish():
            def body(k, carry):
                for stage in range(1, 5):
                    copy(k, stage).wait_send()
                return carry

            lax.fori_loop(0, total, body, 0)
            copy(total - 2, 0).wait_send()
            copy(total - 1, 0).wait_send()

        return total, (begin, join, second, third, fourth, last), finish

    text_total, text_stages, text_finish = stream(
        text_left, text_right, text_extra, text_out, text_send,
        (text_r0, text_r1, text_r2, text_r3, text_r4), text_ss, text_rs, TEXT_MARKS, 0,
    )
    image_total, image_stages, image_finish = stream(
        image_left, image_right, None, image_out, image_send,
        (image_r0, image_r1, image_r2, image_r3, image_r4), image_ss, image_rs, IMAGE_MARKS, 1,
    )
    lags = STAGE_LAGS
    partners = (core, along_x, along_y, near, far)

    def norm_copy(stage):
        return pltpu.make_async_remote_copy(
            src_ref=norms if stage == 0 else norm_buf.at[stage - 1],
            dst_ref=norm_buf.at[stage],
            send_sem=norm_ss.at[stage], recv_sem=norm_rs.at[stage],
            device_id=partners[stage], device_id_type=MESH_ID,
        )

    def turn(t, carry):
        for lag, text_stage, image_stage in zip(lags, text_stages, image_stages):
            k = t - lag
            pl.when((k >= 0) & (k < text_total))(functools.partial(text_stage, k))
            pl.when((k >= 0) & (k < image_total))(functools.partial(image_stage, k))
        for stage in range(6):

            @pl.when(t == 2 * stage)
            def _(stage=stage):
                if stage > 0:
                    norm_copy(stage - 1).wait_recv()
                    held = norms[...] if stage == 1 else norm_buf[stage - 2]
                    if stage < 5:
                        norm_buf[stage - 1] += held
                    else:
                        norm_out[...] = norm_buf[stage - 1] + held
                if stage < 5:
                    norm_copy(stage).start()

        return carry

    lax.fori_loop(0, max(text_total, image_total) + lags[-1], turn, 0)
    text_finish()
    image_finish()
    for stage in range(5):
        norm_copy(stage).wait_send()


def reduce_all(text_left, text_right, text_extra, image_left, image_right, norms, unit):
    bf16, f32 = jnp.bfloat16, jnp.float32

    def buffers(right, left):
        total, rows = right.shape[0], left.shape[-2]
        tail = (rows, 256)
        return [
            pltpu.VMEM((total, 2, 2, 2, 2) + tail, bf16),
            pltpu.VMEM((total, 2, 2, 2) + tail, bf16),
            pltpu.VMEM((total, 2, 2) + tail, bf16),
            pltpu.VMEM((total, 2) + tail, bf16),
            pltpu.VMEM((total,) + tail, bf16),
        ]

    def outgoing(left):
        return pltpu.VMEM((2, 2, 2, 2, 2, left.shape[-2], 256), bf16)

    texts, images = text_right.shape[0], image_right.shape[0]
    sems = []
    for total in (texts, images):
        sems += [pltpu.SemaphoreType.DMA((total, 5))] * 2
    sems += [pltpu.SemaphoreType.DMA((5,))] * 2
    return pl.pallas_call(
        functools.partial(reduce_kernel, unit),
        out_shape=[
            jax.ShapeDtypeStruct((texts, text_left.shape[-2], 256), f32),
            jax.ShapeDtypeStruct((images, image_left.shape[-2], 256), f32),
            jax.ShapeDtypeStruct(norms.shape, f32),
        ],
        in_specs=[pl.BlockSpec(memory_space=pltpu.VMEM)] * 6,
        out_specs=[pl.BlockSpec(memory_space=pltpu.VMEM)] * 3,
        scratch_shapes=[outgoing(text_left), outgoing(image_left)]
        + buffers(text_right, text_left)
        + buffers(image_right, image_left)
        + [pltpu.VMEM((5,) + norms.shape, f32)]
        + sems,
        compiler_params=pltpu.CompilerParams(
            collective_id=1, has_side_effects=True, vmem_limit_bytes=67043328
        ),
        name="reduce_gradients",
    )(text_left, text_right, text_extra, image_left, image_right, norms)


ROOT_HALF = math.sqrt(0.5)
DENSITY = 1.0 / math.sqrt(2.0 * math.pi)
TILE = 256
BLOCK = 32


def dot_nn(a, b):
    return jnp.dot(a, b, preferred_element_type=jnp.float32)


def dot_nt(a, b):
    return lax.dot_general(a, b, (((1,), (1,)), ((), ())), preferred_element_type=jnp.float32)


def dot_tn(a, b):
    return lax.dot_general(a, b, (((0,), (0,)), ((), ())), preferred_element_type=jnp.float32)


def row_blocks(rows, body):
    def step(i, carry):
        body(pl.ds(pl.multiple_of(i * BLOCK, BLOCK), BLOCK))
        return carry

    lax.fori_loop(0, rows // BLOCK, step, 0)


def tile_at(j):
    return pl.ds(pl.multiple_of(j * TILE, TILE), TILE)


def probabilities(query, keys, mask, head_size):
    scores = dot_nt(query, keys) * (1.0 / math.sqrt(head_size))
    scores = jnp.where(mask > 0.5, scores, MASKED)
    lifted = jnp.exp(scores - jnp.max(scores, -1, keepdims=True))
    return lifted / jnp.sum(lifted, -1, keepdims=True)


def head_forward(query, keys, values, mask, head_size):
    probs = probabilities(query, keys, mask, head_size)
    return dot_nn(probs.astype(jnp.bfloat16), values).astype(jnp.bfloat16)


def head_back(query, keys, values, mask, head_size, context_grad):
    bf16 = jnp.bfloat16
    probs = probabilities(query, keys, mask, head_size)
    value_grad = dot_tn(probs.astype(bf16), context_grad)
    prob_grad = dot_nt(context_grad, values)
    inner = jnp.sum(probs * prob_grad, -1, keepdims=True)
    score_grad = (probs * (prob_grad - inner)).astype(bf16)
    scale = 1.0 / math.sqrt(head_size)
    query_grad = dot_nn(score_grad, keys) * scale
    key_grad = dot_tn(score_grad, query) * scale
    return query_grad.astype(bf16), key_grad.astype(bf16), value_grad.astype(bf16)


def norm_forward(number, res, acc, xhat, rstd, gains, shifts, lows):
    def block(rows):
        hidden = res[rows, :] + acc[rows, :]
        centred = hidden - jnp.mean(hidden, -1, keepdims=True)
        scale = lax.rsqrt(jnp.mean(centred * centred, -1, keepdims=True) + EPSILON)
        unit = centred * scale
        xhat[number, rows, :] = unit
        rstd[number, rows, :] = jnp.broadcast_to(scale, (BLOCK, 128))
        out = unit * gains[number : number + 1, :] + shifts[number : number + 1, :]
        res[rows, :] = out
        if lows is not None:
            lows[rows, :] = out.astype(jnp.bfloat16)

    row_blocks(res.shape[0], block)


def norm_backward(number, grad, acc, xhat, rstd, gains, low, norms):
    count = gains.shape[0]
    width = grad.shape[1]

    def step(i, carry):
        gain_sum, shift_sum = carry
        rows = pl.ds(pl.multiple_of(i * BLOCK, BLOCK), BLOCK)
        coming = grad[rows, :] if acc is None else grad[rows, :] + acc[rows, :]
        unit = xhat[number, rows, :]
        gain_sum += jnp.sum(coming * unit, 0, keepdims=True)
        shift_sum += jnp.sum(coming, 0, keepdims=True)
        scaled = coming * gains[number : number + 1, :]
        mean = jnp.mean(scaled, -1, keepdims=True)
        slope = jnp.mean(scaled * unit, -1, keepdims=True)
        out = (scaled - mean - unit * slope) * rstd[number, rows, 0:1]
        grad[rows, :] = out
        low[rows, :] = out.astype(jnp.bfloat16)
        return gain_sum, shift_sum

    zero = jnp.zeros((1, width), jnp.float32)
    gain_sum, shift_sum = lax.fori_loop(0, grad.shape[0] // BLOCK, step, (zero, zero))
    norms[number : number + 1, :] = gain_sum
    norms[count + number : count + number + 1, :] = shift_sum


def turn_over(left, tokens, rows):
    part = left.shape[4]
    for number, source in enumerate((tokens, rows.at[2], rows.at[0], rows.at[3], rows.at[1], rows.at[4])):
        turned = source[...].T
        for y in range(2):
            for x in range(2):
                for c in range(2):
                    first = (4 * y + 2 * x + c) * part
                    left[c, number, y, x] = turned[first : first + part]


def layer_kernel(
    lengths, counts, text_tokens, image_tokens, text_cot, image_cot,
    text_gains, text_shifts, image_gains, image_shifts,
    text_cross, image_cross, text_cross_out, image_cross_out, text_up, text_down,
    image_up, image_down, text_self, image_self, image_self_out,
    text_output, image_output, text_grad, image_grad,
    text_left, image_left, text_right, text_extra, image_right, text_norms, image_norms,
    slot, load_sem, text_acc, image_acc, text_xhat, image_xhat, text_rstd, image_rstd,
    text_slope, image_slope, text_qkv, image_qkv, text_sqkv, image_sqkv,
    mask_ti, mask_it, mask_tt, mask_ii, text_rows, image_rows,
):
    f32, bf16 = jnp.float32, jnp.bfloat16
    rows_t, rows_i = text_tokens.shape[0], image_tokens.shape[0]
    width_t, width_i = text_tokens.shape[1], image_tokens.shape[1]
    pairs = lengths.shape[0]
    per_t, per_i = rows_t // pairs, rows_i // pairs
    zs = text_right.shape[1]
    inner = zs * TILE
    ups = text_up.shape[1] // (zs * TILE)

    def whole(ref, row):
        flat = ref
        return [(flat, slice(None), row, ref.shape[-2], ref.shape[-1])]

    def three(ref):
        return [(ref.at[n], slice(None), n * ref.shape[1], ref.shape[1], ref.shape[2]) for n in range(ref.shape[0])]

    wide = slot.shape[2]
    loads = {
        "tc": three(text_cross),
        "ic": three(image_cross),
        "out": whole(text_cross_out, 0) + whole(image_cross_out, inner),
        "tu": [
            (text_up, pl.ds(n * wide, wide), n * width_t, width_t, wide)
            for n in range(text_up.shape[1] // wide)
        ],
        "td": whole(text_down, 0),
        "if": whole(image_up, 0) + whole(image_down, width_i),
        "ts": three(text_self),
        "is": three(image_self),
        "io": whole(image_self_out, 0),
    }
    order = ["tc", "ic", "out", "tu", "td", "if", "ts", "is", "io"]
    order += ["td", "if", "tu", "out", "tc", "ic"]
    slots = [0, 1, 2, 0, 1, 2, 0, 1, 2, 2, 0, 1, 2, 0, 1]

    def copies(number):
        where = slots[number]
        return [
            pltpu.make_async_copy(
                ref.at[:, cols] if isinstance(cols, slice) is False else ref,
                slot.at[where, pl.ds(row, rows), pl.ds(0, width)],
                load_sem.at[number, part],
            )
            for part, (ref, cols, row, rows, width) in enumerate(loads[order[number]])
        ]

    def start(number):
        for copy in copies(number):
            copy.start()

    def ready(number):
        for copy in copies(number):
            copy.wait()
        return slot.at[slots[number]]

    for number in range(3):
        start(number)

    def set_mask(ref, query_per, key_per, limits):
        query = lax.broadcasted_iota(jnp.int32, ref.shape, 0)
        key = lax.broadcasted_iota(jnp.int32, ref.shape, 1)
        seen = jnp.zeros(ref.shape, f32)
        for pair in range(pairs):
            inside = (query >= pair * query_per) & (query < (pair + 1) * query_per)
            inside &= (key >= pair * key_per) & (key < pair * key_per + limits[pair])
            seen = jnp.where(inside, 1.0, seen)
        ref[...] = seen

    set_mask(mask_ti, per_t, per_i, counts)
    set_mask(mask_it, per_i, per_t, lengths)
    set_mask(mask_tt, per_t, per_t, lengths)
    set_mask(mask_ii, per_i, per_i, counts)
    text_output[...] = text_tokens[...].astype(f32)
    image_output[...] = image_tokens[...].astype(f32)

    def clear():
        text_acc[...] = jnp.zeros(text_acc.shape, f32)
        image_acc[...] = jnp.zeros(image_acc.shape, f32)

    clear()

    def project_tiles(rows_ref, weights, width, kept):
        def body(z, carry):
            for n in range(3):
                tile = dot_nn(rows_ref[...], weights[n * width : (n + 1) * width, tile_at(z)])
                kept[n, :, tile_at(z)] = tile.astype(bf16)
            return carry

        lax.fori_loop(0, zs, body, 0)

    def halves(tile):
        return tile[:, :128], tile[:, 128:]

    def pair_heads(fn, count, *tiles):
        size = TILE // count if count == 2 else 64
        results = []
        for h in range(count):
            results.append(fn(*[tile[:, h * size : (h + 1) * size] for tile in tiles]))
        return results

    project_tiles(text_tokens, ready(0), width_t, text_qkv)
    project_tiles(image_tokens, ready(1), width_i, image_qkv)
    start(3)
    start(4)
    outs = ready(2)

    def cross_forward_tile(z, carry):
        tq, tk, tv = [text_qkv[n, :, tile_at(z)] for n in range(3)]
        iq, ik, iv = [image_qkv[n, :, tile_at(z)] for n in range(3)]
        text_heads = pair_heads(
            lambda q, k, v: head_forward(q, k, v, mask_ti[...], CROSS_HEAD), 2, tq, ik, iv
        )
        image_heads = pair_heads(
            lambda q, k, v: head_forward(q, k, v, mask_it[...], CROSS_HEAD), 2, iq, tk, tv
        )
        text_context = jnp.concatenate(text_heads, -1)
        image_context = jnp.concatenate(image_heads, -1)
        text_right[3, z] = text_context
        image_right[3, z] = image_context
        text_acc[...] += dot_nn(text_context, outs[tile_at(z), 0:width_t])
        offset = pl.ds(pl.multiple_of(inner + z * TILE, TILE), TILE)
        image_acc[...] += dot_nn(image_context, outs[offset, 0:width_i])
        return carry

    lax.fori_loop(0, zs, cross_forward_tile, 0)
    start(5)
    norm_forward(0, text_output, text_acc, text_xhat, text_rstd, text_gains, text_shifts, text_rows.at[0])
    norm_forward(0, image_output, image_acc, image_xhat, image_rstd, image_gains, image_shifts, image_rows.at[0])

    def gelu_tile(upper):
        normal = 0.5 * (1.0 + lax.erf(upper * ROOT_HALF))
        slope = normal + upper * (DENSITY * jnp.exp(-0.5 * upper * upper))
        return (upper * normal).astype(bf16), slope

    up_t = ready(3)
    per_wide = wide // TILE

    def text_up_tile(j, carry):
        rows = pl.ds(pl.multiple_of((j // per_wide) * width_t, 8), width_t)
        upper = dot_nn(text_rows[0], up_t[rows, tile_at(j % per_wide)])
        middle, slope = gelu_tile(upper)
        text_slope[j] = slope
        text_right[7 + j % ups, j // ups] = middle
        return carry

    lax.fori_loop(0, zs * ups, text_up_tile, 0)
    start(6)
    down_t = ready(4)
    clear()

    def text_down_tile(j, carry):
        text_acc[...] += dot_nn(text_right[7 + j % ups, j // ups], down_t[tile_at(j), 0:width_t])
        return carry

    lax.fori_loop(0, zs * ups, text_down_tile, 0)
    start(7)
    both_i = ready(5)

    def image_up_tile(z, carry):
        middle, slope = gelu_tile(dot_nn(image_rows[0], both_i[0:width_i, tile_at(z)]))
        image_slope[z] = slope
        image_right[5, z] = middle
        offset = pl.ds(pl.multiple_of(width_i + z * TILE, TILE), TILE)
        image_acc[...] += dot_nn(middle, both_i[offset, 0:width_i])
        return carry

    lax.fori_loop(0, zs, image_up_tile, 0)
    start(8)
    norm_forward(1, text_output, text_acc, text_xhat, text_rstd, text_gains, text_shifts, text_rows.at[1])
    norm_forward(1, image_output, image_acc, image_xhat, image_rstd, image_gains, image_shifts, image_rows.at[1])

    clear()
    self_t = ready(6)
    project_tiles(text_rows.at[1], self_t, width_t, text_sqkv)
    self_i = ready(7)
    project_tiles(image_rows.at[1], self_i, width_i, image_sqkv)
    out_i = ready(8)
    share = TILE - TEXT_HEAD
    heads_t = share // TEXT_HEAD

    def self_forward_tile(z, carry):
        text_tiles = [text_sqkv[n, :, tile_at(z)] for n in range(3)]
        heads = pair_heads(
            lambda q, k, v: head_forward(q, k, v, mask_tt[...], TEXT_HEAD), heads_t, *text_tiles
        )
        blank = jnp.zeros((rows_t, TEXT_HEAD), bf16)
        text_extra[z] = jnp.concatenate([blank] + heads, -1)
        context = jnp.concatenate(heads + [blank], -1)
        text_acc[...] += dot_nt(context, self_t[3 * width_t : 4 * width_t, tile_at(z)])
        image_tiles = [image_sqkv[n, :, tile_at(z)] for n in range(3)]
        image_heads = pair_heads(
            lambda q, k, v: head_forward(q, k, v, mask_ii[...], IMAGE_HEAD), 2, *image_tiles
        )
        image_context = jnp.concatenate(image_heads, -1)
        image_right[9, z] = image_context
        image_acc[...] += dot_nn(image_context, out_i[tile_at(z), 0:width_i])
        return carry

    lax.fori_loop(0, zs, self_forward_tile, 0)
    norm_forward(2, text_output, text_acc, text_xhat, text_rstd, text_gains, text_shifts, None)
    norm_forward(2, image_output, image_acc, image_xhat, image_rstd, image_gains, image_shifts, None)

    text_grad[...] = text_cot[...].astype(f32)
    image_grad[...] = image_cot[...].astype(f32)
    norm_backward(2, text_grad, None, text_xhat, text_rstd, text_gains, text_rows.at[4], text_norms)
    norm_backward(2, image_grad, None, image_xhat, image_rstd, image_gains, image_rows.at[4], image_norms)
    clear()

    def self_back_tile(z, carry):
        text_tiles = [text_sqkv[n, :, tile_at(z)] for n in range(3)]
        context_grad = dot_nt_rows(text_rows[4], self_t, z)
        grads = pair_heads(
            lambda q, k, v, d: head_back(q, k, v, mask_tt[...], TEXT_HEAD, d),
            heads_t, *text_tiles, context_grad,
        )
        blank = jnp.zeros((rows_t, TEXT_HEAD), bf16)
        dq, dk, dv = [[grads[h][n] for h in range(heads_t)] for n in range(3)]
        pieces = dq + dk + dv
        text_right[10, z] = jnp.concatenate(pieces[0:4], -1)
        text_right[11, z] = jnp.concatenate(pieces[4:8], -1)
        text_right[12, z] = jnp.concatenate(pieces[8:9] + [blank] * 3, -1)
        total = jnp.zeros((rows_t, width_t), f32)
        for n, parts in enumerate((dq, dk, dv)):
            joined = jnp.concatenate(parts + [blank], -1)
            total += dot_nt(joined, self_t[n * width_t : (n + 1) * width_t, tile_at(z)])
        text_acc[...] += total
        return carry

    def dot_nt_rows(coming, weights, z):
        return dot_nn(coming, weights[3 * width_t : 4 * width_t, tile_at(z)]).astype(bf16)

    def self_back_image(z, carry):
        image_tiles = [image_sqkv[n, :, tile_at(z)] for n in range(3)]
        context_grad = dot_nt(image_rows[4], out_i[tile_at(z), 0:width_i]).astype(bf16)
        grads = pair_heads(
            lambda q, k, v, d: head_back(q, k, v, mask_ii[...], IMAGE_HEAD, d),
            2, *image_tiles, context_grad,
        )
        total = jnp.zeros((rows_i, width_i), f32)
        for n in range(3):
            joined = jnp.concatenate([grads[0][n], grads[1][n]], -1)
            image_right[6 + n, z] = joined
            total += dot_nt(joined, self_i[n * width_i : (n + 1) * width_i, tile_at(z)])
        image_acc[...] += total
        return carry

    lax.fori_loop(0, zs, self_back_image, 0)
    start(9)
    lax.fori_loop(0, zs, self_back_tile, 0)
    start(10)
    start(11)
    norm_backward(1, text_grad, text_acc, text_xhat, text_rstd, text_gains, text_rows.at[3], text_norms)
    norm_backward(1, image_grad, image_acc, image_xhat, image_rstd, image_gains, image_rows.at[3], image_norms)
    clear()

    back_down = ready(9)

    def text_down_back(j, carry):
        middle_grad = dot_nt(text_rows[3], back_down[tile_at(j), 0:width_t])
        text_right[4 + j % ups, j // ups] = (middle_grad * text_slope[j]).astype(bf16)
        return carry

    lax.fori_loop(0, zs * ups, text_down_back, 0)
    start(12)
    back_i = ready(10)

    def image_ffn_back(z, carry):
        offset = pl.ds(pl.multiple_of(width_i + z * TILE, TILE), TILE)
        middle_grad = dot_nt(image_rows[3], back_i[offset, 0:width_i])
        upper_grad = (middle_grad * image_slope[z]).astype(bf16)
        image_right[4, z] = upper_grad
        image_acc[...] += dot_nt(upper_grad, back_i[0:width_i, tile_at(z)])
        return carry

    lax.fori_loop(0, zs, image_ffn_back, 0)
    start(13)
    back_up = ready(11)

    def text_up_back(j, carry):
        rows = pl.ds(pl.multiple_of((j // per_wide) * width_t, 8), width_t)
        text_acc[...] += dot_nt(text_right[4 + j % ups, j // ups], back_up[rows, tile_at(j % per_wide)])
        return carry

    lax.fori_loop(0, zs * ups, text_up_back, 0)
    start(14)
    norm_backward(0, text_grad, text_acc, text_xhat, text_rstd, text_gains, text_rows.at[2], text_norms)
    norm_backward(0, image_grad, image_acc, image_xhat, image_rstd, image_gains, image_rows.at[2], image_norms)
    clear()

    back_out = ready(12)
    cross_t = ready(13)
    cross_i = ready(14)

    def cross_back_tile(z, carry):
        tq, tk, tv = [text_qkv[n, :, tile_at(z)] for n in range(3)]
        iq, ik, iv = [image_qkv[n, :, tile_at(z)] for n in range(3)]
        text_ctx_grad = dot_nt(text_rows[2], back_out[tile_at(z), 0:width_t]).astype(bf16)
        offset = pl.ds(pl.multiple_of(inner + z * TILE, TILE), TILE)
        image_ctx_grad = dot_nt(image_rows[2], back_out[offset, 0:width_i]).astype(bf16)
        text_side = pair_heads(
            lambda q, k, v, d: head_back(q, k, v, mask_ti[...], CROSS_HEAD, d), 2, tq, ik, iv, text_ctx_grad
        )
        image_side = pair_heads(
            lambda q, k, v, d: head_back(q, k, v, mask_it[...], CROSS_HEAD, d), 2, iq, tk, tv, image_ctx_grad
        )

        def joined(side, n):
            return jnp.concatenate([side[0][n], side[1][n]], -1)

        text_parts = (joined(text_side, 0), joined(image_side, 1), joined(image_side, 2))
        image_parts = (joined(image_side, 0), joined(text_side, 1), joined(text_side, 2))
        total_t = jnp.zeros((rows_t, width_t), f32)
        total_i = jnp.zeros((rows_i, width_i), f32)
        for n in range(3):
            text_right[n, z] = text_parts[n]
            image_right[n, z] = image_parts[n]
            total_t += dot_nt(text_parts[n], cross_t[n * width_t : (n + 1) * width_t, tile_at(z)])
            total_i += dot_nt(image_parts[n], cross_i[n * width_i : (n + 1) * width_i, tile_at(z)])
        text_acc[...] += total_t
        image_acc[...] += total_i
        return carry

    lax.fori_loop(0, zs, cross_back_tile, 0)
    text_grad[...] += text_acc[...]
    image_grad[...] += image_acc[...]
    turn_over(text_left, text_tokens, text_rows)
    turn_over(image_left, image_tokens, image_rows)


def layer(lengths, counts, rows, params, weights, mp):
    f32, bf16 = jnp.float32, jnp.bfloat16
    text_tokens, image_tokens = rows[0], rows[1]
    rows_t, width_t = text_tokens.shape
    rows_i, width_i = image_tokens.shape
    text_up = weights[4]
    text_tiles = text_up.shape[1] // TILE
    inner = mp * TILE

    vmem = pl.BlockSpec(memory_space=pltpu.VMEM)
    out_shape = [
        jax.ShapeDtypeStruct((rows_t, width_t), f32),
        jax.ShapeDtypeStruct((rows_i, width_i), f32),
        jax.ShapeDtypeStruct((rows_t, width_t), f32),
        jax.ShapeDtypeStruct((rows_i, width_i), f32),
        jax.ShapeDtypeStruct((2, 6, 2, 2, width_t // 8, rows_t), bf16),
        jax.ShapeDtypeStruct((2, 6, 2, 2, width_i // 8, rows_i), bf16),
        jax.ShapeDtypeStruct((13, mp, rows_t, TILE), bf16),
        jax.ShapeDtypeStruct((mp, rows_t, TILE), bf16),
        jax.ShapeDtypeStruct((10, mp, rows_i, TILE), bf16),
        jax.ShapeDtypeStruct((2 * params[0].shape[0], width_t), f32),
        jax.ShapeDtypeStruct((2 * params[0].shape[0], width_i), f32),
    ]
    return pl.pallas_call(
        layer_kernel,
        out_shape=out_shape,
        in_specs=[pl.BlockSpec(memory_space=pltpu.SMEM)] * 2
        + [vmem] * 8
        + [pl.BlockSpec(memory_space=pl.ANY)] * len(weights),
        out_specs=[vmem] * len(out_shape),
        scratch_shapes=[
            pltpu.VMEM((3, 3 * width_i, inner), bf16),
            pltpu.SemaphoreType.DMA((15, 4)),
            pltpu.VMEM((rows_t, width_t), f32),
            pltpu.VMEM((rows_i, width_i), f32),
            pltpu.VMEM((3, rows_t, width_t), f32),
            pltpu.VMEM((3, rows_i, width_i), f32),
            pltpu.VMEM((3, rows_t, 128), f32),
            pltpu.VMEM((3, rows_i, 128), f32),
            pltpu.VMEM((text_tiles, rows_t, TILE), f32),
            pltpu.VMEM((mp, rows_i, TILE), f32),
            pltpu.VMEM((3, rows_t, inner), bf16),
            pltpu.VMEM((3, rows_i, inner), bf16),
            pltpu.VMEM((3, rows_t, inner), bf16),
            pltpu.VMEM((3, rows_i, inner), bf16),
            pltpu.VMEM((rows_t, rows_i), f32),
            pltpu.VMEM((rows_i, rows_t), f32),
            pltpu.VMEM((rows_t, rows_t), f32),
            pltpu.VMEM((rows_i, rows_i), f32),
            pltpu.VMEM((5, rows_t, width_t), bf16),
            pltpu.VMEM((5, rows_i, width_i), bf16),
        ],
        compiler_params=pltpu.CompilerParams(vmem_limit_bytes=67043328),
        name="layer",
    )(lengths, counts, *rows, *params, *weights)


def shards(
    text_tokens, image_regions, lengths, region_counts, text_cross, image_cross, text_cross_out,
    image_cross_out, text_up, text_down, image_up, image_down, text_self, text_self_out, image_self,
    image_self_out, text_gains, text_shifts, image_gains, image_shifts, text_cotangent, image_cotangent,
):
    mp, dp = lax.axis_size("mp"), lax.axis_size("dp")
    more = dp // 8
    text_out_turned = text_self_out.T[None]
    text_four = jnp.concatenate([text_self, text_out_turned])
    spare = 256 - text_four.shape[-1]
    text_four = jnp.pad(text_four, ((0, 0), (0, 0), (0, spare)))
    weights = gather_all(
        (
            text_cross, image_cross, text_cross_out, image_cross_out, text_up, text_down, image_up,
            image_down, text_four, image_self, image_self_out,
        ),
        KINDS, chunk_plan(), mp, more,
    )
    pairs, regions = image_regions.shape[0], image_regions.shape[1]
    padding = (-regions) % 16

    def pad_regions(array):
        return jnp.pad(array, ((0, 0), (0, padding), (0, 0))).reshape(-1, array.shape[-1])

    def flat(array):
        return array.reshape(-1, array.shape[-1])

    (
        text_result, image_result, text_input_grad, image_input_grad,
        text_left, image_left, text_right, text_extra, image_right, text_norms, image_norms,
    ) = layer(
        lengths, region_counts,
        (flat(text_tokens), pad_regions(image_regions), flat(text_cotangent), pad_regions(image_cotangent)),
        (text_gains, text_shifts, image_gains, image_shifts),
        weights, mp,
    )
    text_result, text_input_grad = [
        array.reshape(text_tokens.shape) for array in (text_result, text_input_grad)
    ]
    image_result, image_input_grad = [
        array.reshape(pairs, regions + padding, -1)[:, :regions]
        for array in (image_result, image_input_grad)
    ]
    norms = jnp.concatenate([text_norms.reshape(-1, 128), image_norms.reshape(-1, 128)])
    text_sums, image_sums, norm_sums = reduce_all(
        text_left, text_right, text_extra, image_left, image_right, norms, more
    )
    if more > 1:
        norm_sums = lax.psum(norm_sums, "dp") / 8
        text_sums, image_sums = outer_sum(text_sums, more), outer_sum(image_sums, more)
    text_sums = text_sums.transpose(1, 0, 2).reshape(text_sums.shape[1], -1)
    image_sums = image_sums.transpose(1, 0, 2).reshape(image_sums.shape[1], -1)

    def columns(sums, widths):
        parts, start = [], 0
        for width in widths:
            parts.append(sums[:, start : start + width])
            start += width
        return parts

    def triple(parts):
        return jnp.stack(parts[:3])

    text_widths = [text_cross.shape[-1]] * 3 + [text_cross_out.shape[0]]
    text_widths += [text_up.shape[-1], text_down.shape[0]]
    text_widths += [text_self.shape[-1]] * 3 + [text_self_out.shape[0]]
    image_widths = [image_cross.shape[-1]] * 3 + [image_cross_out.shape[0]]
    image_widths += [image_up.shape[-1], image_down.shape[0]]
    image_widths += [image_self.shape[-1]] * 3 + [image_self_out.shape[0]]
    text_parts = columns(text_sums, text_widths)
    image_parts = columns(image_sums, image_widths)
    flat_norms = norm_sums.reshape(-1)
    text_size, image_size = text_gains.size, image_gains.size
    text_end = 2 * text_size
    return (
        text_result,
        image_result,
        text_input_grad,
        image_input_grad,
        triple(text_parts[:3]),
        triple(image_parts[:3]),
        text_parts[3].T,
        image_parts[3].T,
        text_parts[4],
        text_parts[5].T,
        image_parts[4],
        image_parts[5].T,
        triple(text_parts[6:9]),
        text_parts[9].T,
        triple(image_parts[6:9]),
        image_parts[9].T,
        flat_norms[:text_size].reshape(text_gains.shape),
        flat_norms[text_size:text_end].reshape(text_shifts.shape),
        flat_norms[text_end : text_end + image_size].reshape(image_gains.shape),
        flat_norms[text_end + image_size :].reshape(image_shifts.shape),
    )


def outer_sum(sums, more):
    chunks, rows, width = sums.shape
    apart = sums.reshape(chunks, 1, more, rows // more, width)
    low = lax.axis_index("dp") // more
    spread = jnp.zeros((chunks, 8, more, rows // more, width), sums.dtype)
    spread = lax.dynamic_update_slice(spread, apart, (0, low, 0, 0, 0))
    spread = spread.reshape(chunks, 8 * rows, width)
    return lax.psum_scatter(spread, "dp", scatter_dimension=1, tiled=True)


def solution(mesh):
    in_specs = (
        P(("dp", "mp"), None, None),
        P(("dp", "mp"), None, None),
        P(("dp", "mp")),
        P(("dp", "mp")),
        P(None, None, "mp"),
        P(None, None, "mp"),
        P("mp", None),
        P("mp", None),
        P(None, "mp"),
        P("mp", None),
        P(None, "mp"),
        P("mp", None),
        P(None, None, "mp"),
        P("mp", None),
        P(None, None, "mp"),
        P("mp", None),
        P(),
        P(),
        P(),
        P(),
        P(("dp", "mp"), None, None),
        P(("dp", "mp"), None, None),
    )
    out_specs = (
        P(("dp", "mp"), None, None),
        P(("dp", "mp"), None, None),
        P(("dp", "mp"), None, None),
        P(("dp", "mp"), None, None),
        P(None, "dp", "mp"),
        P(None, "dp", "mp"),
        P("mp", "dp"),
        P("mp", "dp"),
        P("dp", "mp"),
        P("mp", "dp"),
        P("dp", "mp"),
        P("mp", "dp"),
        P(None, "dp", "mp"),
        P("mp", "dp"),
        P(None, "dp", "mp"),
        P("mp", "dp"),
        P(),
        P(),
        P(),
        P(),
    )
    return jax.shard_map(shards, mesh=mesh, in_specs=in_specs, out_specs=out_specs, check_vma=False)
```

```python
import functools
import math

import jax
import jax.numpy as jnp
from jax import lax
from jax.experimental import pallas as pl
from jax.experimental.pallas import tpu as pltpu
from jax.sharding import PartitionSpec as P

TEXT_HEAD = 64
CROSS_HEAD = 128
IMAGE_HEAD = 128


EPSILON = 1e-05
MASKED = -1e30
MESH_ID = pl.DeviceIdType.MESH


def flip(index, step):
    return index + step * (1 - 2 * ((index // step) % 2))


def position(unit):
    data, model = lax.axis_index("dp"), lax.axis_index("mp")
    return data, model, (data // unit) % 2, (data // (2 * unit)) % 2, (data // (4 * unit)) % 2


def greet(data, model, unit):
    barrier = pltpu.get_barrier_semaphore()
    partners = [(flip(data, step * unit), model) for step in (1, 2, 4)]
    partners += [(data, flip(model, step)) for step in (1, 2)]
    for partner in partners:
        pl.semaphore_signal(barrier, inc=1, device_id=partner, device_id_type=MESH_ID)
    pl.semaphore_wait(barrier, len(partners))


LAGS = (0, 2, 4, 6, 8)


def gather_steps(unit, kinds, chunks, ins, outs, send_sem, recv_sem):
    data, model, c, x, y = position(unit)
    near, far = flip(model, 1), flip(model, 2)
    corner = flip(near, 2)
    copies = {}

    def send(n, slot, source, target, partner):
        copies[n, slot] = pltpu.make_async_remote_copy(
            src_ref=source,
            dst_ref=target,
            send_sem=send_sem.at[n, slot],
            recv_sem=recv_sem.at[n, slot],
            device_id=partner,
            device_id_type=MESH_ID,
        )
        copies[n, slot].start()

    def rows_of(height, first, base, span):
        start, count = span
        return pl.ds(pl.multiple_of(base + start * (height // 8), 8), count * (height // 8))

    def mine(n, span):
        k, matrix, unused, unused = chunks[n]
        if kinds[k] == "cols":
            return ins[k].at[matrix, rows_of(ins[k].shape[1], 0, 0, span), :]
        return ins[k].at[rows_of(ins[k].shape[0], 0, 0, span), :]

    def piece(n, shard, span):
        k, matrix, unused, unused = chunks[n]
        if kinds[k] == "cols":
            width = ins[k].shape[2]
            columns = pl.ds(pl.multiple_of(shard * width, 128), width)
            return outs[k].at[matrix, rows_of(ins[k].shape[1], 0, 0, span), columns]
        height = ins[k].shape[0]
        return outs[k].at[rows_of(height, 0, shard * height, span), :]

    x_side = (flip(data, 2 * unit), model)
    y_side = (flip(data, 4 * unit), model)
    z_side = (data, near)

    def relay(n, slot, shard, span, partner):
        block = piece(n, shard, span)
        send(n, slot, block, block, partner)

    def advance(n, stage):
        x_first, early = chunks[n][2:]
        first, second = (x_side, y_side) if x_first else (y_side, x_side)
        low_bit, middle_bit = (x, y) if x_first else (y, x)
        single = (4 * c + 2 * middle_bit + low_bit, 1)
        double = (4 * c + 2 * middle_bit, 2)
        if stage == 0:
            send(n, 0, mine(n, single), piece(n, model, single), (data, far))
        elif stage == 1 and not early:
            send(n, 1, mine(n, single), piece(n, model, single), z_side)
            copies[n, 0].wait_recv()
            relay(n, 2, far, single, z_side)
        elif stage == 2 and not early:
            relay(n, 3, far, single, first)
            copies[n, 1].wait_recv()
            relay(n, 4, near, single, first)
            copies[n, 2].wait_recv()
            relay(n, 5, corner, single, first)
        elif stage == 1:
            copies[n, 0].wait_recv()
            relay(n, 3, far, single, first)
        elif stage == 2:
            send(n, 1, mine(n, double), piece(n, model, double), z_side)
            copies[n, 3].wait_recv()
            relay(n, 2, far, double, z_side)
        elif stage == 3:
            before = (None, 1, 2) if early else (3, 4, 5)
            for number, shard in enumerate((far, near, corner)):
                if before[number] is not None:
                    copies[n, before[number]].wait_recv()
                relay(n, 6 + number, shard, double, second)
        else:
            for number, shard in enumerate((far, near, corner)):
                copies[n, 6 + number].wait_recv()
                relay(n, 9 + number, shard, (4 * c, 4), (flip(data, unit), model))

    total = len(chunks)
    done = [0]

    def run(limit):
        while done[0] < min(limit, total + LAGS[-1]):
            for stage, lag in enumerate(LAGS):
                if 0 <= done[0] - lag < total:
                    advance(done[0] - lag, stage)
            done[0] += 1

    def arrived(numbers):
        run(max(numbers) + LAGS[-1] + 1)
        for n in numbers:
            for slot in range(9, 12):
                copies[n, slot].wait_recv()

    def finish():
        for copy in copies.values():
            copy.wait_send()

    return run, arrived, finish


KINDS = ("cols", "cols", "rows", "rows", "cols", "rows", "cols", "rows", "cols", "cols", "rows")
SEQUENCE = (
    (0, 0), (1, 0), (0, 1), (1, 1), (0, 2), (1, 2), (2, None), (3, None), (4, 0), (6, 0), (5, None), (7, None),
    (8, 0), (9, 0), (8, 1), (9, 1), (8, 2), (9, 2), (8, 3), (10, None),
)


def chunk_plan():
    return tuple(
        (k, matrix, n % 4 in (0, 3), n % 2 == 1) for n, (k, matrix) in enumerate(SEQUENCE)
    )


def steps_up(k, marks):
    total = 0
    for mark in marks:
        total = total + jnp.where(k >= mark, 1, 0)
    return total


STAGE_LAGS = (0, 2, 4, 6, 8, 10)
TEXT_MARKS = (3, 4, 7, 10)
IMAGE_MARKS = (3, 4, 5, 6, 9)


def reduce_kernel(
    unit,
    text_left, text_right, text_extra, image_left, image_right, norms,
    text_out, image_out, norm_out,
    text_send, image_send,
    text_r0, text_r1, text_r2, text_r3, text_r4,
    image_r0, image_r1, image_r2, image_r3, image_r4,
    norm_buf,
    text_ss, text_rs, image_ss, image_rs, norm_ss, norm_rs,
):
    data, model, c, x, y = position(unit)
    low, high = model % 2, (model // 2) % 2
    f32, bf16 = jnp.float32, jnp.bfloat16
    core = (flip(data, unit), model)
    along_x = (flip(data, 2 * unit), model)
    along_y = (flip(data, 4 * unit), model)
    near = (data, flip(model, 1))
    far = (data, flip(model, 2))
    greet(data, model, unit)

    def stream(left, right, extra, out, outgoing, bufs, send_sem, recv_sem, marks, turn_first):
        r0, r1, r2, r3, r4 = bufs
        total = right.shape[0]
        rows = left.shape[-2]

        def order(k):
            by_y = (k + turn_first) % 2
            by_x = 1 - by_y
            first, second = x * by_x + y * by_y, y * by_x + x * by_y
            return by_x, first, second

        def copy(k, stage):
            by_x, first, second = order(k)
            if stage == 0:
                pair = (outgoing.at[k % 2], r0.at[k], core)
            elif stage == 1:
                pair = (r0.at[k, 1 - first], r1.at[k], (flip(data, (4 - 2 * by_x) * unit), model))
            elif stage == 2:
                pair = (r1.at[k, :, :, 1 - low], r2.at[k], near)
            elif stage == 3:
                pair = (r2.at[k, 1 - second], r3.at[k], (flip(data, (2 + 2 * by_x) * unit), model))
            else:
                pair = (r3.at[k, 1 - high], r4.at[k], far)
            return pltpu.make_async_remote_copy(
                src_ref=pair[0], dst_ref=pair[1],
                send_sem=send_sem.at[k, stage], recv_sem=recv_sem.at[k, stage],
                device_id=pair[2], device_id_type=MESH_ID,
            )

        def products(k, half, put):
            lhs = left[half, steps_up(k, marks)].reshape(4 * rows, left.shape[-1])

            def plain():
                for z in range(4):
                    value = jnp.dot(lhs, right[k, z], preferred_element_type=f32)
                    put(z, value.reshape(2, 2, rows, 256))

            if extra is None:
                plain()
                return
            pl.when(k != total - 1)(plain)

            @pl.when(k == total - 1)
            def _():
                more = left[half, 5].reshape(4 * rows, left.shape[-1])
                for z in range(4):
                    value = jnp.dot(lhs, right[k, z], preferred_element_type=f32)
                    value += jnp.dot(more, extra[z], preferred_element_type=f32)
                    put(z, value.reshape(2, 2, rows, 256))

        def places(k):
            by_x, unused, unused = order(k)
            for y_side in range(2):
                for x_side in range(2):
                    first = x_side * by_x + y_side * (1 - by_x)
                    yield y_side, x_side, first, y_side + x_side - first

        def begin(k):
            @pl.when(k >= 2)
            def _():
                copy(k - 2, 0).wait_send()

            def put(z, value):
                for y_side, x_side, first, second in places(k):
                    outgoing[k % 2, first, second, z // 2, z % 2] = value[y_side, x_side].astype(bf16)

            products(k, 1 - c, put)
            copy(k, 0).start()

        def join(k):
            copy(k, 0).wait_recv()

            def put(z, value):
                for y_side, x_side, first, second in places(k):
                    held = r0[k, first, second, z // 2, z % 2].astype(f32)
                    r0[k, first, second, z // 2, z % 2] = (held + value[y_side, x_side]).astype(bf16)

            products(k, c, put)
            copy(k, 1).start()

        def add_into(target, k, kept):
            target[k] = (target[k].astype(f32) + kept.astype(f32)).astype(bf16)

        def second(k):
            copy(k, 1).wait_recv()
            add_into(r1, k, r0[k, order(k)[1]])
            copy(k, 2).start()

        def third(k):
            copy(k, 2).wait_recv()
            add_into(r2, k, r1[k, :, :, low])
            copy(k, 3).start()

        def fourth(k):
            copy(k, 3).wait_recv()
            add_into(r3, k, r2[k, order(k)[2]])
            copy(k, 4).start()

        def last(k):
            copy(k, 4).wait_recv()
            out[k] = r4[k].astype(f32) + r3[k, high].astype(f32)

        def finish():
            def body(k, carry):
                for stage in range(1, 5):
                    copy(k, stage).wait_send()
                return carry

            lax.fori_loop(0, total, body, 0)
            copy(total - 2, 0).wait_send()
            copy(total - 1, 0).wait_send()

        return total, (begin, join, second, third, fourth, last), finish

    text_total, text_stages, text_finish = stream(
        text_left, text_right, text_extra, text_out, text_send,
        (text_r0, text_r1, text_r2, text_r3, text_r4), text_ss, text_rs, TEXT_MARKS, 0,
    )
    image_total, image_stages, image_finish = stream(
        image_left, image_right, None, image_out, image_send,
        (image_r0, image_r1, image_r2, image_r3, image_r4), image_ss, image_rs, IMAGE_MARKS, 1,
    )
    lags = STAGE_LAGS
    partners = (core, along_x, along_y, near, far)

    def norm_copy(stage):
        return pltpu.make_async_remote_copy(
            src_ref=norms if stage == 0 else norm_buf.at[stage - 1],
            dst_ref=norm_buf.at[stage],
            send_sem=norm_ss.at[stage], recv_sem=norm_rs.at[stage],
            device_id=partners[stage], device_id_type=MESH_ID,
        )

    def turn(t, carry):
        for lag, text_stage, image_stage in zip(lags, text_stages, image_stages):
            k = t - lag
            pl.when((k >= 0) & (k < text_total))(functools.partial(text_stage, k))
            pl.when((k >= 0) & (k < image_total))(functools.partial(image_stage, k))
        for stage in range(6):

            @pl.when(t == 2 * stage)
            def _(stage=stage):
                if stage > 0:
                    norm_copy(stage - 1).wait_recv()
                    held = norms[...] if stage == 1 else norm_buf[stage - 2]
                    if stage < 5:
                        norm_buf[stage - 1] += held
                    else:
                        norm_out[...] = norm_buf[stage - 1] + held
                if stage < 5:
                    norm_copy(stage).start()

        return carry

    lax.fori_loop(0, max(text_total, image_total) + lags[-1], turn, 0)
    text_finish()
    image_finish()
    for stage in range(5):
        norm_copy(stage).wait_send()


def reduce_all(text_left, text_right, text_extra, image_left, image_right, norms, unit):
    bf16, f32 = jnp.bfloat16, jnp.float32

    def buffers(right, left):
        total, rows = right.shape[0], left.shape[-2]
        tail = (rows, 256)
        return [
            pltpu.VMEM((total, 2, 2, 2, 2) + tail, bf16),
            pltpu.VMEM((total, 2, 2, 2) + tail, bf16),
            pltpu.VMEM((total, 2, 2) + tail, bf16),
            pltpu.VMEM((total, 2) + tail, bf16),
            pltpu.VMEM((total,) + tail, bf16),
        ]

    def outgoing(left):
        return pltpu.VMEM((2, 2, 2, 2, 2, left.shape[-2], 256), bf16)

    texts, images = text_right.shape[0], image_right.shape[0]
    sems = []
    for total in (texts, images):
        sems += [pltpu.SemaphoreType.DMA((total, 5))] * 2
    sems += [pltpu.SemaphoreType.DMA((5,))] * 2
    return pl.pallas_call(
        functools.partial(reduce_kernel, unit),
        out_shape=[
            jax.ShapeDtypeStruct((texts, text_left.shape[-2], 256), f32),
            jax.ShapeDtypeStruct((images, image_left.shape[-2], 256), f32),
            jax.ShapeDtypeStruct(norms.shape, f32),
        ],
        in_specs=[pl.BlockSpec(memory_space=pltpu.VMEM)] * 6,
        out_specs=[pl.BlockSpec(memory_space=pltpu.VMEM)] * 3,
        scratch_shapes=[outgoing(text_left), outgoing(image_left)]
        + buffers(text_right, text_left)
        + buffers(image_right, image_left)
        + [pltpu.VMEM((5,) + norms.shape, f32)]
        + sems,
        compiler_params=pltpu.CompilerParams(
            collective_id=1, has_side_effects=True, vmem_limit_bytes=67043328
        ),
        name="reduce_gradients",
    )(text_left, text_right, text_extra, image_left, image_right, norms)


ROOT_HALF = math.sqrt(0.5)
DENSITY = 1.0 / math.sqrt(2.0 * math.pi)
TILE = 256
BLOCK = 32


def dot_nn(a, b):
    return jnp.dot(a, b, preferred_element_type=jnp.float32)


def dot_nt(a, b):
    return lax.dot_general(a, b, (((1,), (1,)), ((), ())), preferred_element_type=jnp.float32)


def dot_tn(a, b):
    return lax.dot_general(a, b, (((0,), (0,)), ((), ())), preferred_element_type=jnp.float32)


def row_blocks(rows, body):
    def step(i, carry):
        body(pl.ds(pl.multiple_of(i * BLOCK, BLOCK), BLOCK))
        return carry

    lax.fori_loop(0, rows // BLOCK, step, 0)


def tile_at(j):
    return pl.ds(pl.multiple_of(j * TILE, TILE), TILE)


def probabilities(query, keys, mask, head_size):
    scores = dot_nt(query, keys) * (1.0 / math.sqrt(head_size))
    scores = jnp.where(mask > 0.5, scores, MASKED)
    lifted = jnp.exp(scores - jnp.max(scores, -1, keepdims=True))
    return lifted / jnp.sum(lifted, -1, keepdims=True)


def head_forward(query, keys, values, mask, head_size):
    probs = probabilities(query, keys, mask, head_size)
    return dot_nn(probs.astype(jnp.bfloat16), values).astype(jnp.bfloat16)


def head_back(query, keys, values, mask, head_size, context_grad):
    bf16 = jnp.bfloat16
    probs = probabilities(query, keys, mask, head_size)
    value_grad = dot_tn(probs.astype(bf16), context_grad)
    prob_grad = dot_nt(context_grad, values)
    inner = jnp.sum(probs * prob_grad, -1, keepdims=True)
    score_grad = (probs * (prob_grad - inner)).astype(bf16)
    scale = 1.0 / math.sqrt(head_size)
    query_grad = dot_nn(score_grad, keys) * scale
    key_grad = dot_tn(score_grad, query) * scale
    return query_grad.astype(bf16), key_grad.astype(bf16), value_grad.astype(bf16)


def norm_forward(number, res, acc, xhat, rstd, gains, shifts, lows):
    def block(rows):
        hidden = res[rows, :] + acc[rows, :]
        centred = hidden - jnp.mean(hidden, -1, keepdims=True)
        scale = lax.rsqrt(jnp.mean(centred * centred, -1, keepdims=True) + EPSILON)
        unit = centred * scale
        xhat[number, rows, :] = unit
        rstd[number, rows, :] = jnp.broadcast_to(scale, (BLOCK, 128))
        out = unit * gains[number : number + 1, :] + shifts[number : number + 1, :]
        res[rows, :] = out
        if lows is not None:
            lows[rows, :] = out.astype(jnp.bfloat16)

    row_blocks(res.shape[0], block)


def norm_backward(number, grad, acc, xhat, rstd, gains, low, norms):
    count = gains.shape[0]
    width = grad.shape[1]

    def step(i, carry):
        gain_sum, shift_sum = carry
        rows = pl.ds(pl.multiple_of(i * BLOCK, BLOCK), BLOCK)
        coming = grad[rows, :] if acc is None else grad[rows, :] + acc[rows, :]
        unit = xhat[number, rows, :]
        gain_sum += jnp.sum(coming * unit, 0, keepdims=True)
        shift_sum += jnp.sum(coming, 0, keepdims=True)
        scaled = coming * gains[number : number + 1, :]
        mean = jnp.mean(scaled, -1, keepdims=True)
        slope = jnp.mean(scaled * unit, -1, keepdims=True)
        out = (scaled - mean - unit * slope) * rstd[number, rows, 0:1]
        grad[rows, :] = out
        low[rows, :] = out.astype(jnp.bfloat16)
        return gain_sum, shift_sum

    zero = jnp.zeros((1, width), jnp.float32)
    gain_sum, shift_sum = lax.fori_loop(0, grad.shape[0] // BLOCK, step, (zero, zero))
    norms[number : number + 1, :] = gain_sum
    norms[count + number : count + number + 1, :] = shift_sum


def turn_over(left, tokens, rows):
    part = left.shape[4]
    for number, source in enumerate((tokens, rows.at[2], rows.at[0], rows.at[3], rows.at[1], rows.at[4])):
        turned = source[...].T
        for y in range(2):
            for x in range(2):
                for c in range(2):
                    first = (4 * y + 2 * x + c) * part
                    left[c, number, y, x] = turned[first : first + part]


def layer_kernel(
    unit,
    lengths, counts, text_tokens, image_tokens, text_cot, image_cot,
    text_gains, text_shifts, image_gains, image_shifts,
    in_a, in_b, in_c, in_d, in_e, in_f, in_g, in_h, in_i, in_j, in_k,
    text_output, image_output, text_grad, image_grad,
    text_left, image_left, text_right, text_extra, image_right, text_norms, image_norms,
    full_a, full_b, full_c, full_d, full_e, full_f, full_g, full_h, full_i, full_j, full_k,
    send_sem, recv_sem, slot, load_sem, text_acc, image_acc, text_xhat, image_xhat, text_rstd, image_rstd,
    text_slope, image_slope, text_qkv, image_qkv, text_sqkv, image_sqkv,
    mask_ti, mask_it, mask_tt, mask_ii, text_rows, image_rows,
):
    f32, bf16 = jnp.float32, jnp.bfloat16
    rows_t, rows_i = text_tokens.shape[0], image_tokens.shape[0]
    width_t, width_i = text_tokens.shape[1], image_tokens.shape[1]
    pairs = lengths.shape[0]
    per_t, per_i = rows_t // pairs, rows_i // pairs
    zs = text_right.shape[1]
    inner = zs * TILE
    ins = (in_a, in_b, in_c, in_d, in_e, in_f, in_g, in_h, in_i, in_j, in_k)
    fulls = (full_a, full_b, full_c, full_d, full_e, full_f, full_g, full_h, full_i, full_j, full_k)
    ups = in_e.shape[2] // TILE
    data, model, unused, unused, unused = position(unit)
    greet(data, model, unit)
    run, arrived, finish = gather_steps(unit, KINDS, chunk_plan(), ins, fulls, send_sem, recv_sem)
    run(6)

    def three(k):
        return [(k, n, n * ins[k].shape[1], False) for n in range(ins[k].shape[0])]

    loads = {
        "tc": three(0),
        "ic": three(1),
        "out": [(2, None, 0, False), (3, None, inner, False)],
        "tu": [(4, 0, 0, True)],
        "td": [(5, None, 0, False)],
        "if": [(6, 0, 0, False), (7, None, width_i, False)],
        "ts": three(8),
        "is": three(9),
        "io": [(10, None, 0, False)],
    }
    order = ["tc", "ic", "out", "tu", "td", "if", "ts", "is", "io"]
    order += ["td", "if", "tu", "out", "tc", "ic"]
    slots = [0, 1, 2, 0, 1, 2, 0, 1, 2, 2, 0, 1, 2, 0, 1]

    def copies(number):
        where, found = slots[number], []
        for k, matrix, row, stacked in loads[order[number]]:
            for turn in range(zs):
                shard = (model + turn) % zs
                if matrix is None:
                    height, width = ins[k].shape
                    source = fulls[k].at[pl.ds(pl.multiple_of(shard * height, 8), height), :]
                    source = ins[k] if turn == 0 else source
                    rows = pl.ds(pl.multiple_of(row + shard * height, 8), height)
                    target = slot.at[where, rows, pl.ds(0, width)]
                else:
                    unused, height, width = ins[k].shape
                    columns = pl.ds(pl.multiple_of(shard * width, 128), width)
                    source = ins[k].at[matrix] if turn == 0 else fulls[k].at[matrix, :, columns]
                    if stacked:
                        rows = pl.ds(pl.multiple_of(row + shard * height, 8), height)
                        target = slot.at[where, rows, pl.ds(0, width)]
                    else:
                        target = slot.at[where, pl.ds(row, height), columns]
                found.append(pltpu.make_async_copy(source, target, load_sem.at[number, len(found)]))
        return found

    def start(number):
        if number < 9:
            wanted = {k for k, unused, unused, unused in loads[order[number]]}
            arrived([n for n, chunk in enumerate(SEQUENCE) if chunk[0] in wanted])
        for copy in copies(number):
            copy.start()

    def ready(number):
        for copy in copies(number):
            copy.wait()
        return slot.at[slots[number]]

    def set_mask(ref, query_per, key_per, limits):
        query = lax.broadcasted_iota(jnp.int32, ref.shape, 0)
        key = lax.broadcasted_iota(jnp.int32, ref.shape, 1)
        seen = jnp.zeros(ref.shape, f32)
        for pair in range(pairs):
            inside = (query >= pair * query_per) & (query < (pair + 1) * query_per)
            inside &= (key >= pair * key_per) & (key < pair * key_per + limits[pair])
            seen = jnp.where(inside, 1.0, seen)
        ref[...] = seen

    set_mask(mask_ti, per_t, per_i, counts)
    set_mask(mask_it, per_i, per_t, lengths)
    set_mask(mask_tt, per_t, per_t, lengths)
    set_mask(mask_ii, per_i, per_i, counts)
    text_output[...] = text_tokens[...].astype(f32)
    image_output[...] = image_tokens[...].astype(f32)

    def clear():
        text_acc[...] = jnp.zeros(text_acc.shape, f32)
        image_acc[...] = jnp.zeros(image_acc.shape, f32)

    clear()

    def project_tiles(rows_ref, weights, width, kept):
        def body(z, carry):
            for n in range(3):
                tile = dot_nn(rows_ref[...], weights[n * width : (n + 1) * width, tile_at(z)])
                kept[n, :, tile_at(z)] = tile.astype(bf16)
            return carry

        lax.fori_loop(0, zs, body, 0)

    def halves(tile):
        return tile[:, :128], tile[:, 128:]

    def pair_heads(fn, count, *tiles):
        size = TILE // count if count == 2 else 64
        results = []
        for h in range(count):
            results.append(fn(*[tile[:, h * size : (h + 1) * size] for tile in tiles]))
        return results

    start(0)
    start(1)
    run(16)
    project_tiles(text_tokens, ready(0), width_t, text_qkv)
    start(2)
    project_tiles(image_tokens, ready(1), width_i, image_qkv)
    run(18)
    outs = ready(2)

    def cross_forward_tile(z, carry):
        tq, tk, tv = [text_qkv[n, :, tile_at(z)] for n in range(3)]
        iq, ik, iv = [image_qkv[n, :, tile_at(z)] for n in range(3)]
        text_heads = pair_heads(
            lambda q, k, v: head_forward(q, k, v, mask_ti[...], CROSS_HEAD), 2, tq, ik, iv
        )
        image_heads = pair_heads(
            lambda q, k, v: head_forward(q, k, v, mask_it[...], CROSS_HEAD), 2, iq, tk, tv
        )
        text_context = jnp.concatenate(text_heads, -1)
        image_context = jnp.concatenate(image_heads, -1)
        text_right[3, z] = text_context
        image_right[3, z] = image_context
        text_acc[...] += dot_nn(text_context, outs[tile_at(z), 0:width_t])
        offset = pl.ds(pl.multiple_of(inner + z * TILE, TILE), TILE)
        image_acc[...] += dot_nn(image_context, outs[offset, 0:width_i])
        return carry

    lax.fori_loop(0, zs // 2, cross_forward_tile, 0)
    start(3)
    run(19)
    lax.fori_loop(zs // 2, zs, cross_forward_tile, 0)
    start(4)
    norm_forward(0, text_output, text_acc, text_xhat, text_rstd, text_gains, text_shifts, text_rows.at[0])
    norm_forward(0, image_output, image_acc, image_xhat, image_rstd, image_gains, image_shifts, image_rows.at[0])

    def gelu_tile(upper):
        normal = 0.5 * (1.0 + lax.erf(upper * ROOT_HALF))
        slope = normal + upper * (DENSITY * jnp.exp(-0.5 * upper * upper))
        return (upper * normal).astype(bf16), slope

    start(5)
    run(21)
    up_t = ready(3)

    def text_up_tile(j, carry):
        rows = pl.ds(pl.multiple_of((j // ups) * width_t, 8), width_t)
        upper = dot_nn(text_rows[0], up_t[rows, tile_at(j % ups)])
        middle, slope = gelu_tile(upper)
        text_slope[j] = slope
        text_right[7 + j % ups, j // ups] = middle
        return carry

    lax.fori_loop(0, zs * ups // 2, text_up_tile, 0)
    run(22)
    lax.fori_loop(zs * ups // 2, zs * ups, text_up_tile, 0)
    run(23)
    down_t = ready(4)
    clear()

    def text_down_tile(j, carry):
        text_acc[...] += dot_nn(text_right[7 + j % ups, j // ups], down_t[tile_at(j), 0:width_t])
        return carry

    lax.fori_loop(0, zs * ups, text_down_tile, 0)
    run(24)
    both_i = ready(5)

    def image_up_tile(z, carry):
        middle, slope = gelu_tile(dot_nn(image_rows[0], both_i[0:width_i, tile_at(z)]))
        image_slope[z] = slope
        image_right[5, z] = middle
        offset = pl.ds(pl.multiple_of(width_i + z * TILE, TILE), TILE)
        image_acc[...] += dot_nn(middle, both_i[offset, 0:width_i])
        return carry

    lax.fori_loop(0, zs, image_up_tile, 0)
    run(25)
    norm_forward(1, text_output, text_acc, text_xhat, text_rstd, text_gains, text_shifts, text_rows.at[1])
    norm_forward(1, image_output, image_acc, image_xhat, image_rstd, image_gains, image_shifts, image_rows.at[1])

    clear()
    start(6)
    start(7)
    start(8)
    self_t = ready(6)
    project_tiles(text_rows.at[1], self_t, width_t, text_sqkv)
    self_i = ready(7)
    project_tiles(image_rows.at[1], self_i, width_i, image_sqkv)
    out_i = ready(8)
    share = TILE - TEXT_HEAD
    heads_t = share // TEXT_HEAD

    def self_forward_tile(z, carry):
        text_tiles = [text_sqkv[n, :, tile_at(z)] for n in range(3)]
        heads = pair_heads(
            lambda q, k, v: head_forward(q, k, v, mask_tt[...], TEXT_HEAD), heads_t, *text_tiles
        )
        blank = jnp.zeros((rows_t, TEXT_HEAD), bf16)
        text_extra[z] = jnp.concatenate([blank] + heads, -1)
        context = jnp.concatenate(heads + [blank], -1)
        text_acc[...] += dot_nt(context, self_t[3 * width_t : 4 * width_t, tile_at(z)])
        image_tiles = [image_sqkv[n, :, tile_at(z)] for n in range(3)]
        image_heads = pair_heads(
            lambda q, k, v: head_forward(q, k, v, mask_ii[...], IMAGE_HEAD), 2, *image_tiles
        )
        image_context = jnp.concatenate(image_heads, -1)
        image_right[9, z] = image_context
        image_acc[...] += dot_nn(image_context, out_i[tile_at(z), 0:width_i])
        return carry

    lax.fori_loop(0, zs, self_forward_tile, 0)
    norm_forward(2, text_output, text_acc, text_xhat, text_rstd, text_gains, text_shifts, None)
    norm_forward(2, image_output, image_acc, image_xhat, image_rstd, image_gains, image_shifts, None)

    text_grad[...] = text_cot[...].astype(f32)
    image_grad[...] = image_cot[...].astype(f32)
    norm_backward(2, text_grad, None, text_xhat, text_rstd, text_gains, text_rows.at[4], text_norms)
    norm_backward(2, image_grad, None, image_xhat, image_rstd, image_gains, image_rows.at[4], image_norms)
    clear()

    def self_back_tile(z, carry):
        text_tiles = [text_sqkv[n, :, tile_at(z)] for n in range(3)]
        context_grad = dot_nt_rows(text_rows[4], self_t, z)
        grads = pair_heads(
            lambda q, k, v, d: head_back(q, k, v, mask_tt[...], TEXT_HEAD, d),
            heads_t, *text_tiles, context_grad,
        )
        blank = jnp.zeros((rows_t, TEXT_HEAD), bf16)
        dq, dk, dv = [[grads[h][n] for h in range(heads_t)] for n in range(3)]
        pieces = dq + dk + dv
        text_right[10, z] = jnp.concatenate(pieces[0:4], -1)
        text_right[11, z] = jnp.concatenate(pieces[4:8], -1)
        text_right[12, z] = jnp.concatenate(pieces[8:9] + [blank] * 3, -1)
        total = jnp.zeros((rows_t, width_t), f32)
        for n, parts in enumerate((dq, dk, dv)):
            joined = jnp.concatenate(parts + [blank], -1)
            total += dot_nt(joined, self_t[n * width_t : (n + 1) * width_t, tile_at(z)])
        text_acc[...] += total
        return carry

    def dot_nt_rows(coming, weights, z):
        return dot_nn(coming, weights[3 * width_t : 4 * width_t, tile_at(z)]).astype(bf16)

    def self_back_image(z, carry):
        image_tiles = [image_sqkv[n, :, tile_at(z)] for n in range(3)]
        context_grad = dot_nt(image_rows[4], out_i[tile_at(z), 0:width_i]).astype(bf16)
        grads = pair_heads(
            lambda q, k, v, d: head_back(q, k, v, mask_ii[...], IMAGE_HEAD, d),
            2, *image_tiles, context_grad,
        )
        total = jnp.zeros((rows_i, width_i), f32)
        for n in range(3):
            joined = jnp.concatenate([grads[0][n], grads[1][n]], -1)
            image_right[6 + n, z] = joined
            total += dot_nt(joined, self_i[n * width_i : (n + 1) * width_i, tile_at(z)])
        image_acc[...] += total
        return carry

    lax.fori_loop(0, zs, self_back_image, 0)
    start(9)
    lax.fori_loop(0, zs, self_back_tile, 0)
    start(10)
    start(11)
    norm_backward(1, text_grad, text_acc, text_xhat, text_rstd, text_gains, text_rows.at[3], text_norms)
    norm_backward(1, image_grad, image_acc, image_xhat, image_rstd, image_gains, image_rows.at[3], image_norms)
    clear()

    back_down = ready(9)

    def text_down_back(j, carry):
        middle_grad = dot_nt(text_rows[3], back_down[tile_at(j), 0:width_t])
        text_right[4 + j % ups, j // ups] = (middle_grad * text_slope[j]).astype(bf16)
        return carry

    lax.fori_loop(0, zs * ups, text_down_back, 0)
    start(12)
    back_i = ready(10)

    def image_ffn_back(z, carry):
        offset = pl.ds(pl.multiple_of(width_i + z * TILE, TILE), TILE)
        middle_grad = dot_nt(image_rows[3], back_i[offset, 0:width_i])
        upper_grad = (middle_grad * image_slope[z]).astype(bf16)
        image_right[4, z] = upper_grad
        image_acc[...] += dot_nt(upper_grad, back_i[0:width_i, tile_at(z)])
        return carry

    lax.fori_loop(0, zs, image_ffn_back, 0)
    start(13)
    back_up = ready(11)

    def text_up_back(j, carry):
        rows = pl.ds(pl.multiple_of((j // ups) * width_t, 8), width_t)
        text_acc[...] += dot_nt(text_right[4 + j % ups, j // ups], back_up[rows, tile_at(j % ups)])
        return carry

    lax.fori_loop(0, zs * ups, text_up_back, 0)
    start(14)
    norm_backward(0, text_grad, text_acc, text_xhat, text_rstd, text_gains, text_rows.at[2], text_norms)
    norm_backward(0, image_grad, image_acc, image_xhat, image_rstd, image_gains, image_rows.at[2], image_norms)
    clear()

    back_out = ready(12)
    cross_t = ready(13)
    cross_i = ready(14)

    def cross_back_tile(z, carry):
        tq, tk, tv = [text_qkv[n, :, tile_at(z)] for n in range(3)]
        iq, ik, iv = [image_qkv[n, :, tile_at(z)] for n in range(3)]
        text_ctx_grad = dot_nt(text_rows[2], back_out[tile_at(z), 0:width_t]).astype(bf16)
        offset = pl.ds(pl.multiple_of(inner + z * TILE, TILE), TILE)
        image_ctx_grad = dot_nt(image_rows[2], back_out[offset, 0:width_i]).astype(bf16)
        text_side = pair_heads(
            lambda q, k, v, d: head_back(q, k, v, mask_ti[...], CROSS_HEAD, d), 2, tq, ik, iv, text_ctx_grad
        )
        image_side = pair_heads(
            lambda q, k, v, d: head_back(q, k, v, mask_it[...], CROSS_HEAD, d), 2, iq, tk, tv, image_ctx_grad
        )

        def joined(side, n):
            return jnp.concatenate([side[0][n], side[1][n]], -1)

        text_parts = (joined(text_side, 0), joined(image_side, 1), joined(image_side, 2))
        image_parts = (joined(image_side, 0), joined(text_side, 1), joined(text_side, 2))
        total_t = jnp.zeros((rows_t, width_t), f32)
        total_i = jnp.zeros((rows_i, width_i), f32)
        for n in range(3):
            text_right[n, z] = text_parts[n]
            image_right[n, z] = image_parts[n]
            total_t += dot_nt(text_parts[n], cross_t[n * width_t : (n + 1) * width_t, tile_at(z)])
            total_i += dot_nt(image_parts[n], cross_i[n * width_i : (n + 1) * width_i, tile_at(z)])
        text_acc[...] += total_t
        image_acc[...] += total_i
        return carry

    lax.fori_loop(0, zs, cross_back_tile, 0)
    text_grad[...] += text_acc[...]
    image_grad[...] += image_acc[...]
    finish()
    turn_over(text_left, text_tokens, text_rows)
    turn_over(image_left, image_tokens, image_rows)


def layer(lengths, counts, rows, params, weights, mp, unit):
    f32, bf16 = jnp.float32, jnp.bfloat16
    text_tokens, image_tokens = rows[0], rows[1]
    rows_t, width_t = text_tokens.shape
    rows_i, width_i = image_tokens.shape
    text_tiles = mp * weights[4].shape[2] // TILE
    inner = mp * TILE

    vmem = pl.BlockSpec(memory_space=pltpu.VMEM)
    out_shape = [
        jax.ShapeDtypeStruct((rows_t, width_t), f32),
        jax.ShapeDtypeStruct((rows_i, width_i), f32),
        jax.ShapeDtypeStruct((rows_t, width_t), f32),
        jax.ShapeDtypeStruct((rows_i, width_i), f32),
        jax.ShapeDtypeStruct((2, 6, 2, 2, width_t // 8, rows_t), bf16),
        jax.ShapeDtypeStruct((2, 6, 2, 2, width_i // 8, rows_i), bf16),
        jax.ShapeDtypeStruct((13, mp, rows_t, TILE), bf16),
        jax.ShapeDtypeStruct((mp, rows_t, TILE), bf16),
        jax.ShapeDtypeStruct((10, mp, rows_i, TILE), bf16),
        jax.ShapeDtypeStruct((2 * params[0].shape[0], width_t), f32),
        jax.ShapeDtypeStruct((2 * params[0].shape[0], width_i), f32),
    ]
    fulls = []
    for array, kind in zip(weights, KINDS):
        shape = array.shape[:-1] + (mp * array.shape[-1],) if kind == "cols" else (mp * array.shape[0], array.shape[1])
        fulls.append(jax.ShapeDtypeStruct(shape, bf16))
    chunks = len(SEQUENCE)
    results = pl.pallas_call(
        functools.partial(layer_kernel, unit),
        out_shape=out_shape + fulls,
        in_specs=[pl.BlockSpec(memory_space=pltpu.SMEM)] * 2
        + [vmem] * 8
        + [pl.BlockSpec(memory_space=pl.ANY)] * len(weights),
        out_specs=[vmem] * len(out_shape) + [pl.BlockSpec(memory_space=pl.ANY)] * len(fulls),
        scratch_shapes=[
            pltpu.SemaphoreType.DMA((chunks, 12)),
            pltpu.SemaphoreType.DMA((chunks, 12)),
            pltpu.VMEM((3, 3 * width_i, inner), bf16),
            pltpu.SemaphoreType.DMA((15, 4 * mp)),
            pltpu.VMEM((rows_t, width_t), f32),
            pltpu.VMEM((rows_i, width_i), f32),
            pltpu.VMEM((3, rows_t, width_t), f32),
            pltpu.VMEM((3, rows_i, width_i), f32),
            pltpu.VMEM((3, rows_t, 128), f32),
            pltpu.VMEM((3, rows_i, 128), f32),
            pltpu.VMEM((text_tiles, rows_t, TILE), f32),
            pltpu.VMEM((mp, rows_i, TILE), f32),
            pltpu.VMEM((3, rows_t, inner), bf16),
            pltpu.VMEM((3, rows_i, inner), bf16),
            pltpu.VMEM((3, rows_t, inner), bf16),
            pltpu.VMEM((3, rows_i, inner), bf16),
            pltpu.VMEM((rows_t, rows_i), f32),
            pltpu.VMEM((rows_i, rows_t), f32),
            pltpu.VMEM((rows_t, rows_t), f32),
            pltpu.VMEM((rows_i, rows_i), f32),
            pltpu.VMEM((5, rows_t, width_t), bf16),
            pltpu.VMEM((5, rows_i, width_i), bf16),
        ],
        compiler_params=pltpu.CompilerParams(
            collective_id=0, has_side_effects=True, vmem_limit_bytes=67043328
        ),
        name="layer",
    )(lengths, counts, *rows, *params, *weights)
    return results[: len(out_shape)]


def shards(
    text_tokens, image_regions, lengths, region_counts, text_cross, image_cross, text_cross_out,
    image_cross_out, text_up, text_down, image_up, image_down, text_self, text_self_out, image_self,
    image_self_out, text_gains, text_shifts, image_gains, image_shifts, text_cotangent, image_cotangent,
):
    mp, dp = lax.axis_size("mp"), lax.axis_size("dp")
    more = dp // 8
    text_out_turned = text_self_out.T[None]
    text_four = jnp.concatenate([text_self, text_out_turned])
    spare = 256 - text_four.shape[-1]
    text_four = jnp.pad(text_four, ((0, 0), (0, 0), (0, spare)))
    weights = (
        text_cross, image_cross, text_cross_out, image_cross_out, text_up[None], text_down,
        image_up[None], image_down, text_four, image_self, image_self_out,
    )
    pairs, regions = image_regions.shape[0], image_regions.shape[1]
    padding = (-regions) % 16

    def pad_regions(array):
        return jnp.pad(array, ((0, 0), (0, padding), (0, 0))).reshape(-1, array.shape[-1])

    def flat(array):
        return array.reshape(-1, array.shape[-1])

    (
        text_result, image_result, text_input_grad, image_input_grad,
        text_left, image_left, text_right, text_extra, image_right, text_norms, image_norms,
    ) = layer(
        lengths, region_counts,
        (flat(text_tokens), pad_regions(image_regions), flat(text_cotangent), pad_regions(image_cotangent)),
        (text_gains, text_shifts, image_gains, image_shifts),
        weights, mp, more,
    )
    text_result, text_input_grad = [
        array.reshape(text_tokens.shape) for array in (text_result, text_input_grad)
    ]
    image_result, image_input_grad = [
        array.reshape(pairs, regions + padding, -1)[:, :regions]
        for array in (image_result, image_input_grad)
    ]
    norms = jnp.concatenate([text_norms.reshape(-1, 128), image_norms.reshape(-1, 128)])
    text_sums, image_sums, norm_sums = reduce_all(
        text_left, text_right, text_extra, image_left, image_right, norms, more
    )
    if more > 1:
        norm_sums = lax.psum(norm_sums, "dp") / 8
        text_sums, image_sums = outer_sum(text_sums, more), outer_sum(image_sums, more)
    text_sums = text_sums.transpose(1, 0, 2).reshape(text_sums.shape[1], -1)
    image_sums = image_sums.transpose(1, 0, 2).reshape(image_sums.shape[1], -1)

    def columns(sums, widths):
        parts, start = [], 0
        for width in widths:
            parts.append(sums[:, start : start + width])
            start += width
        return parts

    def triple(parts):
        return jnp.stack(parts[:3])

    text_widths = [text_cross.shape[-1]] * 3 + [text_cross_out.shape[0]]
    text_widths += [text_up.shape[-1], text_down.shape[0]]
    text_widths += [text_self.shape[-1]] * 3 + [text_self_out.shape[0]]
    image_widths = [image_cross.shape[-1]] * 3 + [image_cross_out.shape[0]]
    image_widths += [image_up.shape[-1], image_down.shape[0]]
    image_widths += [image_self.shape[-1]] * 3 + [image_self_out.shape[0]]
    text_parts = columns(text_sums, text_widths)
    image_parts = columns(image_sums, image_widths)
    flat_norms = norm_sums.reshape(-1)
    text_size, image_size = text_gains.size, image_gains.size
    text_end = 2 * text_size
    return (
        text_result,
        image_result,
        text_input_grad,
        image_input_grad,
        triple(text_parts[:3]),
        triple(image_parts[:3]),
        text_parts[3].T,
        image_parts[3].T,
        text_parts[4],
        text_parts[5].T,
        image_parts[4],
        image_parts[5].T,
        triple(text_parts[6:9]),
        text_parts[9].T,
        triple(image_parts[6:9]),
        image_parts[9].T,
        flat_norms[:text_size].reshape(text_gains.shape),
        flat_norms[text_size:text_end].reshape(text_shifts.shape),
        flat_norms[text_end : text_end + image_size].reshape(image_gains.shape),
        flat_norms[text_end + image_size :].reshape(image_shifts.shape),
    )


def outer_sum(sums, more):
    chunks, rows, width = sums.shape
    apart = sums.reshape(chunks, 1, more, rows // more, width)
    low = lax.axis_index("dp") // more
    spread = jnp.zeros((chunks, 8, more, rows // more, width), sums.dtype)
    spread = lax.dynamic_update_slice(spread, apart, (0, low, 0, 0, 0))
    spread = spread.reshape(chunks, 8 * rows, width)
    return lax.psum_scatter(spread, "dp", scatter_dimension=1, tiled=True)


def solution(mesh):
    in_specs = (
        P(("dp", "mp"), None, None),
        P(("dp", "mp"), None, None),
        P(("dp", "mp")),
        P(("dp", "mp")),
        P(None, None, "mp"),
        P(None, None, "mp"),
        P("mp", None),
        P("mp", None),
        P(None, "mp"),
        P("mp", None),
        P(None, "mp"),
        P("mp", None),
        P(None, None, "mp"),
        P("mp", None),
        P(None, None, "mp"),
        P("mp", None),
        P(),
        P(),
        P(),
        P(),
        P(("dp", "mp"), None, None),
        P(("dp", "mp"), None, None),
    )
    out_specs = (
        P(("dp", "mp"), None, None),
        P(("dp", "mp"), None, None),
        P(("dp", "mp"), None, None),
        P(("dp", "mp"), None, None),
        P(None, "dp", "mp"),
        P(None, "dp", "mp"),
        P("mp", "dp"),
        P("mp", "dp"),
        P("dp", "mp"),
        P("mp", "dp"),
        P("dp", "mp"),
        P("mp", "dp"),
        P(None, "dp", "mp"),
        P("mp", "dp"),
        P(None, "dp", "mp"),
        P("mp", "dp"),
        P(),
        P(),
        P(),
        P(),
    )
    return jax.shard_map(shards, mesh=mesh, in_specs=in_specs, out_specs=out_specs, check_vma=False)
```

```python
import functools
import math

import jax
import jax.numpy as jnp
from jax import lax
from jax.experimental import pallas as pl
from jax.experimental.pallas import tpu as pltpu
from jax.sharding import PartitionSpec as P

TEXT_HEAD = 64
CROSS_HEAD = 128
IMAGE_HEAD = 128


EPSILON = 1e-05
MASKED = -1e30
MESH_ID = pl.DeviceIdType.MESH


def flip(index, step):
    return index + step * (1 - 2 * ((index // step) % 2))


def position(unit):
    data, model = lax.axis_index("dp"), lax.axis_index("mp")
    return data, model, (data // unit) % 2, (data // (2 * unit)) % 2, (data // (4 * unit)) % 2


def greet(data, model, unit):
    barrier = pltpu.get_barrier_semaphore()
    partners = [(flip(data, step * unit), model) for step in (1, 2, 4)]
    partners += [(data, flip(model, step)) for step in (1, 2)]
    for partner in partners:
        pl.semaphore_signal(barrier, inc=1, device_id=partner, device_id_type=MESH_ID)
    pl.semaphore_wait(barrier, len(partners))


LAGS = (0, 2, 4, 6, 8)


def gather_steps(unit, kinds, chunks, ins, outs, send_sem, recv_sem):
    data, model, c, x, y = position(unit)
    near, far = flip(model, 1), flip(model, 2)
    corner = flip(near, 2)
    copies = {}

    def send(n, slot, source, target, partner):
        copies[n, slot] = pltpu.make_async_remote_copy(
            src_ref=source,
            dst_ref=target,
            send_sem=send_sem.at[n, slot],
            recv_sem=recv_sem.at[n, slot],
            device_id=partner,
            device_id_type=MESH_ID,
        )
        copies[n, slot].start()

    def rows_of(height, first, base, span):
        start, count = span
        return pl.ds(pl.multiple_of(base + start * (height // 8), 8), count * (height // 8))

    def mine(n, span):
        k, matrix, unused, unused = chunks[n]
        if kinds[k] == "cols":
            return ins[k].at[matrix, rows_of(ins[k].shape[1], 0, 0, span), :]
        return ins[k].at[rows_of(ins[k].shape[0], 0, 0, span), :]

    def piece(n, shard, span):
        k, matrix, unused, unused = chunks[n]
        if kinds[k] == "cols":
            width = ins[k].shape[2]
            columns = pl.ds(pl.multiple_of(shard * width, 128), width)
            return outs[k].at[matrix, rows_of(ins[k].shape[1], 0, 0, span), columns]
        height = ins[k].shape[0]
        return outs[k].at[rows_of(height, 0, shard * height, span), :]

    x_side = (flip(data, 2 * unit), model)
    y_side = (flip(data, 4 * unit), model)
    z_side = (data, near)

    def relay(n, slot, shard, span, partner):
        block = piece(n, shard, span)
        send(n, slot, block, block, partner)

    def advance(n, stage):
        x_first, early = chunks[n][2:]
        first, second = (x_side, y_side) if x_first else (y_side, x_side)
        low_bit, middle_bit = (x, y) if x_first else (y, x)
        single = (4 * c + 2 * middle_bit + low_bit, 1)
        double = (4 * c + 2 * middle_bit, 2)
        if stage == 0:
            send(n, 0, mine(n, single), piece(n, model, single), (data, far))
        elif stage == 1 and not early:
            send(n, 1, mine(n, single), piece(n, model, single), z_side)
            copies[n, 0].wait_recv()
            relay(n, 2, far, single, z_side)
        elif stage == 2 and not early:
            relay(n, 3, far, single, first)
            copies[n, 1].wait_recv()
            relay(n, 4, near, single, first)
            copies[n, 2].wait_recv()
            relay(n, 5, corner, single, first)
        elif stage == 1:
            copies[n, 0].wait_recv()
            relay(n, 3, far, single, first)
        elif stage == 2:
            send(n, 1, mine(n, double), piece(n, model, double), z_side)
            copies[n, 3].wait_recv()
            relay(n, 2, far, double, z_side)
        elif stage == 3:
            before = (None, 1, 2) if early else (3, 4, 5)
            for number, shard in enumerate((far, near, corner)):
                if before[number] is not None:
                    copies[n, before[number]].wait_recv()
                relay(n, 6 + number, shard, double, second)
        else:
            for number, shard in enumerate((far, near, corner)):
                copies[n, 6 + number].wait_recv()
                relay(n, 9 + number, shard, (4 * c, 4), (flip(data, unit), model))

    total = len(chunks)
    done = [0]

    def run(limit):
        while done[0] < min(limit, total + LAGS[-1]):
            for stage, lag in enumerate(LAGS):
                if 0 <= done[0] - lag < total:
                    advance(done[0] - lag, stage)
            done[0] += 1

    def arrived(numbers):
        run(max(numbers) + LAGS[-1] + 1)
        for n in numbers:
            for slot in range(9, 12):
                copies[n, slot].wait_recv()

    def finish():
        for copy in copies.values():
            copy.wait_send()

    return run, arrived, finish


KINDS = ("cols", "cols", "rows", "rows", "cols", "rows", "cols", "rows", "cols", "cols", "rows")
SEQUENCE = (
    (0, 0), (1, 0), (0, 1), (1, 1), (0, 2), (1, 2), (2, None), (3, None), (4, 0), (6, 0), (5, None), (7, None),
    (8, 0), (9, 0), (8, 1), (9, 1), (8, 2), (9, 2), (8, 3), (10, None),
)


def chunk_plan():
    return tuple(
        (k, matrix, n % 4 in (0, 3), n % 2 == 1) for n, (k, matrix) in enumerate(SEQUENCE)
    )


def steps_up(k, marks):
    total = 0
    for mark in marks:
        total = total + jnp.where(k >= mark, 1, 0)
    return total


STAGE_LAGS = (0, 2, 4, 6, 8, 10)
TEXT_MARKS = (3, 4, 7, 10)
IMAGE_MARKS = (3, 4, 5, 6, 9)


def reduce_kernel(
    unit,
    text_left, text_right, text_extra, image_left, image_right, norms,
    text_out, image_out, norm_out,
    text_send, image_send,
    text_r0, text_r1, text_r2, text_r3, text_r4,
    image_r0, image_r1, image_r2, image_r3, image_r4,
    norm_buf,
    text_ss, text_rs, image_ss, image_rs, norm_ss, norm_rs,
):
    data, model, c, x, y = position(unit)
    low, high = model % 2, (model // 2) % 2
    f32, bf16 = jnp.float32, jnp.bfloat16
    core = (flip(data, unit), model)
    along_x = (flip(data, 2 * unit), model)
    along_y = (flip(data, 4 * unit), model)
    near = (data, flip(model, 1))
    far = (data, flip(model, 2))
    greet(data, model, unit)

    def stream(left, right, extra, out, outgoing, bufs, send_sem, recv_sem, marks, turn_first):
        r0, r1, r2, r3, r4 = bufs
        total = right.shape[0]
        rows = left.shape[-2]

        def order(k):
            by_y = (k + turn_first) % 2
            by_x = 1 - by_y
            first, second = x * by_x + y * by_y, y * by_x + x * by_y
            return by_x, first, second

        def copy(k, stage):
            by_x, first, second = order(k)
            if stage == 0:
                pair = (outgoing.at[k % 2], r0.at[k], core)
            elif stage == 1:
                pair = (r0.at[k, 1 - first], r1.at[k], (flip(data, (4 - 2 * by_x) * unit), model))
            elif stage == 2:
                pair = (r1.at[k, :, :, 1 - low], r2.at[k], near)
            elif stage == 3:
                pair = (r2.at[k, 1 - second], r3.at[k], (flip(data, (2 + 2 * by_x) * unit), model))
            else:
                pair = (r3.at[k, 1 - high], r4.at[k], far)
            return pltpu.make_async_remote_copy(
                src_ref=pair[0], dst_ref=pair[1],
                send_sem=send_sem.at[k, stage], recv_sem=recv_sem.at[k, stage],
                device_id=pair[2], device_id_type=MESH_ID,
            )

        def products(k, half, put):
            lhs = left[half, steps_up(k, marks)].reshape(4 * rows, left.shape[-1])

            def plain():
                for z in range(4):
                    value = jnp.dot(lhs, right[k, z], preferred_element_type=f32)
                    put(z, value.reshape(2, 2, rows, 256))

            if extra is None:
                plain()
                return
            pl.when(k != total - 1)(plain)

            @pl.when(k == total - 1)
            def _():
                more = left[half, 5].reshape(4 * rows, left.shape[-1])
                for z in range(4):
                    value = jnp.dot(lhs, right[k, z], preferred_element_type=f32)
                    value += jnp.dot(more, extra[z], preferred_element_type=f32)
                    put(z, value.reshape(2, 2, rows, 256))

        def places(k):
            by_x, unused, unused = order(k)
            for y_side in range(2):
                for x_side in range(2):
                    first = x_side * by_x + y_side * (1 - by_x)
                    yield y_side, x_side, first, y_side + x_side - first

        def begin(k):
            @pl.when(k >= 2)
            def _():
                copy(k - 2, 0).wait_send()

            def put(z, value):
                for y_side, x_side, first, second in places(k):
                    outgoing[k % 2, first, second, z // 2, z % 2] = value[y_side, x_side].astype(bf16)

            products(k, 1 - c, put)
            copy(k, 0).start()

        def join(k):
            copy(k, 0).wait_recv()

            def put(z, value):
                for y_side, x_side, first, second in places(k):
                    held = r0[k, first, second, z // 2, z % 2].astype(f32)
                    r0[k, first, second, z // 2, z % 2] = (held + value[y_side, x_side]).astype(bf16)

            products(k, c, put)
            copy(k, 1).start()

        def add_into(target, k, kept):
            target[k] = (target[k].astype(f32) + kept.astype(f32)).astype(bf16)

        def second(k):
            copy(k, 1).wait_recv()
            add_into(r1, k, r0[k, order(k)[1]])
            copy(k, 2).start()

        def third(k):
            copy(k, 2).wait_recv()
            add_into(r2, k, r1[k, :, :, low])
            copy(k, 3).start()

        def fourth(k):
            copy(k, 3).wait_recv()
            add_into(r3, k, r2[k, order(k)[2]])
            copy(k, 4).start()

        def last(k):
            copy(k, 4).wait_recv()
            out[k] = r4[k].astype(f32) + r3[k, high].astype(f32)

        def finish():
            def body(k, carry):
                for stage in range(1, 5):
                    copy(k, stage).wait_send()
                return carry

            lax.fori_loop(0, total, body, 0)
            copy(total - 2, 0).wait_send()
            copy(total - 1, 0).wait_send()

        return total, (begin, join, second, third, fourth, last), finish

    text_total, text_stages, text_finish = stream(
        text_left, text_right, text_extra, text_out, text_send,
        (text_r0, text_r1, text_r2, text_r3, text_r4), text_ss, text_rs, TEXT_MARKS, 0,
    )
    image_total, image_stages, image_finish = stream(
        image_left, image_right, None, image_out, image_send,
        (image_r0, image_r1, image_r2, image_r3, image_r4), image_ss, image_rs, IMAGE_MARKS, 1,
    )
    lags = STAGE_LAGS
    partners = (core, along_x, along_y, near, far)

    def norm_copy(stage):
        return pltpu.make_async_remote_copy(
            src_ref=norms if stage == 0 else norm_buf.at[stage - 1],
            dst_ref=norm_buf.at[stage],
            send_sem=norm_ss.at[stage], recv_sem=norm_rs.at[stage],
            device_id=partners[stage], device_id_type=MESH_ID,
        )

    def turn(t, carry):
        for lag, text_stage, image_stage in zip(lags, text_stages, image_stages):
            k = t - lag
            pl.when((k >= 0) & (k < text_total))(functools.partial(text_stage, k))
            pl.when((k >= 0) & (k < image_total))(functools.partial(image_stage, k))
        for stage in range(6):

            @pl.when(t == 2 * stage)
            def _(stage=stage):
                if stage > 0:
                    norm_copy(stage - 1).wait_recv()
                    held = norms[...] if stage == 1 else norm_buf[stage - 2]
                    if stage < 5:
                        norm_buf[stage - 1] += held
                    else:
                        norm_out[...] = norm_buf[stage - 1] + held
                if stage < 5:
                    norm_copy(stage).start()

        return carry

    lax.fori_loop(0, max(text_total, image_total) + lags[-1], turn, 0)
    text_finish()
    image_finish()
    for stage in range(5):
        norm_copy(stage).wait_send()


def reduce_all(text_left, text_right, text_extra, image_left, image_right, norms, unit):
    bf16, f32 = jnp.bfloat16, jnp.float32

    def buffers(right, left):
        total, rows = right.shape[0], left.shape[-2]
        tail = (rows, 256)
        return [
            pltpu.VMEM((total, 2, 2, 2, 2) + tail, bf16),
            pltpu.VMEM((total, 2, 2, 2) + tail, bf16),
            pltpu.VMEM((total, 2, 2) + tail, bf16),
            pltpu.VMEM((total, 2) + tail, bf16),
            pltpu.VMEM((total,) + tail, bf16),
        ]

    def outgoing(left):
        return pltpu.VMEM((2, 2, 2, 2, 2, left.shape[-2], 256), bf16)

    texts, images = text_right.shape[0], image_right.shape[0]
    sems = []
    for total in (texts, images):
        sems += [pltpu.SemaphoreType.DMA((total, 5))] * 2
    sems += [pltpu.SemaphoreType.DMA((5,))] * 2
    return pl.pallas_call(
        functools.partial(reduce_kernel, unit),
        out_shape=[
            jax.ShapeDtypeStruct((texts, text_left.shape[-2], 256), f32),
            jax.ShapeDtypeStruct((images, image_left.shape[-2], 256), f32),
            jax.ShapeDtypeStruct(norms.shape, f32),
        ],
        in_specs=[pl.BlockSpec(memory_space=pltpu.VMEM)] * 6,
        out_specs=[pl.BlockSpec(memory_space=pltpu.VMEM)] * 3,
        scratch_shapes=[outgoing(text_left), outgoing(image_left)]
        + buffers(text_right, text_left)
        + buffers(image_right, image_left)
        + [pltpu.VMEM((5,) + norms.shape, f32)]
        + sems,
        compiler_params=pltpu.CompilerParams(
            collective_id=1, has_side_effects=True, vmem_limit_bytes=67043328
        ),
        name="reduce_gradients",
    )(text_left, text_right, text_extra, image_left, image_right, norms)


ROOT_HALF = math.sqrt(0.5)
DENSITY = 1.0 / math.sqrt(2.0 * math.pi)
TILE = 256


def block_of(rows):
    return next(size for size in (64, 48, 32, 16) if rows % size == 0)


def dot_nn(a, b):
    return jnp.dot(a, b, preferred_element_type=jnp.float32)


def dot_nt(a, b):
    return lax.dot_general(a, b, (((1,), (1,)), ((), ())), preferred_element_type=jnp.float32)


def joint_nt(parts, weights, width, z):
    tiles = [weights[n * width : (n + 1) * width, tile_at(z)] for n in range(len(parts))]
    return dot_nt(jnp.concatenate(parts, -1), jnp.concatenate(tiles, -1))


def dot_tn(a, b):
    return lax.dot_general(a, b, (((0,), (0,)), ((), ())), preferred_element_type=jnp.float32)


def row_blocks(rows, body):
    size = block_of(rows)

    def step(i, carry):
        body(pl.ds(pl.multiple_of(i * size, size), size))
        return carry

    lax.fori_loop(0, rows // size, step, 0)


def tile_at(j):
    return pl.ds(pl.multiple_of(j * TILE, TILE), TILE)


def probabilities(query, keys, mask, head_size):
    scores = dot_nt(query, keys) * (1.0 / math.sqrt(head_size))
    scores = jnp.where(mask > 0.5, scores, MASKED)
    lifted = jnp.exp(scores - jnp.max(scores, -1, keepdims=True))
    return lifted / jnp.sum(lifted, -1, keepdims=True)


def head_forward(query, keys, values, mask, head_size):
    probs = probabilities(query, keys, mask, head_size)
    return dot_nn(probs.astype(jnp.bfloat16), values).astype(jnp.bfloat16)


def head_back(query, keys, values, mask, head_size, context_grad):
    bf16 = jnp.bfloat16
    probs = probabilities(query, keys, mask, head_size)
    value_grad = dot_tn(probs.astype(bf16), context_grad)
    prob_grad = dot_nt(context_grad, values)
    inner = jnp.sum(probs * prob_grad, -1, keepdims=True)
    score_grad = (probs * (prob_grad - inner)).astype(bf16)
    scale = 1.0 / math.sqrt(head_size)
    query_grad = dot_nn(score_grad, keys) * scale
    key_grad = dot_tn(score_grad, query) * scale
    return query_grad.astype(bf16), key_grad.astype(bf16), value_grad.astype(bf16)


def norm_forward(number, res, acc, xhat, rstd, gains, shifts, lows):
    def block(rows):
        hidden = res[rows, :] + acc[rows, :]
        centred = hidden - jnp.mean(hidden, -1, keepdims=True)
        scale = lax.rsqrt(jnp.mean(centred * centred, -1, keepdims=True) + EPSILON)
        unit = centred * scale
        xhat[number, rows, :] = unit
        rstd[number, rows, :] = jnp.broadcast_to(scale, (scale.shape[0], 128))
        out = unit * gains[number : number + 1, :] + shifts[number : number + 1, :]
        res[rows, :] = out
        if lows is not None:
            lows[rows, :] = out.astype(jnp.bfloat16)

    row_blocks(res.shape[0], block)


def norm_backward(number, grad, acc, xhat, rstd, gains, low, norms):
    count = gains.shape[0]
    width = grad.shape[1]
    size = block_of(grad.shape[0])

    def step(i, carry):
        gain_sum, shift_sum = carry
        rows = pl.ds(pl.multiple_of(i * size, size), size)
        coming = grad[rows, :] if acc is None else grad[rows, :] + acc[rows, :]
        unit = xhat[number, rows, :]
        gain_sum += jnp.sum(coming * unit, 0, keepdims=True)
        shift_sum += jnp.sum(coming, 0, keepdims=True)
        scaled = coming * gains[number : number + 1, :]
        mean = jnp.mean(scaled, -1, keepdims=True)
        slope = jnp.mean(scaled * unit, -1, keepdims=True)
        out = (scaled - mean - unit * slope) * rstd[number, rows, 0:1]
        grad[rows, :] = out
        low[rows, :] = out.astype(jnp.bfloat16)
        return gain_sum, shift_sum

    zero = jnp.zeros((1, width), jnp.float32)
    gain_sum, shift_sum = lax.fori_loop(0, grad.shape[0] // size, step, (zero, zero))
    norms[number : number + 1, :] = gain_sum
    norms[count + number : count + number + 1, :] = shift_sum


def turn_over(left, tokens, rows):
    part = left.shape[4]
    for number, source in enumerate((tokens, rows.at[2], rows.at[0], rows.at[3], rows.at[1], rows.at[4])):
        turned = source[...].T
        for y in range(2):
            for x in range(2):
                for c in range(2):
                    first = (4 * y + 2 * x + c) * part
                    left[c, number, y, x] = turned[first : first + part]


def layer_kernel(
    unit,
    lengths, counts, text_tokens, image_tokens, text_cot, image_cot,
    text_gains, text_shifts, image_gains, image_shifts,
    in_a, in_b, in_c, in_d, in_e, in_f, in_g, in_h, in_i, in_j, in_k,
    text_output, image_output, text_grad, image_grad,
    text_left, image_left, text_right, text_extra, image_right, text_norms, image_norms,
    full_a, full_b, full_c, full_d, full_e, full_f, full_g, full_h, full_i, full_j, full_k,
    send_sem, recv_sem, slot, load_sem, text_acc, image_acc, text_xhat, image_xhat, text_rstd, image_rstd,
    text_slope, image_slope, text_qkv, image_qkv, text_sqkv, image_sqkv,
    mask_ti, mask_it, mask_tt, mask_ii, text_rows, image_rows,
):
    f32, bf16 = jnp.float32, jnp.bfloat16
    rows_t, rows_i = text_tokens.shape[0], image_tokens.shape[0]
    width_t, width_i = text_tokens.shape[1], image_tokens.shape[1]
    pairs = lengths.shape[0]
    per_t, per_i = rows_t // pairs, rows_i // pairs
    zs = text_right.shape[1]
    inner = zs * TILE
    ins = (in_a, in_b, in_c, in_d, in_e, in_f, in_g, in_h, in_i, in_j, in_k)
    fulls = (full_a, full_b, full_c, full_d, full_e, full_f, full_g, full_h, full_i, full_j, full_k)
    ups = in_e.shape[2] // TILE
    data, model, unused, unused, unused = position(unit)
    greet(data, model, unit)
    run, arrived, finish = gather_steps(unit, KINDS, chunk_plan(), ins, fulls, send_sem, recv_sem)
    run(6)

    def three(k):
        return [(k, n, n * ins[k].shape[1], False) for n in range(ins[k].shape[0])]

    loads = {
        "tc": three(0),
        "ic": three(1),
        "out": [(2, None, 0, False), (3, None, inner, False)],
        "tu": [(4, 0, 0, True)],
        "td": [(5, None, 0, False)],
        "if": [(6, 0, 0, False), (7, None, width_i, False)],
        "ts": three(8),
        "is": three(9),
        "io": [(10, None, 0, False)],
    }
    order = ["tc", "ic", "out", "tu", "td", "if", "ts", "is", "io"]
    order += ["td", "if", "tu", "out", "tc", "ic"]
    slots = [0, 1, 2, 0, 1, 2, 0, 1, 2, 2, 0, 1, 2, 0, 1]

    def copies(number):
        where, found = slots[number], []
        for k, matrix, row, stacked in loads[order[number]]:
            for turn in range(zs):
                shard = (model + turn) % zs
                if matrix is None:
                    height, width = ins[k].shape
                    source = fulls[k].at[pl.ds(pl.multiple_of(shard * height, 8), height), :]
                    source = ins[k] if turn == 0 else source
                    rows = pl.ds(pl.multiple_of(row + shard * height, 8), height)
                    target = slot.at[where, rows, pl.ds(0, width)]
                else:
                    unused, height, width = ins[k].shape
                    columns = pl.ds(pl.multiple_of(shard * width, 128), width)
                    source = ins[k].at[matrix] if turn == 0 else fulls[k].at[matrix, :, columns]
                    if stacked:
                        rows = pl.ds(pl.multiple_of(row + shard * height, 8), height)
                        target = slot.at[where, rows, pl.ds(0, width)]
                    else:
                        target = slot.at[where, pl.ds(row, height), columns]
                found.append(pltpu.make_async_copy(source, target, load_sem.at[number, len(found)]))
        return found

    def start(number):
        if number < 9:
            wanted = {k for k, unused, unused, unused in loads[order[number]]}
            arrived([n for n, chunk in enumerate(SEQUENCE) if chunk[0] in wanted])
        for copy in copies(number):
            copy.start()

    def ready(number):
        for copy in copies(number):
            copy.wait()
        return slot.at[slots[number]]

    def set_mask(ref, query_per, key_per, limits):
        query = lax.broadcasted_iota(jnp.int32, ref.shape, 0)
        key = lax.broadcasted_iota(jnp.int32, ref.shape, 1)
        seen = jnp.zeros(ref.shape, f32)
        for pair in range(pairs):
            inside = (query >= pair * query_per) & (query < (pair + 1) * query_per)
            inside &= (key >= pair * key_per) & (key < pair * key_per + limits[pair])
            seen = jnp.where(inside, 1.0, seen)
        ref[...] = seen

    set_mask(mask_ti, per_t, per_i, counts)
    set_mask(mask_it, per_i, per_t, lengths)
    set_mask(mask_tt, per_t, per_t, lengths)
    set_mask(mask_ii, per_i, per_i, counts)
    text_output[...] = text_tokens[...].astype(f32)
    image_output[...] = image_tokens[...].astype(f32)

    def clear():
        text_acc[...] = jnp.zeros(text_acc.shape, f32)
        image_acc[...] = jnp.zeros(image_acc.shape, f32)

    clear()

    def project_tiles(rows_ref, weights, width, kept):
        def body(z, carry):
            for n in range(3):
                tile = dot_nn(rows_ref[...], weights[n * width : (n + 1) * width, tile_at(z)])
                kept[n, :, tile_at(z)] = tile.astype(bf16)
            return carry

        lax.fori_loop(0, zs, body, 0, unroll=True)

    def halves(tile):
        return tile[:, :128], tile[:, 128:]

    def pair_heads(fn, count, *tiles):
        size = TILE // count if count == 2 else 64
        results = []
        for h in range(count):
            results.append(fn(*[tile[:, h * size : (h + 1) * size] for tile in tiles]))
        return results

    start(0)
    start(1)
    run(16)
    project_tiles(text_tokens, ready(0), width_t, text_qkv)
    start(2)
    project_tiles(image_tokens, ready(1), width_i, image_qkv)
    run(18)
    outs = ready(2)

    def cross_forward_tile(z, carry):
        tq, tk, tv = [text_qkv[n, :, tile_at(z)] for n in range(3)]
        iq, ik, iv = [image_qkv[n, :, tile_at(z)] for n in range(3)]
        text_heads = pair_heads(
            lambda q, k, v: head_forward(q, k, v, mask_ti[...], CROSS_HEAD), 2, tq, ik, iv
        )
        image_heads = pair_heads(
            lambda q, k, v: head_forward(q, k, v, mask_it[...], CROSS_HEAD), 2, iq, tk, tv
        )
        text_context = jnp.concatenate(text_heads, -1)
        image_context = jnp.concatenate(image_heads, -1)
        text_right[3, z] = text_context
        image_right[3, z] = image_context
        text_acc[...] += dot_nn(text_context, outs[tile_at(z), 0:width_t])
        offset = pl.ds(pl.multiple_of(inner + z * TILE, TILE), TILE)
        image_acc[...] += dot_nn(image_context, outs[offset, 0:width_i])
        return carry

    lax.fori_loop(0, zs // 2, cross_forward_tile, 0)
    start(3)
    run(19)
    lax.fori_loop(zs // 2, zs, cross_forward_tile, 0)
    start(4)
    norm_forward(0, text_output, text_acc, text_xhat, text_rstd, text_gains, text_shifts, text_rows.at[0])
    norm_forward(0, image_output, image_acc, image_xhat, image_rstd, image_gains, image_shifts, image_rows.at[0])

    def gelu_tile(upper):
        normal = 0.5 * (1.0 + lax.erf(upper * ROOT_HALF))
        slope = normal + upper * (DENSITY * jnp.exp(-0.5 * upper * upper))
        return (upper * normal).astype(bf16), slope

    start(5)
    run(21)
    up_t = ready(3)

    def text_up_tile(j, carry):
        rows = pl.ds(pl.multiple_of((j // ups) * width_t, 8), width_t)
        upper = dot_nn(text_rows[0], up_t[rows, tile_at(j % ups)])
        middle, slope = gelu_tile(upper)
        text_slope[j] = slope
        text_right[7 + j % ups, j // ups] = middle
        return carry

    lax.fori_loop(0, zs * ups // 2, text_up_tile, 0, unroll=3)
    run(22)
    lax.fori_loop(zs * ups // 2, zs * ups, text_up_tile, 0, unroll=3)
    run(23)
    down_t = ready(4)
    clear()

    def text_down_tile(j, carry):
        joined = jnp.concatenate([text_right[7 + part, j] for part in range(ups)], -1)
        rows = pl.ds(pl.multiple_of(j * ups * TILE, TILE), ups * TILE)
        text_acc[...] += dot_nn(joined, down_t[rows, 0:width_t])
        return carry

    lax.fori_loop(0, zs, text_down_tile, 0)
    run(24)
    both_i = ready(5)

    def image_up_tile(z, carry):
        middle, slope = gelu_tile(dot_nn(image_rows[0], both_i[0:width_i, tile_at(z)]))
        image_slope[z] = slope
        image_right[5, z] = middle
        offset = pl.ds(pl.multiple_of(width_i + z * TILE, TILE), TILE)
        image_acc[...] += dot_nn(middle, both_i[offset, 0:width_i])
        return carry

    lax.fori_loop(0, zs, image_up_tile, 0, unroll=True)
    run(25)
    norm_forward(1, text_output, text_acc, text_xhat, text_rstd, text_gains, text_shifts, text_rows.at[1])
    norm_forward(1, image_output, image_acc, image_xhat, image_rstd, image_gains, image_shifts, image_rows.at[1])

    clear()
    start(6)
    start(7)
    start(8)
    self_t = ready(6)
    project_tiles(text_rows.at[1], self_t, width_t, text_sqkv)
    self_i = ready(7)
    project_tiles(image_rows.at[1], self_i, width_i, image_sqkv)
    out_i = ready(8)
    share = TILE - TEXT_HEAD
    heads_t = share // TEXT_HEAD

    def self_forward_tile(z, carry):
        text_tiles = [text_sqkv[n, :, tile_at(z)] for n in range(3)]
        heads = pair_heads(
            lambda q, k, v: head_forward(q, k, v, mask_tt[...], TEXT_HEAD), heads_t, *text_tiles
        )
        blank = jnp.zeros((rows_t, TEXT_HEAD), bf16)
        text_extra[z] = jnp.concatenate([blank] + heads, -1)
        context = jnp.concatenate(heads + [blank], -1)
        text_acc[...] += dot_nt(context, self_t[3 * width_t : 4 * width_t, tile_at(z)])
        image_tiles = [image_sqkv[n, :, tile_at(z)] for n in range(3)]
        image_heads = pair_heads(
            lambda q, k, v: head_forward(q, k, v, mask_ii[...], IMAGE_HEAD), 2, *image_tiles
        )
        image_context = jnp.concatenate(image_heads, -1)
        image_right[9, z] = image_context
        image_acc[...] += dot_nn(image_context, out_i[tile_at(z), 0:width_i])
        return carry

    lax.fori_loop(0, zs, self_forward_tile, 0, unroll=2)
    norm_forward(2, text_output, text_acc, text_xhat, text_rstd, text_gains, text_shifts, None)
    norm_forward(2, image_output, image_acc, image_xhat, image_rstd, image_gains, image_shifts, None)

    text_grad[...] = text_cot[...].astype(f32)
    image_grad[...] = image_cot[...].astype(f32)
    norm_backward(2, text_grad, None, text_xhat, text_rstd, text_gains, text_rows.at[4], text_norms)
    norm_backward(2, image_grad, None, image_xhat, image_rstd, image_gains, image_rows.at[4], image_norms)
    clear()

    def self_back_tile(z, carry):
        text_tiles = [text_sqkv[n, :, tile_at(z)] for n in range(3)]
        context_grad = dot_nt_rows(text_rows[4], self_t, z)
        grads = pair_heads(
            lambda q, k, v, d: head_back(q, k, v, mask_tt[...], TEXT_HEAD, d),
            heads_t, *text_tiles, context_grad,
        )
        blank = jnp.zeros((rows_t, TEXT_HEAD), bf16)
        dq, dk, dv = [[grads[h][n] for h in range(heads_t)] for n in range(3)]
        pieces = dq + dk + dv
        text_right[10, z] = jnp.concatenate(pieces[0:4], -1)
        text_right[11, z] = jnp.concatenate(pieces[4:8], -1)
        text_right[12, z] = jnp.concatenate(pieces[8:9] + [blank] * 3, -1)
        joined = [jnp.concatenate(parts + [blank], -1) for parts in (dq, dk, dv)]
        text_acc[...] += joint_nt(joined, self_t, width_t, z)
        return carry

    def dot_nt_rows(coming, weights, z):
        return dot_nn(coming, weights[3 * width_t : 4 * width_t, tile_at(z)]).astype(bf16)

    def self_back_image(z, carry):
        image_tiles = [image_sqkv[n, :, tile_at(z)] for n in range(3)]
        context_grad = dot_nt(image_rows[4], out_i[tile_at(z), 0:width_i]).astype(bf16)
        grads = pair_heads(
            lambda q, k, v, d: head_back(q, k, v, mask_ii[...], IMAGE_HEAD, d),
            2, *image_tiles, context_grad,
        )
        joined = [jnp.concatenate([grads[0][n], grads[1][n]], -1) for n in range(3)]
        for n in range(3):
            image_right[6 + n, z] = joined[n]
        image_acc[...] += joint_nt(joined, self_i, width_i, z)
        return carry

    lax.fori_loop(0, zs, self_back_image, 0, unroll=True)
    start(9)
    lax.fori_loop(0, zs, self_back_tile, 0, unroll=2)
    start(10)
    start(11)
    norm_backward(1, text_grad, text_acc, text_xhat, text_rstd, text_gains, text_rows.at[3], text_norms)
    norm_backward(1, image_grad, image_acc, image_xhat, image_rstd, image_gains, image_rows.at[3], image_norms)
    clear()

    back_down = ready(9)

    def text_down_back(j, carry):
        middle_grad = dot_nt(text_rows[3], back_down[tile_at(j), 0:width_t])
        text_right[4 + j % ups, j // ups] = (middle_grad * text_slope[j]).astype(bf16)
        return carry

    lax.fori_loop(0, zs * ups, text_down_back, 0, unroll=4)
    start(12)
    back_i = ready(10)

    def image_ffn_back(z, carry):
        offset = pl.ds(pl.multiple_of(width_i + z * TILE, TILE), TILE)
        middle_grad = dot_nt(image_rows[3], back_i[offset, 0:width_i])
        upper_grad = (middle_grad * image_slope[z]).astype(bf16)
        image_right[4, z] = upper_grad
        image_acc[...] += dot_nt(upper_grad, back_i[0:width_i, tile_at(z)])
        return carry

    lax.fori_loop(0, zs, image_ffn_back, 0, unroll=True)
    start(13)
    back_up = ready(11)

    def text_up_back(j, carry):
        joined = jnp.concatenate([text_right[4 + part, j] for part in range(ups)], -1)
        rows = pl.ds(pl.multiple_of(j * width_t, 8), width_t)
        text_acc[...] += dot_nt(joined, back_up[rows, 0 : ups * TILE])
        return carry

    lax.fori_loop(0, zs, text_up_back, 0)
    start(14)
    norm_backward(0, text_grad, text_acc, text_xhat, text_rstd, text_gains, text_rows.at[2], text_norms)
    norm_backward(0, image_grad, image_acc, image_xhat, image_rstd, image_gains, image_rows.at[2], image_norms)
    clear()

    back_out = ready(12)
    cross_t = ready(13)
    cross_i = ready(14)

    def cross_back_tile(z, carry):
        tq, tk, tv = [text_qkv[n, :, tile_at(z)] for n in range(3)]
        iq, ik, iv = [image_qkv[n, :, tile_at(z)] for n in range(3)]
        text_ctx_grad = dot_nt(text_rows[2], back_out[tile_at(z), 0:width_t]).astype(bf16)
        offset = pl.ds(pl.multiple_of(inner + z * TILE, TILE), TILE)
        image_ctx_grad = dot_nt(image_rows[2], back_out[offset, 0:width_i]).astype(bf16)
        text_side = pair_heads(
            lambda q, k, v, d: head_back(q, k, v, mask_ti[...], CROSS_HEAD, d), 2, tq, ik, iv, text_ctx_grad
        )
        image_side = pair_heads(
            lambda q, k, v, d: head_back(q, k, v, mask_it[...], CROSS_HEAD, d), 2, iq, tk, tv, image_ctx_grad
        )

        def joined(side, n):
            return jnp.concatenate([side[0][n], side[1][n]], -1)

        text_parts = (joined(text_side, 0), joined(image_side, 1), joined(image_side, 2))
        image_parts = (joined(image_side, 0), joined(text_side, 1), joined(text_side, 2))
        for n in range(3):
            text_right[n, z] = text_parts[n]
            image_right[n, z] = image_parts[n]
        text_acc[...] += joint_nt(text_parts, cross_t, width_t, z)
        image_acc[...] += joint_nt(image_parts, cross_i, width_i, z)
        return carry

    lax.fori_loop(0, zs, cross_back_tile, 0, unroll=2)
    text_grad[...] += text_acc[...]
    image_grad[...] += image_acc[...]
    finish()
    turn_over(text_left, text_tokens, text_rows)
    turn_over(image_left, image_tokens, image_rows)


def layer(lengths, counts, rows, params, weights, mp, unit):
    f32, bf16 = jnp.float32, jnp.bfloat16
    text_tokens, image_tokens = rows[0], rows[1]
    rows_t, width_t = text_tokens.shape
    rows_i, width_i = image_tokens.shape
    text_tiles = mp * weights[4].shape[2] // TILE
    inner = mp * TILE

    vmem = pl.BlockSpec(memory_space=pltpu.VMEM)
    out_shape = [
        jax.ShapeDtypeStruct((rows_t, width_t), f32),
        jax.ShapeDtypeStruct((rows_i, width_i), f32),
        jax.ShapeDtypeStruct((rows_t, width_t), f32),
        jax.ShapeDtypeStruct((rows_i, width_i), f32),
        jax.ShapeDtypeStruct((2, 6, 2, 2, width_t // 8, rows_t), bf16),
        jax.ShapeDtypeStruct((2, 6, 2, 2, width_i // 8, rows_i), bf16),
        jax.ShapeDtypeStruct((13, mp, rows_t, TILE), bf16),
        jax.ShapeDtypeStruct((mp, rows_t, TILE), bf16),
        jax.ShapeDtypeStruct((10, mp, rows_i, TILE), bf16),
        jax.ShapeDtypeStruct((2 * params[0].shape[0], width_t), f32),
        jax.ShapeDtypeStruct((2 * params[0].shape[0], width_i), f32),
    ]
    fulls = []
    for array, kind in zip(weights, KINDS):
        shape = array.shape[:-1] + (mp * array.shape[-1],) if kind == "cols" else (mp * array.shape[0], array.shape[1])
        fulls.append(jax.ShapeDtypeStruct(shape, bf16))
    chunks = len(SEQUENCE)
    results = pl.pallas_call(
        functools.partial(layer_kernel, unit),
        out_shape=out_shape + fulls,
        in_specs=[pl.BlockSpec(memory_space=pltpu.SMEM)] * 2
        + [vmem] * 8
        + [pl.BlockSpec(memory_space=pl.ANY)] * len(weights),
        out_specs=[vmem] * len(out_shape) + [pl.BlockSpec(memory_space=pl.ANY)] * len(fulls),
        scratch_shapes=[
            pltpu.SemaphoreType.DMA((chunks, 12)),
            pltpu.SemaphoreType.DMA((chunks, 12)),
            pltpu.VMEM((3, 3 * width_i, inner), bf16),
            pltpu.SemaphoreType.DMA((15, 4 * mp)),
            pltpu.VMEM((rows_t, width_t), f32),
            pltpu.VMEM((rows_i, width_i), f32),
            pltpu.VMEM((3, rows_t, width_t), f32),
            pltpu.VMEM((3, rows_i, width_i), f32),
            pltpu.VMEM((3, rows_t, 128), f32),
            pltpu.VMEM((3, rows_i, 128), f32),
            pltpu.VMEM((text_tiles, rows_t, TILE), f32),
            pltpu.VMEM((mp, rows_i, TILE), f32),
            pltpu.VMEM((3, rows_t, inner), bf16),
            pltpu.VMEM((3, rows_i, inner), bf16),
            pltpu.VMEM((3, rows_t, inner), bf16),
            pltpu.VMEM((3, rows_i, inner), bf16),
            pltpu.VMEM((rows_t, rows_i), f32),
            pltpu.VMEM((rows_i, rows_t), f32),
            pltpu.VMEM((rows_t, rows_t), f32),
            pltpu.VMEM((rows_i, rows_i), f32),
            pltpu.VMEM((5, rows_t, width_t), bf16),
            pltpu.VMEM((5, rows_i, width_i), bf16),
        ],
        compiler_params=pltpu.CompilerParams(
            collective_id=0, has_side_effects=True, vmem_limit_bytes=67043328
        ),
        name="layer",
    )(lengths, counts, *rows, *params, *weights)
    return results[: len(out_shape)]


def shards(
    text_tokens, image_regions, lengths, region_counts, text_cross, image_cross, text_cross_out,
    image_cross_out, text_up, text_down, image_up, image_down, text_self, text_self_out, image_self,
    image_self_out, text_gains, text_shifts, image_gains, image_shifts, text_cotangent, image_cotangent,
):
    mp, dp = lax.axis_size("mp"), lax.axis_size("dp")
    more = dp // 8
    text_out_turned = text_self_out.T[None]
    text_four = jnp.concatenate([text_self, text_out_turned])
    spare = 256 - text_four.shape[-1]
    text_four = jnp.pad(text_four, ((0, 0), (0, 0), (0, spare)))
    weights = (
        text_cross, image_cross, text_cross_out, image_cross_out, text_up[None], text_down,
        image_up[None], image_down, text_four, image_self, image_self_out,
    )
    pairs, regions = image_regions.shape[0], image_regions.shape[1]
    padding = (-regions) % 16

    def pad_regions(array):
        return jnp.pad(array, ((0, 0), (0, padding), (0, 0))).reshape(-1, array.shape[-1])

    def flat(array):
        return array.reshape(-1, array.shape[-1])

    (
        text_result, image_result, text_input_grad, image_input_grad,
        text_left, image_left, text_right, text_extra, image_right, text_norms, image_norms,
    ) = layer(
        lengths, region_counts,
        (flat(text_tokens), pad_regions(image_regions), flat(text_cotangent), pad_regions(image_cotangent)),
        (text_gains, text_shifts, image_gains, image_shifts),
        weights, mp, more,
    )
    text_result, text_input_grad = [
        array.reshape(text_tokens.shape) for array in (text_result, text_input_grad)
    ]
    image_result, image_input_grad = [
        array.reshape(pairs, regions + padding, -1)[:, :regions]
        for array in (image_result, image_input_grad)
    ]
    norms = jnp.concatenate([text_norms.reshape(-1, 128), image_norms.reshape(-1, 128)])
    text_sums, image_sums, norm_sums = reduce_all(
        text_left, text_right, text_extra, image_left, image_right, norms, more
    )
    if more > 1:
        norm_sums = lax.psum(norm_sums, "dp") / 8
        text_sums, image_sums = outer_sum(text_sums, more), outer_sum(image_sums, more)

    def wide(sums, first, last):
        return jnp.concatenate([sums[n] for n in range(first, last)], -1)

    share, ups = text_self.shape[-1], text_up.shape[-1] // 256
    selfs = wide(text_sums, 4 + 2 * ups, text_sums.shape[0])
    text_parts = [text_sums[0:3], text_sums[3], wide(text_sums, 4, 4 + ups), wide(text_sums, 4 + ups, 4 + 2 * ups)]
    text_parts += [jnp.stack([selfs[:, n * share : (n + 1) * share] for n in range(3)]), selfs[:, 3 * share :]]
    image_parts = [image_sums[0:3], image_sums[3], image_sums[4], image_sums[5], image_sums[6:9], image_sums[9]]
    flat_norms = norm_sums.reshape(-1)
    text_size, image_size = text_gains.size, image_gains.size
    text_end = 2 * text_size
    return (
        text_result,
        image_result,
        text_input_grad,
        image_input_grad,
        text_parts[0],
        image_parts[0],
        text_parts[1].T,
        image_parts[1].T,
        text_parts[2],
        text_parts[3].T,
        image_parts[2],
        image_parts[3].T,
        text_parts[4],
        text_parts[5].T,
        image_parts[4],
        image_parts[5].T,
        flat_norms[:text_size].reshape(text_gains.shape),
        flat_norms[text_size:text_end].reshape(text_shifts.shape),
        flat_norms[text_end : text_end + image_size].reshape(image_gains.shape),
        flat_norms[text_end + image_size :].reshape(image_shifts.shape),
    )


def outer_sum(sums, more):
    chunks, rows, width = sums.shape
    apart = sums.reshape(chunks, 1, more, rows // more, width)
    low = lax.axis_index("dp") // more
    spread = jnp.zeros((chunks, 8, more, rows // more, width), sums.dtype)
    spread = lax.dynamic_update_slice(spread, apart, (0, low, 0, 0, 0))
    spread = spread.reshape(chunks, 8 * rows, width)
    return lax.psum_scatter(spread, "dp", scatter_dimension=1, tiled=True)


def solution(mesh):
    in_specs = (
        P(("dp", "mp"), None, None),
        P(("dp", "mp"), None, None),
        P(("dp", "mp")),
        P(("dp", "mp")),
        P(None, None, "mp"),
        P(None, None, "mp"),
        P("mp", None),
        P("mp", None),
        P(None, "mp"),
        P("mp", None),
        P(None, "mp"),
        P("mp", None),
        P(None, None, "mp"),
        P("mp", None),
        P(None, None, "mp"),
        P("mp", None),
        P(),
        P(),
        P(),
        P(),
        P(("dp", "mp"), None, None),
        P(("dp", "mp"), None, None),
    )
    out_specs = (
        P(("dp", "mp"), None, None),
        P(("dp", "mp"), None, None),
        P(("dp", "mp"), None, None),
        P(("dp", "mp"), None, None),
        P(None, "dp", "mp"),
        P(None, "dp", "mp"),
        P("mp", "dp"),
        P("mp", "dp"),
        P("dp", "mp"),
        P("mp", "dp"),
        P("dp", "mp"),
        P("mp", "dp"),
        P(None, "dp", "mp"),
        P("mp", "dp"),
        P(None, "dp", "mp"),
        P("mp", "dp"),
        P(),
        P(),
        P(),
        P(),
    )
    return jax.shard_map(shards, mesh=mesh, in_specs=in_specs, out_specs=out_specs, check_vma=False)
```

```python
import functools
import math

import jax
import jax.numpy as jnp
from jax import lax
from jax.experimental import pallas as pl
from jax.experimental.pallas import tpu as pltpu
from jax.sharding import PartitionSpec as P

TEXT_HEAD = 64
CROSS_HEAD = 128
IMAGE_HEAD = 128


EPSILON = 1e-05
MASKED = -1e30
MESH_ID = pl.DeviceIdType.MESH


def flip(index, step):
    return index + step * (1 - 2 * ((index // step) % 2))


def position(unit):
    data, model = lax.axis_index("dp"), lax.axis_index("mp")
    return data, model, (data // unit) % 2, (data // (2 * unit)) % 2, (data // (4 * unit)) % 2


def greet(data, model, unit):
    barrier = pltpu.get_barrier_semaphore()
    partners = [(flip(data, step * unit), model) for step in (1, 2, 4)]
    partners += [(data, flip(model, step)) for step in (1, 2)]
    for partner in partners:
        pl.semaphore_signal(barrier, inc=1, device_id=partner, device_id_type=MESH_ID)
    pl.semaphore_wait(barrier, len(partners))


LAGS = (0, 2, 4, 6, 8)


def gather_steps(unit, kinds, chunks, ins, outs, send_sem, recv_sem):
    data, model, c, x, y = position(unit)
    near, far = flip(model, 1), flip(model, 2)
    corner = flip(near, 2)
    copies = {}

    def send(n, slot, source, target, partner):
        copies[n, slot] = pltpu.make_async_remote_copy(
            src_ref=source,
            dst_ref=target,
            send_sem=send_sem.at[n, slot],
            recv_sem=recv_sem.at[n, slot],
            device_id=partner,
            device_id_type=MESH_ID,
        )
        copies[n, slot].start()

    def rows_of(height, first, base, span):
        start, count = span
        return pl.ds(pl.multiple_of(base + start * (height // 8), 8), count * (height // 8))

    def mine(n, span):
        k, matrix, unused, unused = chunks[n]
        if kinds[k] == "cols":
            return ins[k].at[matrix, rows_of(ins[k].shape[1], 0, 0, span), :]
        return ins[k].at[rows_of(ins[k].shape[0], 0, 0, span), :]

    def piece(n, shard, span):
        k, matrix, unused, unused = chunks[n]
        if kinds[k] == "cols":
            width = ins[k].shape[2]
            columns = pl.ds(pl.multiple_of(shard * width, 128), width)
            return outs[k].at[matrix, rows_of(ins[k].shape[1], 0, 0, span), columns]
        height = ins[k].shape[0]
        return outs[k].at[rows_of(height, 0, shard * height, span), :]

    x_side = (flip(data, 2 * unit), model)
    y_side = (flip(data, 4 * unit), model)
    z_side = (data, near)

    def relay(n, slot, shard, span, partner):
        block = piece(n, shard, span)
        send(n, slot, block, block, partner)

    def advance(n, stage):
        x_first, early = chunks[n][2:]
        first, second = (x_side, y_side) if x_first else (y_side, x_side)
        low_bit, middle_bit = (x, y) if x_first else (y, x)
        single = (4 * c + 2 * middle_bit + low_bit, 1)
        double = (4 * c + 2 * middle_bit, 2)
        if stage == 0:
            send(n, 0, mine(n, single), piece(n, model, single), (data, far))
        elif stage == 1 and not early:
            send(n, 1, mine(n, single), piece(n, model, single), z_side)
            copies[n, 0].wait_recv()
            relay(n, 2, far, single, z_side)
        elif stage == 2 and not early:
            relay(n, 3, far, single, first)
            copies[n, 1].wait_recv()
            relay(n, 4, near, single, first)
            copies[n, 2].wait_recv()
            relay(n, 5, corner, single, first)
        elif stage == 1:
            copies[n, 0].wait_recv()
            relay(n, 3, far, single, first)
        elif stage == 2:
            send(n, 1, mine(n, double), piece(n, model, double), z_side)
            copies[n, 3].wait_recv()
            relay(n, 2, far, double, z_side)
        elif stage == 3:
            before = (None, 1, 2) if early else (3, 4, 5)
            for number, shard in enumerate((far, near, corner)):
                if before[number] is not None:
                    copies[n, before[number]].wait_recv()
                relay(n, 6 + number, shard, double, second)
        else:
            for number, shard in enumerate((far, near, corner)):
                copies[n, 6 + number].wait_recv()
                relay(n, 9 + number, shard, (4 * c, 4), (flip(data, unit), model))

    total = len(chunks)
    done = [0]

    def run(limit):
        while done[0] < min(limit, total + LAGS[-1]):
            for stage, lag in enumerate(LAGS):
                if 0 <= done[0] - lag < total:
                    advance(done[0] - lag, stage)
            done[0] += 1

    def arrived(numbers):
        run(max(numbers) + LAGS[-1] + 1)
        for n in numbers:
            for slot in range(9, 12):
                copies[n, slot].wait_recv()

    def finish():
        for copy in copies.values():
            copy.wait_send()

    return run, arrived, finish


KINDS = ("cols", "cols", "rows", "rows", "cols", "rows", "cols", "rows", "cols", "cols", "rows")
SEQUENCE = (
    (0, 0), (1, 0), (0, 1), (1, 1), (0, 2), (1, 2), (2, None), (3, None), (4, 0), (6, 0), (5, None), (7, None),
    (8, 0), (9, 0), (8, 1), (9, 1), (8, 2), (9, 2), (8, 3), (10, None),
)


def chunk_plan():
    return tuple(
        (k, matrix, n % 4 in (0, 3), n % 2 == 1) for n, (k, matrix) in enumerate(SEQUENCE)
    )


def steps_up(k, marks):
    total = 0
    for mark in marks:
        total = total + jnp.where(k >= mark, 1, 0)
    return total


STAGE_LAGS = (0, 2, 4, 6, 8, 10)
TEXT_MARKS = (3, 4, 7, 10)
IMAGE_MARKS = (3, 4, 5, 6, 9)


def reduce_kernel(
    unit,
    text_left, text_right, text_extra, image_left, image_right, norms,
    text_out, image_out, norm_out,
    text_send, image_send,
    text_r0, text_r1, text_r2, text_r3, text_r4,
    image_r0, image_r1, image_r2, image_r3, image_r4,
    norm_buf,
    text_ss, text_rs, image_ss, image_rs, norm_ss, norm_rs,
):
    data, model, c, x, y = position(unit)
    low, high = model % 2, (model // 2) % 2
    f32, bf16 = jnp.float32, jnp.bfloat16
    core = (flip(data, unit), model)
    along_x = (flip(data, 2 * unit), model)
    along_y = (flip(data, 4 * unit), model)
    near = (data, flip(model, 1))
    far = (data, flip(model, 2))
    greet(data, model, unit)

    def stream(left, right, extra, out, outgoing, bufs, send_sem, recv_sem, marks, turn_first):
        r0, r1, r2, r3, r4 = bufs
        total = right.shape[0]
        rows = left.shape[-2]

        def order(k):
            by_y = (k + turn_first) % 2
            by_x = 1 - by_y
            first, second = x * by_x + y * by_y, y * by_x + x * by_y
            return by_x, first, second

        def copy(k, stage):
            by_x, first, second = order(k)
            if stage == 0:
                pair = (outgoing.at[k % 2], r0.at[k], core)
            elif stage == 1:
                pair = (r0.at[k, 1 - first], r1.at[k], (flip(data, (4 - 2 * by_x) * unit), model))
            elif stage == 2:
                pair = (r1.at[k, :, :, 1 - low], r2.at[k], near)
            elif stage == 3:
                pair = (r2.at[k, 1 - second], r3.at[k], (flip(data, (2 + 2 * by_x) * unit), model))
            else:
                pair = (r3.at[k, 1 - high], r4.at[k], far)
            return pltpu.make_async_remote_copy(
                src_ref=pair[0], dst_ref=pair[1],
                send_sem=send_sem.at[k, stage], recv_sem=recv_sem.at[k, stage],
                device_id=pair[2], device_id_type=MESH_ID,
            )

        def products(k, half, put):
            lhs = left[half, steps_up(k, marks)].reshape(4 * rows, left.shape[-1])

            def plain():
                for z in range(4):
                    value = jnp.dot(lhs, right[k, z], preferred_element_type=f32)
                    put(z, value.reshape(2, 2, rows, 256))

            if extra is None:
                plain()
                return
            pl.when(k != total - 1)(plain)

            @pl.when(k == total - 1)
            def _():
                more = left[half, 5].reshape(4 * rows, left.shape[-1])
                for z in range(4):
                    value = jnp.dot(lhs, right[k, z], preferred_element_type=f32)
                    value += jnp.dot(more, extra[z], preferred_element_type=f32)
                    put(z, value.reshape(2, 2, rows, 256))

        def places(k):
            by_x, unused, unused = order(k)
            for y_side in range(2):
                for x_side in range(2):
                    first = x_side * by_x + y_side * (1 - by_x)
                    yield y_side, x_side, first, y_side + x_side - first

        def begin(k):
            @pl.when(k >= 2)
            def _():
                copy(k - 2, 0).wait_send()

            def put(z, value):
                for y_side, x_side, first, second in places(k):
                    outgoing[k % 2, first, second, z // 2, z % 2] = value[y_side, x_side].astype(bf16)

            products(k, 1 - c, put)
            copy(k, 0).start()

        def join(k):
            copy(k, 0).wait_recv()

            def put(z, value):
                for y_side, x_side, first, second in places(k):
                    held = r0[k, first, second, z // 2, z % 2].astype(f32)
                    r0[k, first, second, z // 2, z % 2] = (held + value[y_side, x_side]).astype(bf16)

            products(k, c, put)
            copy(k, 1).start()

        def add_into(target, k, kept):
            target[k] = (target[k].astype(f32) + kept.astype(f32)).astype(bf16)

        def second(k):
            copy(k, 1).wait_recv()
            add_into(r1, k, r0[k, order(k)[1]])
            copy(k, 2).start()

        def third(k):
            copy(k, 2).wait_recv()
            add_into(r2, k, r1[k, :, :, low])
            copy(k, 3).start()

        def fourth(k):
            copy(k, 3).wait_recv()
            add_into(r3, k, r2[k, order(k)[2]])
            copy(k, 4).start()

        def last(k):
            copy(k, 4).wait_recv()
            out[k] = r4[k].astype(f32) + r3[k, high].astype(f32)

        def finish():
            def body(k, carry):
                for stage in range(1, 5):
                    copy(k, stage).wait_send()
                return carry

            lax.fori_loop(0, total, body, 0)
            copy(total - 2, 0).wait_send()
            copy(total - 1, 0).wait_send()

        return total, (begin, join, second, third, fourth, last), finish

    text_total, text_stages, text_finish = stream(
        text_left, text_right, text_extra, text_out, text_send,
        (text_r0, text_r1, text_r2, text_r3, text_r4), text_ss, text_rs, TEXT_MARKS, 0,
    )
    image_total, image_stages, image_finish = stream(
        image_left, image_right, None, image_out, image_send,
        (image_r0, image_r1, image_r2, image_r3, image_r4), image_ss, image_rs, IMAGE_MARKS, 1,
    )
    lags = STAGE_LAGS
    partners = (core, along_x, along_y, near, far)

    def norm_copy(stage):
        return pltpu.make_async_remote_copy(
            src_ref=norms if stage == 0 else norm_buf.at[stage - 1],
            dst_ref=norm_buf.at[stage],
            send_sem=norm_ss.at[stage], recv_sem=norm_rs.at[stage],
            device_id=partners[stage], device_id_type=MESH_ID,
        )

    def turn(t, carry):
        for lag, text_stage, image_stage in zip(lags, text_stages, image_stages):
            k = t - lag
            pl.when((k >= 0) & (k < text_total))(functools.partial(text_stage, k))
            pl.when((k >= 0) & (k < image_total))(functools.partial(image_stage, k))
        for stage in range(6):

            @pl.when(t == 2 * stage)
            def _(stage=stage):
                if stage > 0:
                    norm_copy(stage - 1).wait_recv()
                    held = norms[...] if stage == 1 else norm_buf[stage - 2]
                    if stage < 5:
                        norm_buf[stage - 1] += held
                    else:
                        norm_out[...] = norm_buf[stage - 1] + held
                if stage < 5:
                    norm_copy(stage).start()

        return carry

    lax.fori_loop(0, max(text_total, image_total) + lags[-1], turn, 0)
    text_finish()
    image_finish()
    for stage in range(5):
        norm_copy(stage).wait_send()


def reduce_all(text_left, text_right, text_extra, image_left, image_right, norms, unit):
    bf16, f32 = jnp.bfloat16, jnp.float32

    def buffers(right, left):
        total, rows = right.shape[0], left.shape[-2]
        tail = (rows, 256)
        return [
            pltpu.VMEM((total, 2, 2, 2, 2) + tail, bf16),
            pltpu.VMEM((total, 2, 2, 2) + tail, bf16),
            pltpu.VMEM((total, 2, 2) + tail, bf16),
            pltpu.VMEM((total, 2) + tail, bf16),
            pltpu.VMEM((total,) + tail, bf16),
        ]

    def outgoing(left):
        return pltpu.VMEM((2, 2, 2, 2, 2, left.shape[-2], 256), bf16)

    texts, images = text_right.shape[0], image_right.shape[0]
    sems = []
    for total in (texts, images):
        sems += [pltpu.SemaphoreType.DMA((total, 5))] * 2
    sems += [pltpu.SemaphoreType.DMA((5,))] * 2
    return pl.pallas_call(
        functools.partial(reduce_kernel, unit),
        out_shape=[
            jax.ShapeDtypeStruct((texts, text_left.shape[-2], 256), f32),
            jax.ShapeDtypeStruct((images, image_left.shape[-2], 256), f32),
            jax.ShapeDtypeStruct(norms.shape, f32),
        ],
        in_specs=[pl.BlockSpec(memory_space=pltpu.VMEM)] * 6,
        out_specs=[pl.BlockSpec(memory_space=pltpu.VMEM)] * 3,
        scratch_shapes=[outgoing(text_left), outgoing(image_left)]
        + buffers(text_right, text_left)
        + buffers(image_right, image_left)
        + [pltpu.VMEM((5,) + norms.shape, f32)]
        + sems,
        compiler_params=pltpu.CompilerParams(
            collective_id=1, has_side_effects=True, vmem_limit_bytes=67043328
        ),
        name="reduce_gradients",
    )(text_left, text_right, text_extra, image_left, image_right, norms)


ROOT_HALF = math.sqrt(0.5)
DENSITY = 1.0 / math.sqrt(2.0 * math.pi)
TILE = 256


def block_of(rows):
    return next(size for size in (64, 48, 32, 16) if rows % size == 0)


def dot_nn(a, b):
    return jnp.dot(a, b, preferred_element_type=jnp.float32)


def dot_nt(a, b):
    return lax.dot_general(a, b, (((1,), (1,)), ((), ())), preferred_element_type=jnp.float32)


def joint_nt(parts, weights, width, z):
    tiles = [weights[n * width : (n + 1) * width, tile_at(z)] for n in range(len(parts))]
    return dot_nt(jnp.concatenate(parts, -1), jnp.concatenate(tiles, -1))


def dot_tn(a, b):
    return lax.dot_general(a, b, (((0,), (0,)), ((), ())), preferred_element_type=jnp.float32)


def row_blocks(rows, body):
    size = block_of(rows)

    def step(i, carry):
        body(pl.ds(pl.multiple_of(i * size, size), size))
        return carry

    lax.fori_loop(0, rows // size, step, 0)


def tile_at(j):
    return pl.ds(pl.multiple_of(j * TILE, TILE), TILE)


def probabilities(query, keys, mask, head_size):
    scores = dot_nt(query, keys) * (1.0 / math.sqrt(head_size))
    scores = jnp.where(mask > 0.5, scores, MASKED)
    lifted = jnp.exp(scores - jnp.max(scores, -1, keepdims=True))
    return lifted / jnp.sum(lifted, -1, keepdims=True)


def head_forward(query, keys, values, mask, head_size):
    probs = probabilities(query, keys, mask, head_size)
    return dot_nn(probs.astype(jnp.bfloat16), values).astype(jnp.bfloat16)


def head_back(query, keys, values, mask, head_size, context_grad):
    bf16 = jnp.bfloat16
    probs = probabilities(query, keys, mask, head_size)
    value_grad = dot_tn(probs.astype(bf16), context_grad)
    prob_grad = dot_nt(context_grad, values)
    inner = jnp.sum(probs * prob_grad, -1, keepdims=True)
    score_grad = (probs * (prob_grad - inner)).astype(bf16)
    scale = 1.0 / math.sqrt(head_size)
    query_grad = dot_nn(score_grad, keys) * scale
    key_grad = dot_tn(score_grad, query) * scale
    return query_grad.astype(bf16), key_grad.astype(bf16), value_grad.astype(bf16)


def norm_forward(number, res, acc, xhat, rstd, gains, shifts, lows):
    def block(rows):
        hidden = res[rows, :] + acc[rows, :]
        centred = hidden - jnp.mean(hidden, -1, keepdims=True)
        scale = lax.rsqrt(jnp.mean(centred * centred, -1, keepdims=True) + EPSILON)
        unit = centred * scale
        xhat[number, rows, :] = unit
        rstd[number, rows, :] = jnp.broadcast_to(scale, (scale.shape[0], 128))
        out = unit * gains[number : number + 1, :] + shifts[number : number + 1, :]
        res[rows, :] = out
        if lows is not None:
            lows[rows, :] = out.astype(jnp.bfloat16)

    row_blocks(res.shape[0], block)


def norm_backward(number, grad, acc, xhat, rstd, gains, low, norms):
    count = gains.shape[0]
    width = grad.shape[1]
    size = block_of(grad.shape[0])

    def step(i, carry):
        gain_sum, shift_sum = carry
        rows = pl.ds(pl.multiple_of(i * size, size), size)
        coming = grad[rows, :] if acc is None else grad[rows, :] + acc[rows, :]
        unit = xhat[number, rows, :]
        gain_sum += jnp.sum(coming * unit, 0, keepdims=True)
        shift_sum += jnp.sum(coming, 0, keepdims=True)
        scaled = coming * gains[number : number + 1, :]
        mean = jnp.mean(scaled, -1, keepdims=True)
        slope = jnp.mean(scaled * unit, -1, keepdims=True)
        out = (scaled - mean - unit * slope) * rstd[number, rows, 0:1]
        grad[rows, :] = out
        low[rows, :] = out.astype(jnp.bfloat16)
        return gain_sum, shift_sum

    zero = jnp.zeros((1, width), jnp.float32)
    gain_sum, shift_sum = lax.fori_loop(0, grad.shape[0] // size, step, (zero, zero))
    norms[number : number + 1, :] = gain_sum
    norms[count + number : count + number + 1, :] = shift_sum


def turn_over(left, tokens, rows):
    part = left.shape[4]
    for number, source in enumerate((tokens, rows.at[2], rows.at[0], rows.at[3], rows.at[1], rows.at[4])):
        turned = source[...].T
        for y in range(2):
            for x in range(2):
                for c in range(2):
                    first = (4 * y + 2 * x + c) * part
                    left[c, number, y, x] = turned[first : first + part]


def layer_kernel(
    unit,
    lengths, counts, text_tokens, image_tokens, text_cot, image_cot,
    text_gains, text_shifts, image_gains, image_shifts,
    in_a, in_b, in_c, in_d, in_e, in_f, in_g, in_h, in_i, in_j, in_k,
    text_output, image_output, text_grad, image_grad,
    text_left, image_left, text_right, text_extra, image_right, text_norms, image_norms,
    full_a, full_b, full_c, full_d, full_e, full_f, full_g, full_h, full_i, full_j, full_k,
    send_sem, recv_sem, slot, load_sem, text_acc, image_acc, text_xhat, image_xhat, text_rstd, image_rstd,
    text_slope, image_slope, text_qkv, image_qkv, text_sqkv, image_sqkv,
    mask_ti, mask_it, mask_tt, mask_ii, text_rows, image_rows,
):
    f32, bf16 = jnp.float32, jnp.bfloat16
    rows_t, rows_i = text_tokens.shape[0], image_tokens.shape[0]
    width_t, width_i = text_tokens.shape[1], image_tokens.shape[1]
    pairs = lengths.shape[0]
    per_t, per_i = rows_t // pairs, rows_i // pairs
    zs = text_right.shape[1]
    inner = zs * TILE
    ins = (in_a, in_b, in_c, in_d, in_e, in_f, in_g, in_h, in_i, in_j, in_k)
    fulls = (full_a, full_b, full_c, full_d, full_e, full_f, full_g, full_h, full_i, full_j, full_k)
    ups = in_e.shape[2] // TILE
    data, model, unused, unused, unused = position(unit)
    greet(data, model, unit)
    run, arrived, finish = gather_steps(unit, KINDS, chunk_plan(), ins, fulls, send_sem, recv_sem)
    run(6)

    def three(k):
        return [(k, n, n * ins[k].shape[1], False) for n in range(ins[k].shape[0])]

    loads = {
        "tc": three(0),
        "ic": three(1),
        "out": [(2, None, 0, False), (3, None, inner, False)],
        "tu": [(4, 0, 0, True)],
        "td": [(5, None, 0, False)],
        "if": [(6, 0, 0, False), (7, None, width_i, False)],
        "ts": three(8),
        "is": three(9),
        "io": [(10, None, 0, False)],
    }
    order = ["tc", "ic", "out", "tu", "td", "if", "ts", "is", "io"]
    order += ["td", "if", "tu", "out", "tc", "ic"]
    slots = [0, 1, 2, 0, 1, 2, 0, 1, 2, 2, 0, 1, 2, 0, 1]

    def copies(number):
        where, found = slots[number], []
        for k, matrix, row, stacked in loads[order[number]]:
            for turn in range(zs):
                shard = (model + turn) % zs
                if matrix is None:
                    height, width = ins[k].shape
                    source = fulls[k].at[pl.ds(pl.multiple_of(shard * height, 8), height), :]
                    source = ins[k] if turn == 0 else source
                    rows = pl.ds(pl.multiple_of(row + shard * height, 8), height)
                    target = slot.at[where, rows, pl.ds(0, width)]
                else:
                    unused, height, width = ins[k].shape
                    columns = pl.ds(pl.multiple_of(shard * width, 128), width)
                    source = ins[k].at[matrix] if turn == 0 else fulls[k].at[matrix, :, columns]
                    if stacked:
                        rows = pl.ds(pl.multiple_of(row + shard * height, 8), height)
                        target = slot.at[where, rows, pl.ds(0, width)]
                    else:
                        target = slot.at[where, pl.ds(row, height), columns]
                found.append(pltpu.make_async_copy(source, target, load_sem.at[number, len(found)]))
        return found

    def start(number):
        if number < 9:
            wanted = {k for k, unused, unused, unused in loads[order[number]]}
            arrived([n for n, chunk in enumerate(SEQUENCE) if chunk[0] in wanted])
        for copy in copies(number):
            copy.start()

    def ready(number):
        for copy in copies(number):
            copy.wait()
        return slot.at[slots[number]]

    def set_mask(ref, query_per, key_per, limits):
        query = lax.broadcasted_iota(jnp.int32, ref.shape, 0)
        key = lax.broadcasted_iota(jnp.int32, ref.shape, 1)
        seen = jnp.zeros(ref.shape, f32)
        for pair in range(pairs):
            inside = (query >= pair * query_per) & (query < (pair + 1) * query_per)
            inside &= (key >= pair * key_per) & (key < pair * key_per + limits[pair])
            seen = jnp.where(inside, 1.0, seen)
        ref[...] = seen

    set_mask(mask_ti, per_t, per_i, counts)
    set_mask(mask_it, per_i, per_t, lengths)
    set_mask(mask_tt, per_t, per_t, lengths)
    set_mask(mask_ii, per_i, per_i, counts)
    text_output[...] = text_tokens[...].astype(f32)
    image_output[...] = image_tokens[...].astype(f32)

    def clear():
        text_acc[...] = jnp.zeros(text_acc.shape, f32)
        image_acc[...] = jnp.zeros(image_acc.shape, f32)

    clear()

    def project_tiles(rows_ref, weights, width, kept):
        def body(z, carry):
            for n in range(3):
                tile = dot_nn(rows_ref[...], weights[n * width : (n + 1) * width, tile_at(z)])
                kept[n, :, tile_at(z)] = tile.astype(bf16)
            return carry

        lax.fori_loop(0, zs, body, 0, unroll=True)

    def halves(tile):
        return tile[:, :128], tile[:, 128:]

    def pair_heads(fn, count, *tiles):
        size = TILE // count if count == 2 else 64
        results = []
        for h in range(count):
            results.append(fn(*[tile[:, h * size : (h + 1) * size] for tile in tiles]))
        return results

    start(0)
    start(1)
    run(16)
    project_tiles(text_tokens, ready(0), width_t, text_qkv)
    start(2)
    project_tiles(image_tokens, ready(1), width_i, image_qkv)
    run(18)
    outs = ready(2)

    def cross_forward_tile(z, carry):
        tq, tk, tv = [text_qkv[n, :, tile_at(z)] for n in range(3)]
        iq, ik, iv = [image_qkv[n, :, tile_at(z)] for n in range(3)]
        text_heads = pair_heads(
            lambda q, k, v: head_forward(q, k, v, mask_ti[...], CROSS_HEAD), 2, tq, ik, iv
        )
        image_heads = pair_heads(
            lambda q, k, v: head_forward(q, k, v, mask_it[...], CROSS_HEAD), 2, iq, tk, tv
        )
        text_context = jnp.concatenate(text_heads, -1)
        image_context = jnp.concatenate(image_heads, -1)
        text_right[3, z] = text_context
        image_right[3, z] = image_context
        text_acc[...] += dot_nn(text_context, outs[tile_at(z), 0:width_t])
        offset = pl.ds(pl.multiple_of(inner + z * TILE, TILE), TILE)
        image_acc[...] += dot_nn(image_context, outs[offset, 0:width_i])
        return carry

    lax.fori_loop(0, zs // 2, cross_forward_tile, 0)
    start(3)
    run(19)
    lax.fori_loop(zs // 2, zs, cross_forward_tile, 0)
    start(4)
    norm_forward(0, text_output, text_acc, text_xhat, text_rstd, text_gains, text_shifts, text_rows.at[0])
    norm_forward(0, image_output, image_acc, image_xhat, image_rstd, image_gains, image_shifts, image_rows.at[0])

    def gelu_tile(upper):
        normal = 0.5 * (1.0 + lax.erf(upper * ROOT_HALF))
        slope = normal + upper * (DENSITY * jnp.exp(-0.5 * upper * upper))
        return (upper * normal).astype(bf16), slope

    start(5)
    run(21)
    up_t = ready(3)

    def text_up_tile(j, carry):
        rows = pl.ds(pl.multiple_of((j // ups) * width_t, 8), width_t)
        upper = dot_nn(text_rows[0], up_t[rows, tile_at(j % ups)])
        middle, slope = gelu_tile(upper)
        text_slope[j] = slope
        text_right[7 + j % ups, j // ups] = middle
        return carry

    lax.fori_loop(0, zs * ups // 2, text_up_tile, 0, unroll=2)
    run(22)
    lax.fori_loop(zs * ups // 2, zs * ups, text_up_tile, 0, unroll=2)
    run(23)
    down_t = ready(4)
    clear()

    def text_down_tile(j, carry):
        joined = jnp.concatenate([text_right[7 + part, j] for part in range(ups)], -1)
        rows = pl.ds(pl.multiple_of(j * ups * TILE, TILE), ups * TILE)
        text_acc[...] += dot_nn(joined, down_t[rows, 0:width_t])
        return carry

    lax.fori_loop(0, zs, text_down_tile, 0)
    run(24)
    both_i = ready(5)

    def image_up_tile(z, carry):
        middle, slope = gelu_tile(dot_nn(image_rows[0], both_i[0:width_i, tile_at(z)]))
        image_slope[z] = slope
        image_right[5, z] = middle
        offset = pl.ds(pl.multiple_of(width_i + z * TILE, TILE), TILE)
        image_acc[...] += dot_nn(middle, both_i[offset, 0:width_i])
        return carry

    lax.fori_loop(0, zs, image_up_tile, 0, unroll=True)
    run(25)
    norm_forward(1, text_output, text_acc, text_xhat, text_rstd, text_gains, text_shifts, text_rows.at[1])
    norm_forward(1, image_output, image_acc, image_xhat, image_rstd, image_gains, image_shifts, image_rows.at[1])

    clear()
    start(6)
    start(7)
    start(8)
    self_t = ready(6)
    project_tiles(text_rows.at[1], self_t, width_t, text_sqkv)
    self_i = ready(7)
    project_tiles(image_rows.at[1], self_i, width_i, image_sqkv)
    out_i = ready(8)
    share = TILE - TEXT_HEAD
    heads_t = share // TEXT_HEAD

    def self_forward_tile(z, carry):
        text_tiles = [text_sqkv[n, :, tile_at(z)] for n in range(3)]
        heads = pair_heads(
            lambda q, k, v: head_forward(q, k, v, mask_tt[...], TEXT_HEAD), heads_t, *text_tiles
        )
        blank = jnp.zeros((rows_t, TEXT_HEAD), bf16)
        text_extra[z] = jnp.concatenate([blank] + heads, -1)
        context = jnp.concatenate(heads + [blank], -1)
        text_acc[...] += dot_nt(context, self_t[3 * width_t : 4 * width_t, tile_at(z)])
        image_tiles = [image_sqkv[n, :, tile_at(z)] for n in range(3)]
        image_heads = pair_heads(
            lambda q, k, v: head_forward(q, k, v, mask_ii[...], IMAGE_HEAD), 2, *image_tiles
        )
        image_context = jnp.concatenate(image_heads, -1)
        image_right[9, z] = image_context
        image_acc[...] += dot_nn(image_context, out_i[tile_at(z), 0:width_i])
        return carry

    lax.fori_loop(0, zs, self_forward_tile, 0)
    norm_forward(2, text_output, text_acc, text_xhat, text_rstd, text_gains, text_shifts, None)
    norm_forward(2, image_output, image_acc, image_xhat, image_rstd, image_gains, image_shifts, None)

    text_grad[...] = text_cot[...].astype(f32)
    image_grad[...] = image_cot[...].astype(f32)
    norm_backward(2, text_grad, None, text_xhat, text_rstd, text_gains, text_rows.at[4], text_norms)
    norm_backward(2, image_grad, None, image_xhat, image_rstd, image_gains, image_rows.at[4], image_norms)
    clear()

    def self_back_tile(z, carry):
        text_tiles = [text_sqkv[n, :, tile_at(z)] for n in range(3)]
        context_grad = dot_nt_rows(text_rows[4], self_t, z)
        grads = pair_heads(
            lambda q, k, v, d: head_back(q, k, v, mask_tt[...], TEXT_HEAD, d),
            heads_t, *text_tiles, context_grad,
        )
        blank = jnp.zeros((rows_t, TEXT_HEAD), bf16)
        dq, dk, dv = [[grads[h][n] for h in range(heads_t)] for n in range(3)]
        pieces = dq + dk + dv
        text_right[10, z] = jnp.concatenate(pieces[0:4], -1)
        text_right[11, z] = jnp.concatenate(pieces[4:8], -1)
        text_right[12, z] = jnp.concatenate(pieces[8:9] + [blank] * 3, -1)
        joined = [jnp.concatenate(parts + [blank], -1) for parts in (dq, dk, dv)]
        text_acc[...] += joint_nt(joined, self_t, width_t, z)
        return carry

    def dot_nt_rows(coming, weights, z):
        return dot_nn(coming, weights[3 * width_t : 4 * width_t, tile_at(z)]).astype(bf16)

    def self_back_image(z, carry):
        image_tiles = [image_sqkv[n, :, tile_at(z)] for n in range(3)]
        context_grad = dot_nt(image_rows[4], out_i[tile_at(z), 0:width_i]).astype(bf16)
        grads = pair_heads(
            lambda q, k, v, d: head_back(q, k, v, mask_ii[...], IMAGE_HEAD, d),
            2, *image_tiles, context_grad,
        )
        joined = [jnp.concatenate([grads[0][n], grads[1][n]], -1) for n in range(3)]
        for n in range(3):
            image_right[6 + n, z] = joined[n]
        image_acc[...] += joint_nt(joined, self_i, width_i, z)
        return carry

    lax.fori_loop(0, zs, self_back_image, 0, unroll=2)
    start(9)
    lax.fori_loop(0, zs, self_back_tile, 0, unroll=2)
    start(10)
    start(11)
    norm_backward(1, text_grad, text_acc, text_xhat, text_rstd, text_gains, text_rows.at[3], text_norms)
    norm_backward(1, image_grad, image_acc, image_xhat, image_rstd, image_gains, image_rows.at[3], image_norms)
    clear()

    back_down = ready(9)

    def text_down_back(j, carry):
        middle_grad = dot_nt(text_rows[3], back_down[tile_at(j), 0:width_t])
        text_right[4 + j % ups, j // ups] = (middle_grad * text_slope[j]).astype(bf16)
        return carry

    lax.fori_loop(0, zs * ups, text_down_back, 0, unroll=2)
    start(12)
    back_i = ready(10)

    def image_ffn_back(z, carry):
        offset = pl.ds(pl.multiple_of(width_i + z * TILE, TILE), TILE)
        middle_grad = dot_nt(image_rows[3], back_i[offset, 0:width_i])
        upper_grad = (middle_grad * image_slope[z]).astype(bf16)
        image_right[4, z] = upper_grad
        image_acc[...] += dot_nt(upper_grad, back_i[0:width_i, tile_at(z)])
        return carry

    lax.fori_loop(0, zs, image_ffn_back, 0, unroll=2)
    start(13)
    back_up = ready(11)

    def text_up_back(j, carry):
        joined = jnp.concatenate([text_right[4 + part, j] for part in range(ups)], -1)
        rows = pl.ds(pl.multiple_of(j * width_t, 8), width_t)
        text_acc[...] += dot_nt(joined, back_up[rows, 0 : ups * TILE])
        return carry

    lax.fori_loop(0, zs, text_up_back, 0)
    start(14)
    norm_backward(0, text_grad, text_acc, text_xhat, text_rstd, text_gains, text_rows.at[2], text_norms)
    norm_backward(0, image_grad, image_acc, image_xhat, image_rstd, image_gains, image_rows.at[2], image_norms)
    clear()

    back_out = ready(12)
    cross_t = ready(13)
    cross_i = ready(14)

    def cross_back_tile(z, carry):
        tq, tk, tv = [text_qkv[n, :, tile_at(z)] for n in range(3)]
        iq, ik, iv = [image_qkv[n, :, tile_at(z)] for n in range(3)]
        text_ctx_grad = dot_nt(text_rows[2], back_out[tile_at(z), 0:width_t]).astype(bf16)
        offset = pl.ds(pl.multiple_of(inner + z * TILE, TILE), TILE)
        image_ctx_grad = dot_nt(image_rows[2], back_out[offset, 0:width_i]).astype(bf16)
        text_side = pair_heads(
            lambda q, k, v, d: head_back(q, k, v, mask_ti[...], CROSS_HEAD, d), 2, tq, ik, iv, text_ctx_grad
        )
        image_side = pair_heads(
            lambda q, k, v, d: head_back(q, k, v, mask_it[...], CROSS_HEAD, d), 2, iq, tk, tv, image_ctx_grad
        )

        def joined(side, n):
            return jnp.concatenate([side[0][n], side[1][n]], -1)

        text_parts = (joined(text_side, 0), joined(image_side, 1), joined(image_side, 2))
        image_parts = (joined(image_side, 0), joined(text_side, 1), joined(text_side, 2))
        for n in range(3):
            text_right[n, z] = text_parts[n]
            image_right[n, z] = image_parts[n]
        text_acc[...] += joint_nt(text_parts, cross_t, width_t, z)
        image_acc[...] += joint_nt(image_parts, cross_i, width_i, z)
        return carry

    lax.fori_loop(0, zs, cross_back_tile, 0, unroll=2)
    text_grad[...] += text_acc[...]
    image_grad[...] += image_acc[...]
    finish()
    turn_over(text_left, text_tokens, text_rows)
    turn_over(image_left, image_tokens, image_rows)


def layer(lengths, counts, rows, params, weights, mp, unit):
    f32, bf16 = jnp.float32, jnp.bfloat16
    text_tokens, image_tokens = rows[0], rows[1]
    rows_t, width_t = text_tokens.shape
    rows_i, width_i = image_tokens.shape
    text_tiles = mp * weights[4].shape[2] // TILE
    inner = mp * TILE

    vmem = pl.BlockSpec(memory_space=pltpu.VMEM)
    out_shape = [
        jax.ShapeDtypeStruct((rows_t, width_t), f32),
        jax.ShapeDtypeStruct((rows_i, width_i), f32),
        jax.ShapeDtypeStruct((rows_t, width_t), f32),
        jax.ShapeDtypeStruct((rows_i, width_i), f32),
        jax.ShapeDtypeStruct((2, 6, 2, 2, width_t // 8, rows_t), bf16),
        jax.ShapeDtypeStruct((2, 6, 2, 2, width_i // 8, rows_i), bf16),
        jax.ShapeDtypeStruct((13, mp, rows_t, TILE), bf16),
        jax.ShapeDtypeStruct((mp, rows_t, TILE), bf16),
        jax.ShapeDtypeStruct((10, mp, rows_i, TILE), bf16),
        jax.ShapeDtypeStruct((2 * params[0].shape[0], width_t), f32),
        jax.ShapeDtypeStruct((2 * params[0].shape[0], width_i), f32),
    ]
    fulls = []
    for array, kind in zip(weights, KINDS):
        shape = array.shape[:-1] + (mp * array.shape[-1],) if kind == "cols" else (mp * array.shape[0], array.shape[1])
        fulls.append(jax.ShapeDtypeStruct(shape, bf16))
    chunks = len(SEQUENCE)
    results = pl.pallas_call(
        functools.partial(layer_kernel, unit),
        out_shape=out_shape + fulls,
        in_specs=[pl.BlockSpec(memory_space=pltpu.SMEM)] * 2
        + [vmem] * 8
        + [pl.BlockSpec(memory_space=pl.ANY)] * len(weights),
        out_specs=[vmem] * len(out_shape) + [pl.BlockSpec(memory_space=pl.ANY)] * len(fulls),
        scratch_shapes=[
            pltpu.SemaphoreType.DMA((chunks, 12)),
            pltpu.SemaphoreType.DMA((chunks, 12)),
            pltpu.VMEM((3, 3 * width_i, inner), bf16),
            pltpu.SemaphoreType.DMA((15, 4 * mp)),
            pltpu.VMEM((rows_t, width_t), f32),
            pltpu.VMEM((rows_i, width_i), f32),
            pltpu.VMEM((3, rows_t, width_t), f32),
            pltpu.VMEM((3, rows_i, width_i), f32),
            pltpu.VMEM((3, rows_t, 128), f32),
            pltpu.VMEM((3, rows_i, 128), f32),
            pltpu.VMEM((text_tiles, rows_t, TILE), f32),
            pltpu.VMEM((mp, rows_i, TILE), f32),
            pltpu.VMEM((3, rows_t, inner), bf16),
            pltpu.VMEM((3, rows_i, inner), bf16),
            pltpu.VMEM((3, rows_t, inner), bf16),
            pltpu.VMEM((3, rows_i, inner), bf16),
            pltpu.VMEM((rows_t, rows_i), f32),
            pltpu.VMEM((rows_i, rows_t), f32),
            pltpu.VMEM((rows_t, rows_t), f32),
            pltpu.VMEM((rows_i, rows_i), f32),
            pltpu.VMEM((5, rows_t, width_t), bf16),
            pltpu.VMEM((5, rows_i, width_i), bf16),
        ],
        compiler_params=pltpu.CompilerParams(
            collective_id=0, has_side_effects=True, vmem_limit_bytes=67043328
        ),
        name="layer",
    )(lengths, counts, *rows, *params, *weights)
    return results[: len(out_shape)]


def shards(
    text_tokens, image_regions, lengths, region_counts, text_cross, image_cross, text_cross_out,
    image_cross_out, text_up, text_down, image_up, image_down, text_self, text_self_out, image_self,
    image_self_out, text_gains, text_shifts, image_gains, image_shifts, text_cotangent, image_cotangent,
):
    mp, dp = lax.axis_size("mp"), lax.axis_size("dp")
    more = dp // 8
    text_out_turned = text_self_out.T[None]
    text_four = jnp.concatenate([text_self, text_out_turned])
    spare = 256 - text_four.shape[-1]
    text_four = jnp.pad(text_four, ((0, 0), (0, 0), (0, spare)))
    weights = (
        text_cross, image_cross, text_cross_out, image_cross_out, text_up[None], text_down,
        image_up[None], image_down, text_four, image_self, image_self_out,
    )
    pairs, regions = image_regions.shape[0], image_regions.shape[1]
    padding = (-regions) % 16

    def pad_regions(array):
        return jnp.pad(array, ((0, 0), (0, padding), (0, 0))).reshape(-1, array.shape[-1])

    def flat(array):
        return array.reshape(-1, array.shape[-1])

    (
        text_result, image_result, text_input_grad, image_input_grad,
        text_left, image_left, text_right, text_extra, image_right, text_norms, image_norms,
    ) = layer(
        lengths, region_counts,
        (flat(text_tokens), pad_regions(image_regions), flat(text_cotangent), pad_regions(image_cotangent)),
        (text_gains, text_shifts, image_gains, image_shifts),
        weights, mp, more,
    )
    text_result, text_input_grad = [
        array.reshape(text_tokens.shape) for array in (text_result, text_input_grad)
    ]
    image_result, image_input_grad = [
        array.reshape(pairs, regions + padding, -1)[:, :regions]
        for array in (image_result, image_input_grad)
    ]
    norms = jnp.concatenate([text_norms.reshape(-1, 128), image_norms.reshape(-1, 128)])
    text_sums, image_sums, norm_sums = reduce_all(
        text_left, text_right, text_extra, image_left, image_right, norms, more
    )
    if more > 1:
        norm_sums = lax.psum(norm_sums, "dp") / 8
        text_sums, image_sums = outer_sum(text_sums, more), outer_sum(image_sums, more)

    def wide(sums, first, last):
        return jnp.concatenate([sums[n] for n in range(first, last)], -1)

    share, ups = text_self.shape[-1], text_up.shape[-1] // 256
    selfs = wide(text_sums, 4 + 2 * ups, text_sums.shape[0])
    text_parts = [text_sums[0:3], text_sums[3], wide(text_sums, 4, 4 + ups), wide(text_sums, 4 + ups, 4 + 2 * ups)]
    text_parts += [jnp.stack([selfs[:, n * share : (n + 1) * share] for n in range(3)]), selfs[:, 3 * share :]]
    image_parts = [image_sums[0:3], image_sums[3], image_sums[4], image_sums[5], image_sums[6:9], image_sums[9]]
    flat_norms = norm_sums.reshape(-1)
    text_size, image_size = text_gains.size, image_gains.size
    text_end = 2 * text_size
    return (
        text_result,
        image_result,
        text_input_grad,
        image_input_grad,
        text_parts[0],
        image_parts[0],
        text_parts[1].T,
        image_parts[1].T,
        text_parts[2],
        text_parts[3].T,
        image_parts[2],
        image_parts[3].T,
        text_parts[4],
        text_parts[5].T,
        image_parts[4],
        image_parts[5].T,
        flat_norms[:text_size].reshape(text_gains.shape),
        flat_norms[text_size:text_end].reshape(text_shifts.shape),
        flat_norms[text_end : text_end + image_size].reshape(image_gains.shape),
        flat_norms[text_end + image_size :].reshape(image_shifts.shape),
    )


def outer_sum(sums, more):
    chunks, rows, width = sums.shape
    apart = sums.reshape(chunks, 1, more, rows // more, width)
    low = lax.axis_index("dp") // more
    spread = jnp.zeros((chunks, 8, more, rows // more, width), sums.dtype)
    spread = lax.dynamic_update_slice(spread, apart, (0, low, 0, 0, 0))
    spread = spread.reshape(chunks, 8 * rows, width)
    return lax.psum_scatter(spread, "dp", scatter_dimension=1, tiled=True)


def solution(mesh):
    in_specs = (
        P(("dp", "mp"), None, None),
        P(("dp", "mp"), None, None),
        P(("dp", "mp")),
        P(("dp", "mp")),
        P(None, None, "mp"),
        P(None, None, "mp"),
        P("mp", None),
        P("mp", None),
        P(None, "mp"),
        P("mp", None),
        P(None, "mp"),
        P("mp", None),
        P(None, None, "mp"),
        P("mp", None),
        P(None, None, "mp"),
        P("mp", None),
        P(),
        P(),
        P(),
        P(),
        P(("dp", "mp"), None, None),
        P(("dp", "mp"), None, None),
    )
    out_specs = (
        P(("dp", "mp"), None, None),
        P(("dp", "mp"), None, None),
        P(("dp", "mp"), None, None),
        P(("dp", "mp"), None, None),
        P(None, "dp", "mp"),
        P(None, "dp", "mp"),
        P("mp", "dp"),
        P("mp", "dp"),
        P("dp", "mp"),
        P("mp", "dp"),
        P("dp", "mp"),
        P("mp", "dp"),
        P(None, "dp", "mp"),
        P("mp", "dp"),
        P(None, "dp", "mp"),
        P("mp", "dp"),
        P(),
        P(),
        P(),
        P(),
    )
    return jax.shard_map(shards, mesh=mesh, in_specs=in_specs, out_specs=out_specs, check_vma=False)
```

```python
import functools
import math

import jax
import jax.numpy as jnp
from jax import lax
from jax.experimental import pallas as pl
from jax.experimental.pallas import tpu as pltpu
from jax.sharding import PartitionSpec as P

TEXT_HEAD = 64
CROSS_HEAD = 128
IMAGE_HEAD = 128


EPSILON = 1e-05
MASKED = -1e30
MESH_ID = pl.DeviceIdType.MESH


def flip(index, step):
    return index + step * (1 - 2 * ((index // step) % 2))


def position(unit):
    data, model = lax.axis_index("dp"), lax.axis_index("mp")
    return data, model, (data // unit) % 2, (data // (2 * unit)) % 2, (data // (4 * unit)) % 2


def greet(data, model, unit):
    barrier = pltpu.get_barrier_semaphore()
    partners = [(flip(data, step * unit), model) for step in (1, 2, 4)]
    partners += [(data, flip(model, step)) for step in (1, 2)]
    for partner in partners:
        pl.semaphore_signal(barrier, inc=1, device_id=partner, device_id_type=MESH_ID)
    pl.semaphore_wait(barrier, len(partners))


LAGS = (0, 2, 4, 6, 8)


def gather_steps(unit, kinds, chunks, ins, outs, send_sem, recv_sem):
    data, model, c, x, y = position(unit)
    near, far = flip(model, 1), flip(model, 2)
    corner = flip(near, 2)
    copies = {}

    def send(n, slot, source, target, partner):
        copies[n, slot] = pltpu.make_async_remote_copy(
            src_ref=source,
            dst_ref=target,
            send_sem=send_sem.at[n, slot],
            recv_sem=recv_sem.at[n, slot],
            device_id=partner,
            device_id_type=MESH_ID,
        )
        copies[n, slot].start()

    def rows_of(height, first, base, span):
        start, count = span
        return pl.ds(pl.multiple_of(base + start * (height // 8), 8), count * (height // 8))

    def mine(n, span):
        k, matrix, unused, unused = chunks[n]
        if kinds[k] == "cols":
            return ins[k].at[matrix, rows_of(ins[k].shape[1], 0, 0, span), :]
        return ins[k].at[rows_of(ins[k].shape[0], 0, 0, span), :]

    def piece(n, shard, span):
        k, matrix, unused, unused = chunks[n]
        if kinds[k] == "cols":
            width = ins[k].shape[2]
            columns = pl.ds(pl.multiple_of(shard * width, 128), width)
            return outs[k].at[matrix, rows_of(ins[k].shape[1], 0, 0, span), columns]
        height = ins[k].shape[0]
        return outs[k].at[rows_of(height, 0, shard * height, span), :]

    x_side = (flip(data, 2 * unit), model)
    y_side = (flip(data, 4 * unit), model)
    z_side = (data, near)

    def relay(n, slot, shard, span, partner):
        block = piece(n, shard, span)
        send(n, slot, block, block, partner)

    def advance(n, stage):
        x_first, early = chunks[n][2:]
        first, second = (x_side, y_side) if x_first else (y_side, x_side)
        low_bit, middle_bit = (x, y) if x_first else (y, x)
        single = (4 * c + 2 * middle_bit + low_bit, 1)
        double = (4 * c + 2 * middle_bit, 2)
        if stage == 0:
            send(n, 0, mine(n, single), piece(n, model, single), (data, far))
        elif stage == 1 and not early:
            send(n, 1, mine(n, single), piece(n, model, single), z_side)
            copies[n, 0].wait_recv()
            relay(n, 2, far, single, z_side)
        elif stage == 2 and not early:
            relay(n, 3, far, single, first)
            copies[n, 1].wait_recv()
            relay(n, 4, near, single, first)
            copies[n, 2].wait_recv()
            relay(n, 5, corner, single, first)
        elif stage == 1:
            copies[n, 0].wait_recv()
            relay(n, 3, far, single, first)
        elif stage == 2:
            send(n, 1, mine(n, double), piece(n, model, double), z_side)
            copies[n, 3].wait_recv()
            relay(n, 2, far, double, z_side)
        elif stage == 3:
            before = (None, 1, 2) if early else (3, 4, 5)
            for number, shard in enumerate((far, near, corner)):
                if before[number] is not None:
                    copies[n, before[number]].wait_recv()
                relay(n, 6 + number, shard, double, second)
        else:
            for number, shard in enumerate((far, near, corner)):
                copies[n, 6 + number].wait_recv()
                relay(n, 9 + number, shard, (4 * c, 4), (flip(data, unit), model))

    total = len(chunks)
    done = [0]

    def run(limit):
        while done[0] < min(limit, total + LAGS[-1]):
            for stage, lag in enumerate(LAGS):
                if 0 <= done[0] - lag < total:
                    advance(done[0] - lag, stage)
            done[0] += 1

    def arrived(numbers):
        run(max(numbers) + LAGS[-1] + 1)
        for n in numbers:
            for slot in range(9, 12):
                copies[n, slot].wait_recv()

    def finish():
        for copy in copies.values():
            copy.wait_send()

    return run, arrived, finish


KINDS = ("cols", "cols", "rows", "rows", "cols", "rows", "cols", "rows", "cols", "cols", "rows")
SEQUENCE = (
    (0, 0), (1, 0), (0, 1), (1, 1), (0, 2), (1, 2), (2, None), (3, None), (4, 0), (6, 0), (5, None), (7, None),
    (8, 0), (9, 0), (8, 1), (9, 1), (8, 2), (9, 2), (8, 3), (10, None),
)


def chunk_plan():
    return tuple(
        (k, matrix, n % 4 in (0, 3), n % 2 == 1) for n, (k, matrix) in enumerate(SEQUENCE)
    )


def steps_up(k, marks):
    total = 0
    for mark in marks:
        total = total + jnp.where(k >= mark, 1, 0)
    return total


STAGE_LAGS = (0, 2, 4, 6, 8, 10)
TEXT_MARKS = (3, 4, 7, 10)
IMAGE_MARKS = (3, 4, 5, 6, 9)


def reduce_kernel(
    unit,
    text_left, text_right, text_extra, image_left, image_right, norms,
    text_out, image_out, norm_out,
    text_send, image_send,
    text_r0, text_r1, text_r2, text_r3, text_r4,
    image_r0, image_r1, image_r2, image_r3, image_r4,
    norm_buf,
    text_ss, text_rs, image_ss, image_rs, norm_ss, norm_rs,
):
    data, model, c, x, y = position(unit)
    low, high = model % 2, (model // 2) % 2
    f32, bf16 = jnp.float32, jnp.bfloat16
    core = (flip(data, unit), model)
    along_x = (flip(data, 2 * unit), model)
    along_y = (flip(data, 4 * unit), model)
    near = (data, flip(model, 1))
    far = (data, flip(model, 2))
    greet(data, model, unit)

    def stream(left, right, extra, out, outgoing, bufs, send_sem, recv_sem, marks, turn_first):
        r0, r1, r2, r3, r4 = bufs
        total = right.shape[0]
        rows = left.shape[-2]

        def order(k):
            by_y = (k + turn_first) % 2
            by_x = 1 - by_y
            first, second = x * by_x + y * by_y, y * by_x + x * by_y
            return by_x, first, second

        def copy(k, stage):
            by_x, first, second = order(k)
            if stage == 0:
                pair = (outgoing.at[k % 2], r0.at[k], core)
            elif stage == 1:
                pair = (r0.at[k, 1 - first], r1.at[k], (flip(data, (4 - 2 * by_x) * unit), model))
            elif stage == 2:
                pair = (r1.at[k, :, :, 1 - low], r2.at[k], near)
            elif stage == 3:
                pair = (r2.at[k, 1 - second], r3.at[k], (flip(data, (2 + 2 * by_x) * unit), model))
            else:
                pair = (r3.at[k, 1 - high], r4.at[k], far)
            return pltpu.make_async_remote_copy(
                src_ref=pair[0], dst_ref=pair[1],
                send_sem=send_sem.at[k, stage], recv_sem=recv_sem.at[k, stage],
                device_id=pair[2], device_id_type=MESH_ID,
            )

        def products(k, half, put):
            lhs = left[half, steps_up(k, marks)].reshape(4 * rows, left.shape[-1])

            def plain():
                for z in range(4):
                    value = jnp.dot(lhs, right[k, z], preferred_element_type=f32)
                    put(z, value.reshape(2, 2, rows, 256))

            if extra is None:
                plain()
                return
            pl.when(k != total - 1)(plain)

            @pl.when(k == total - 1)
            def _():
                more = left[half, 5].reshape(4 * rows, left.shape[-1])
                for z in range(4):
                    value = jnp.dot(lhs, right[k, z], preferred_element_type=f32)
                    value += jnp.dot(more, extra[z], preferred_element_type=f32)
                    put(z, value.reshape(2, 2, rows, 256))

        def places(k):
            by_x, unused, unused = order(k)
            for y_side in range(2):
                for x_side in range(2):
                    first = x_side * by_x + y_side * (1 - by_x)
                    yield y_side, x_side, first, y_side + x_side - first

        def begin(k):
            @pl.when(k >= 2)
            def _():
                copy(k - 2, 0).wait_send()

            def put(z, value):
                for y_side, x_side, first, second in places(k):
                    outgoing[k % 2, first, second, z // 2, z % 2] = value[y_side, x_side].astype(bf16)

            products(k, 1 - c, put)
            copy(k, 0).start()

        def join(k):
            copy(k, 0).wait_recv()

            def put(z, value):
                for y_side, x_side, first, second in places(k):
                    held = r0[k, first, second, z // 2, z % 2].astype(f32)
                    r0[k, first, second, z // 2, z % 2] = (held + value[y_side, x_side]).astype(bf16)

            products(k, c, put)
            copy(k, 1).start()

        def add_into(target, k, kept):
            target[k] = (target[k].astype(f32) + kept.astype(f32)).astype(bf16)

        def second(k):
            copy(k, 1).wait_recv()
            add_into(r1, k, r0[k, order(k)[1]])
            copy(k, 2).start()

        def third(k):
            copy(k, 2).wait_recv()
            add_into(r2, k, r1[k, :, :, low])
            copy(k, 3).start()

        def fourth(k):
            copy(k, 3).wait_recv()
            add_into(r3, k, r2[k, order(k)[2]])
            copy(k, 4).start()

        def last(k):
            copy(k, 4).wait_recv()
            out[k] = r4[k].astype(f32) + r3[k, high].astype(f32)

        def finish():
            def body(k, carry):
                for stage in range(1, 5):
                    copy(k, stage).wait_send()
                return carry

            lax.fori_loop(0, total, body, 0)
            copy(total - 2, 0).wait_send()
            copy(total - 1, 0).wait_send()

        return total, (begin, join, second, third, fourth, last), finish

    text_total, text_stages, text_finish = stream(
        text_left, text_right, text_extra, text_out, text_send,
        (text_r0, text_r1, text_r2, text_r3, text_r4), text_ss, text_rs, TEXT_MARKS, 0,
    )
    image_total, image_stages, image_finish = stream(
        image_left, image_right, None, image_out, image_send,
        (image_r0, image_r1, image_r2, image_r3, image_r4), image_ss, image_rs, IMAGE_MARKS, 1,
    )
    lags = STAGE_LAGS
    partners = (core, along_x, along_y, near, far)

    def norm_copy(stage):
        return pltpu.make_async_remote_copy(
            src_ref=norms if stage == 0 else norm_buf.at[stage - 1],
            dst_ref=norm_buf.at[stage],
            send_sem=norm_ss.at[stage], recv_sem=norm_rs.at[stage],
            device_id=partners[stage], device_id_type=MESH_ID,
        )

    def turn(t, carry):
        for lag, text_stage, image_stage in zip(lags, text_stages, image_stages):
            k = t - lag
            pl.when((k >= 0) & (k < text_total))(functools.partial(text_stage, k))
            pl.when((k >= 0) & (k < image_total))(functools.partial(image_stage, k))
        for stage in range(6):

            @pl.when(t == 2 * stage)
            def _(stage=stage):
                if stage > 0:
                    norm_copy(stage - 1).wait_recv()
                    held = norms[...] if stage == 1 else norm_buf[stage - 2]
                    if stage < 5:
                        norm_buf[stage - 1] += held
                    else:
                        norm_out[...] = norm_buf[stage - 1] + held
                if stage < 5:
                    norm_copy(stage).start()

        return carry

    lax.fori_loop(0, max(text_total, image_total) + lags[-1], turn, 0)
    text_finish()
    image_finish()
    for stage in range(5):
        norm_copy(stage).wait_send()


def reduce_all(text_left, text_right, text_extra, image_left, image_right, norms, unit):
    bf16, f32 = jnp.bfloat16, jnp.float32

    def buffers(right, left):
        total, rows = right.shape[0], left.shape[-2]
        tail = (rows, 256)
        return [
            pltpu.VMEM((total, 2, 2, 2, 2) + tail, bf16),
            pltpu.VMEM((total, 2, 2, 2) + tail, bf16),
            pltpu.VMEM((total, 2, 2) + tail, bf16),
            pltpu.VMEM((total, 2) + tail, bf16),
            pltpu.VMEM((total,) + tail, bf16),
        ]

    def outgoing(left):
        return pltpu.VMEM((2, 2, 2, 2, 2, left.shape[-2], 256), bf16)

    texts, images = text_right.shape[0], image_right.shape[0]
    sems = []
    for total in (texts, images):
        sems += [pltpu.SemaphoreType.DMA((total, 5))] * 2
    sems += [pltpu.SemaphoreType.DMA((5,))] * 2
    return pl.pallas_call(
        functools.partial(reduce_kernel, unit),
        out_shape=[
            jax.ShapeDtypeStruct((texts, text_left.shape[-2], 256), f32),
            jax.ShapeDtypeStruct((images, image_left.shape[-2], 256), f32),
            jax.ShapeDtypeStruct(norms.shape, f32),
        ],
        in_specs=[pl.BlockSpec(memory_space=pltpu.VMEM)] * 6,
        out_specs=[pl.BlockSpec(memory_space=pltpu.VMEM)] * 3,
        scratch_shapes=[outgoing(text_left), outgoing(image_left)]
        + buffers(text_right, text_left)
        + buffers(image_right, image_left)
        + [pltpu.VMEM((5,) + norms.shape, f32)]
        + sems,
        compiler_params=pltpu.CompilerParams(
            collective_id=1, has_side_effects=True, vmem_limit_bytes=67043328
        ),
        name="reduce_gradients",
    )(text_left, text_right, text_extra, image_left, image_right, norms)


ROOT_HALF = math.sqrt(0.5)
DENSITY = 1.0 / math.sqrt(2.0 * math.pi)
TILE = 256


def block_of(rows):
    return next(size for size in (64, 48, 32, 16) if rows % size == 0)


def dot_nn(a, b):
    return jnp.dot(a, b, preferred_element_type=jnp.float32)


def dot_nt(a, b):
    return lax.dot_general(a, b, (((1,), (1,)), ((), ())), preferred_element_type=jnp.float32)


def joint_nt(parts, weights, width, z):
    tiles = [weights[n * width : (n + 1) * width, tile_at(z)] for n in range(len(parts))]
    return dot_nt(jnp.concatenate(parts, -1), jnp.concatenate(tiles, -1))


def dot_tn(a, b):
    return lax.dot_general(a, b, (((0,), (0,)), ((), ())), preferred_element_type=jnp.float32)


def row_blocks(rows, body):
    size = block_of(rows)

    def step(i, carry):
        body(pl.ds(pl.multiple_of(i * size, size), size))
        return carry

    lax.fori_loop(0, rows // size, step, 0)


def tile_at(j):
    return pl.ds(pl.multiple_of(j * TILE, TILE), TILE)


def probabilities(query, keys, mask, head_size):
    scores = dot_nt(query, keys) * (1.0 / math.sqrt(head_size))
    scores = jnp.where(mask > 0.5, scores, MASKED)
    lifted = jnp.exp(scores - jnp.max(scores, -1, keepdims=True))
    return lifted / jnp.sum(lifted, -1, keepdims=True)


def head_forward(query, keys, values, mask, head_size):
    probs = probabilities(query, keys, mask, head_size)
    return dot_nn(probs.astype(jnp.bfloat16), values).astype(jnp.bfloat16)


def head_back(query, keys, values, mask, head_size, context_grad):
    bf16 = jnp.bfloat16
    probs = probabilities(query, keys, mask, head_size)
    value_grad = dot_tn(probs.astype(bf16), context_grad)
    prob_grad = dot_nt(context_grad, values)
    inner = jnp.sum(probs * prob_grad, -1, keepdims=True)
    score_grad = (probs * (prob_grad - inner)).astype(bf16)
    scale = 1.0 / math.sqrt(head_size)
    query_grad = dot_nn(score_grad, keys) * scale
    key_grad = dot_tn(score_grad, query) * scale
    return query_grad.astype(bf16), key_grad.astype(bf16), value_grad.astype(bf16)


def norm_forward(number, res, acc, xhat, rstd, gains, shifts, lows):
    def block(rows):
        hidden = res[rows, :] + acc[rows, :]
        centred = hidden - jnp.mean(hidden, -1, keepdims=True)
        scale = lax.rsqrt(jnp.mean(centred * centred, -1, keepdims=True) + EPSILON)
        unit = centred * scale
        xhat[number, rows, :] = unit
        rstd[number, rows, :] = jnp.broadcast_to(scale, (scale.shape[0], 128))
        out = unit * gains[number : number + 1, :] + shifts[number : number + 1, :]
        res[rows, :] = out
        if lows is not None:
            lows[rows, :] = out.astype(jnp.bfloat16)

    row_blocks(res.shape[0], block)


def norm_backward(number, grad, acc, xhat, rstd, gains, low, norms):
    count = gains.shape[0]
    width = grad.shape[1]
    size = block_of(grad.shape[0])

    def step(i, carry):
        gain_sum, shift_sum = carry
        rows = pl.ds(pl.multiple_of(i * size, size), size)
        coming = grad[rows, :] if acc is None else grad[rows, :] + acc[rows, :]
        unit = xhat[number, rows, :]
        gain_sum += jnp.sum(coming * unit, 0, keepdims=True)
        shift_sum += jnp.sum(coming, 0, keepdims=True)
        scaled = coming * gains[number : number + 1, :]
        mean = jnp.mean(scaled, -1, keepdims=True)
        slope = jnp.mean(scaled * unit, -1, keepdims=True)
        out = (scaled - mean - unit * slope) * rstd[number, rows, 0:1]
        grad[rows, :] = out
        low[rows, :] = out.astype(jnp.bfloat16)
        return gain_sum, shift_sum

    zero = jnp.zeros((1, width), jnp.float32)
    gain_sum, shift_sum = lax.fori_loop(0, grad.shape[0] // size, step, (zero, zero))
    norms[number : number + 1, :] = gain_sum
    norms[count + number : count + number + 1, :] = shift_sum


def turn_over(left, sources):
    part = left.shape[4]
    for number, source in sources:
        turned = source[...].T
        for y in range(2):
            for x in range(2):
                for c in range(2):
                    first = (4 * y + 2 * x + c) * part
                    left[c, number, y, x] = turned[first : first + part]


def layer_kernel(
    unit,
    lengths, counts, text_tokens, image_tokens, text_cot, image_cot,
    text_gains, text_shifts, image_gains, image_shifts,
    in_a, in_b, in_c, in_d, in_e, in_f, in_g, in_h, in_i, in_j, in_k,
    text_output, image_output, text_grad, image_grad,
    text_left, image_left, text_right, text_extra, image_right, text_norms, image_norms,
    full_a, full_b, full_c, full_d, full_e, full_f, full_g, full_h, full_i, full_j, full_k,
    send_sem, recv_sem, slot, load_sem, text_acc, image_acc, text_xhat, image_xhat, text_rstd, image_rstd,
    text_slope, image_slope, text_qkv, image_qkv, text_sqkv, image_sqkv,
    mask_ti, mask_it, mask_tt, mask_ii, text_rows, image_rows,
):
    f32, bf16 = jnp.float32, jnp.bfloat16
    rows_t, rows_i = text_tokens.shape[0], image_tokens.shape[0]
    width_t, width_i = text_tokens.shape[1], image_tokens.shape[1]
    pairs = lengths.shape[0]
    per_t, per_i = rows_t // pairs, rows_i // pairs
    zs = text_right.shape[1]
    inner = zs * TILE
    ins = (in_a, in_b, in_c, in_d, in_e, in_f, in_g, in_h, in_i, in_j, in_k)
    fulls = (full_a, full_b, full_c, full_d, full_e, full_f, full_g, full_h, full_i, full_j, full_k)
    ups = in_e.shape[2] // TILE
    data, model, unused, unused, unused = position(unit)
    greet(data, model, unit)
    run, arrived, finish = gather_steps(unit, KINDS, chunk_plan(), ins, fulls, send_sem, recv_sem)
    run(6)

    def three(k):
        return [(k, n, n * ins[k].shape[1], False) for n in range(ins[k].shape[0])]

    loads = {
        "tc": three(0),
        "ic": three(1),
        "out": [(2, None, 0, False), (3, None, inner, False)],
        "tu": [(4, 0, 0, True)],
        "td": [(5, None, 0, False)],
        "if": [(6, 0, 0, False), (7, None, width_i, False)],
        "ts": three(8),
        "is": three(9),
        "io": [(10, None, 0, False)],
    }
    order = ["tc", "ic", "out", "tu", "td", "if", "ts", "is", "io"]
    order += ["td", "if", "tu", "out", "tc", "ic"]
    slots = [0, 1, 2, 0, 1, 2, 0, 1, 2, 2, 0, 1, 2, 0, 1]

    def copies(number):
        where, found = slots[number], []
        for k, matrix, row, stacked in loads[order[number]]:
            for turn in range(zs):
                shard = (model + turn) % zs
                if matrix is None:
                    height, width = ins[k].shape
                    source = fulls[k].at[pl.ds(pl.multiple_of(shard * height, 8), height), :]
                    source = ins[k] if turn == 0 else source
                    rows = pl.ds(pl.multiple_of(row + shard * height, 8), height)
                    target = slot.at[where, rows, pl.ds(0, width)]
                else:
                    unused, height, width = ins[k].shape
                    columns = pl.ds(pl.multiple_of(shard * width, 128), width)
                    source = ins[k].at[matrix] if turn == 0 else fulls[k].at[matrix, :, columns]
                    if stacked:
                        rows = pl.ds(pl.multiple_of(row + shard * height, 8), height)
                        target = slot.at[where, rows, pl.ds(0, width)]
                    else:
                        target = slot.at[where, pl.ds(row, height), columns]
                found.append(pltpu.make_async_copy(source, target, load_sem.at[number, len(found)]))
        return found

    def start(number):
        if number < 9:
            wanted = {k for k, unused, unused, unused in loads[order[number]]}
            arrived([n for n, chunk in enumerate(SEQUENCE) if chunk[0] in wanted])
        for copy in copies(number):
            copy.start()

    def ready(number):
        for copy in copies(number):
            copy.wait()
        return slot.at[slots[number]]

    def set_mask(ref, query_per, key_per, limits):
        query = lax.broadcasted_iota(jnp.int32, ref.shape, 0)
        key = lax.broadcasted_iota(jnp.int32, ref.shape, 1)
        seen = jnp.zeros(ref.shape, f32)
        for pair in range(pairs):
            inside = (query >= pair * query_per) & (query < (pair + 1) * query_per)
            inside &= (key >= pair * key_per) & (key < pair * key_per + limits[pair])
            seen = jnp.where(inside, 1.0, seen)
        ref[...] = seen

    set_mask(mask_ti, per_t, per_i, counts)
    set_mask(mask_it, per_i, per_t, lengths)
    set_mask(mask_tt, per_t, per_t, lengths)
    set_mask(mask_ii, per_i, per_i, counts)
    text_output[...] = text_tokens[...].astype(f32)
    image_output[...] = image_tokens[...].astype(f32)

    def clear():
        text_acc[...] = jnp.zeros(text_acc.shape, f32)
        image_acc[...] = jnp.zeros(image_acc.shape, f32)

    clear()

    def project_tiles(rows_ref, weights, width, kept):
        def body(z, carry):
            for n in range(3):
                tile = dot_nn(rows_ref[...], weights[n * width : (n + 1) * width, tile_at(z)])
                kept[n, :, tile_at(z)] = tile.astype(bf16)
            return carry

        lax.fori_loop(0, zs, body, 0, unroll=True)

    def halves(tile):
        return tile[:, :128], tile[:, 128:]

    def pair_heads(fn, count, *tiles):
        size = TILE // count if count == 2 else 64
        results = []
        for h in range(count):
            results.append(fn(*[tile[:, h * size : (h + 1) * size] for tile in tiles]))
        return results

    start(0)
    start(1)
    run(16)
    project_tiles(text_tokens, ready(0), width_t, text_qkv)
    start(2)
    project_tiles(image_tokens, ready(1), width_i, image_qkv)
    run(18)
    outs = ready(2)

    def cross_forward_tile(z, carry):
        tq, tk, tv = [text_qkv[n, :, tile_at(z)] for n in range(3)]
        iq, ik, iv = [image_qkv[n, :, tile_at(z)] for n in range(3)]
        text_heads = pair_heads(
            lambda q, k, v: head_forward(q, k, v, mask_ti[...], CROSS_HEAD), 2, tq, ik, iv
        )
        image_heads = pair_heads(
            lambda q, k, v: head_forward(q, k, v, mask_it[...], CROSS_HEAD), 2, iq, tk, tv
        )
        text_context = jnp.concatenate(text_heads, -1)
        image_context = jnp.concatenate(image_heads, -1)
        text_right[3, z] = text_context
        image_right[3, z] = image_context
        text_acc[...] += dot_nn(text_context, outs[tile_at(z), 0:width_t])
        offset = pl.ds(pl.multiple_of(inner + z * TILE, TILE), TILE)
        image_acc[...] += dot_nn(image_context, outs[offset, 0:width_i])
        return carry

    lax.fori_loop(0, zs // 2, cross_forward_tile, 0)
    start(3)
    run(19)
    lax.fori_loop(zs // 2, zs, cross_forward_tile, 0)
    start(4)
    norm_forward(0, text_output, text_acc, text_xhat, text_rstd, text_gains, text_shifts, text_rows.at[0])
    norm_forward(0, image_output, image_acc, image_xhat, image_rstd, image_gains, image_shifts, image_rows.at[0])

    def gelu_tile(upper):
        normal = 0.5 * (1.0 + lax.erf(upper * ROOT_HALF))
        slope = normal + upper * (DENSITY * jnp.exp(-0.5 * upper * upper))
        return (upper * normal).astype(bf16), slope

    start(5)
    run(21)
    up_t = ready(3)

    def text_up_tile(j, carry):
        rows = pl.ds(pl.multiple_of((j // ups) * width_t, 8), width_t)
        upper = dot_nn(text_rows[0], up_t[rows, tile_at(j % ups)])
        middle, slope = gelu_tile(upper)
        text_slope[j] = slope
        text_right[7 + j % ups, j // ups] = middle
        return carry

    lax.fori_loop(0, zs * ups // 2, text_up_tile, 0, unroll=2)
    run(22)
    lax.fori_loop(zs * ups // 2, zs * ups, text_up_tile, 0, unroll=2)
    run(23)
    down_t = ready(4)
    clear()

    def text_down_tile(j, carry):
        joined = jnp.concatenate([text_right[7 + part, j] for part in range(ups)], -1)
        rows = pl.ds(pl.multiple_of(j * ups * TILE, TILE), ups * TILE)
        text_acc[...] += dot_nn(joined, down_t[rows, 0:width_t])
        return carry

    lax.fori_loop(0, zs, text_down_tile, 0)
    run(24)
    both_i = ready(5)

    def image_up_tile(z, carry):
        middle, slope = gelu_tile(dot_nn(image_rows[0], both_i[0:width_i, tile_at(z)]))
        image_slope[z] = slope
        image_right[5, z] = middle
        offset = pl.ds(pl.multiple_of(width_i + z * TILE, TILE), TILE)
        image_acc[...] += dot_nn(middle, both_i[offset, 0:width_i])
        return carry

    lax.fori_loop(0, zs, image_up_tile, 0, unroll=True)
    run(25)
    norm_forward(1, text_output, text_acc, text_xhat, text_rstd, text_gains, text_shifts, text_rows.at[1])
    norm_forward(1, image_output, image_acc, image_xhat, image_rstd, image_gains, image_shifts, image_rows.at[1])

    clear()
    run(26)
    turn_over(text_left, ((0, text_tokens), (2, text_rows.at[0]), (4, text_rows.at[1])))
    run(27)
    turn_over(image_left, ((0, image_tokens), (2, image_rows.at[0]), (4, image_rows.at[1])))
    start(6)
    start(7)
    start(8)
    self_t = ready(6)
    project_tiles(text_rows.at[1], self_t, width_t, text_sqkv)
    self_i = ready(7)
    project_tiles(image_rows.at[1], self_i, width_i, image_sqkv)
    out_i = ready(8)
    share = TILE - TEXT_HEAD
    heads_t = share // TEXT_HEAD

    def self_forward_tile(z, carry):
        text_tiles = [text_sqkv[n, :, tile_at(z)] for n in range(3)]
        heads = pair_heads(
            lambda q, k, v: head_forward(q, k, v, mask_tt[...], TEXT_HEAD), heads_t, *text_tiles
        )
        blank = jnp.zeros((rows_t, TEXT_HEAD), bf16)
        text_extra[z] = jnp.concatenate([blank] + heads, -1)
        context = jnp.concatenate(heads + [blank], -1)
        text_acc[...] += dot_nt(context, self_t[3 * width_t : 4 * width_t, tile_at(z)])
        image_tiles = [image_sqkv[n, :, tile_at(z)] for n in range(3)]
        image_heads = pair_heads(
            lambda q, k, v: head_forward(q, k, v, mask_ii[...], IMAGE_HEAD), 2, *image_tiles
        )
        image_context = jnp.concatenate(image_heads, -1)
        image_right[9, z] = image_context
        image_acc[...] += dot_nn(image_context, out_i[tile_at(z), 0:width_i])
        return carry

    lax.fori_loop(0, zs, self_forward_tile, 0)
    norm_forward(2, text_output, text_acc, text_xhat, text_rstd, text_gains, text_shifts, None)
    norm_forward(2, image_output, image_acc, image_xhat, image_rstd, image_gains, image_shifts, None)

    text_grad[...] = text_cot[...].astype(f32)
    image_grad[...] = image_cot[...].astype(f32)
    norm_backward(2, text_grad, None, text_xhat, text_rstd, text_gains, text_rows.at[4], text_norms)
    norm_backward(2, image_grad, None, image_xhat, image_rstd, image_gains, image_rows.at[4], image_norms)
    clear()

    def self_back_tile(z, carry):
        text_tiles = [text_sqkv[n, :, tile_at(z)] for n in range(3)]
        context_grad = dot_nt_rows(text_rows[4], self_t, z)
        grads = pair_heads(
            lambda q, k, v, d: head_back(q, k, v, mask_tt[...], TEXT_HEAD, d),
            heads_t, *text_tiles, context_grad,
        )
        blank = jnp.zeros((rows_t, TEXT_HEAD), bf16)
        dq, dk, dv = [[grads[h][n] for h in range(heads_t)] for n in range(3)]
        pieces = dq + dk + dv
        text_right[10, z] = jnp.concatenate(pieces[0:4], -1)
        text_right[11, z] = jnp.concatenate(pieces[4:8], -1)
        text_right[12, z] = jnp.concatenate(pieces[8:9] + [blank] * 3, -1)
        joined = [jnp.concatenate(parts + [blank], -1) for parts in (dq, dk, dv)]
        text_acc[...] += joint_nt(joined, self_t, width_t, z)
        return carry

    def dot_nt_rows(coming, weights, z):
        return dot_nn(coming, weights[3 * width_t : 4 * width_t, tile_at(z)]).astype(bf16)

    def self_back_image(z, carry):
        image_tiles = [image_sqkv[n, :, tile_at(z)] for n in range(3)]
        context_grad = dot_nt(image_rows[4], out_i[tile_at(z), 0:width_i]).astype(bf16)
        grads = pair_heads(
            lambda q, k, v, d: head_back(q, k, v, mask_ii[...], IMAGE_HEAD, d),
            2, *image_tiles, context_grad,
        )
        joined = [jnp.concatenate([grads[0][n], grads[1][n]], -1) for n in range(3)]
        for n in range(3):
            image_right[6 + n, z] = joined[n]
        image_acc[...] += joint_nt(joined, self_i, width_i, z)
        return carry

    lax.fori_loop(0, zs, self_back_image, 0, unroll=2)
    start(9)
    lax.fori_loop(0, zs, self_back_tile, 0, unroll=2)
    start(10)
    start(11)
    norm_backward(1, text_grad, text_acc, text_xhat, text_rstd, text_gains, text_rows.at[3], text_norms)
    norm_backward(1, image_grad, image_acc, image_xhat, image_rstd, image_gains, image_rows.at[3], image_norms)
    clear()

    back_down = ready(9)

    def text_down_back(j, carry):
        middle_grad = dot_nt(text_rows[3], back_down[tile_at(j), 0:width_t])
        text_right[4 + j % ups, j // ups] = (middle_grad * text_slope[j]).astype(bf16)
        return carry

    lax.fori_loop(0, zs * ups, text_down_back, 0, unroll=2)
    start(12)
    back_i = ready(10)

    def image_ffn_back(z, carry):
        offset = pl.ds(pl.multiple_of(width_i + z * TILE, TILE), TILE)
        middle_grad = dot_nt(image_rows[3], back_i[offset, 0:width_i])
        upper_grad = (middle_grad * image_slope[z]).astype(bf16)
        image_right[4, z] = upper_grad
        image_acc[...] += dot_nt(upper_grad, back_i[0:width_i, tile_at(z)])
        return carry

    lax.fori_loop(0, zs, image_ffn_back, 0, unroll=2)
    start(13)
    back_up = ready(11)

    def text_up_back(j, carry):
        joined = jnp.concatenate([text_right[4 + part, j] for part in range(ups)], -1)
        rows = pl.ds(pl.multiple_of(j * width_t, 8), width_t)
        text_acc[...] += dot_nt(joined, back_up[rows, 0 : ups * TILE])
        return carry

    lax.fori_loop(0, zs, text_up_back, 0)
    start(14)
    norm_backward(0, text_grad, text_acc, text_xhat, text_rstd, text_gains, text_rows.at[2], text_norms)
    norm_backward(0, image_grad, image_acc, image_xhat, image_rstd, image_gains, image_rows.at[2], image_norms)
    clear()

    back_out = ready(12)
    cross_t = ready(13)
    cross_i = ready(14)

    def cross_back_tile(z, carry):
        tq, tk, tv = [text_qkv[n, :, tile_at(z)] for n in range(3)]
        iq, ik, iv = [image_qkv[n, :, tile_at(z)] for n in range(3)]
        text_ctx_grad = dot_nt(text_rows[2], back_out[tile_at(z), 0:width_t]).astype(bf16)
        offset = pl.ds(pl.multiple_of(inner + z * TILE, TILE), TILE)
        image_ctx_grad = dot_nt(image_rows[2], back_out[offset, 0:width_i]).astype(bf16)
        text_side = pair_heads(
            lambda q, k, v, d: head_back(q, k, v, mask_ti[...], CROSS_HEAD, d), 2, tq, ik, iv, text_ctx_grad
        )
        image_side = pair_heads(
            lambda q, k, v, d: head_back(q, k, v, mask_it[...], CROSS_HEAD, d), 2, iq, tk, tv, image_ctx_grad
        )

        def joined(side, n):
            return jnp.concatenate([side[0][n], side[1][n]], -1)

        text_parts = (joined(text_side, 0), joined(image_side, 1), joined(image_side, 2))
        image_parts = (joined(image_side, 0), joined(text_side, 1), joined(text_side, 2))
        for n in range(3):
            text_right[n, z] = text_parts[n]
            image_right[n, z] = image_parts[n]
        text_acc[...] += joint_nt(text_parts, cross_t, width_t, z)
        image_acc[...] += joint_nt(image_parts, cross_i, width_i, z)
        return carry

    lax.fori_loop(0, zs, cross_back_tile, 0, unroll=2)
    text_grad[...] += text_acc[...]
    image_grad[...] += image_acc[...]
    finish()
    for left, rows in ((text_left, text_rows), (image_left, image_rows)):
        turn_over(left, ((1, rows.at[2]), (3, rows.at[3]), (5, rows.at[4])))


def layer(lengths, counts, rows, params, weights, mp, unit):
    f32, bf16 = jnp.float32, jnp.bfloat16
    text_tokens, image_tokens = rows[0], rows[1]
    rows_t, width_t = text_tokens.shape
    rows_i, width_i = image_tokens.shape
    text_tiles = mp * weights[4].shape[2] // TILE
    inner = mp * TILE

    vmem = pl.BlockSpec(memory_space=pltpu.VMEM)
    out_shape = [
        jax.ShapeDtypeStruct((rows_t, width_t), f32),
        jax.ShapeDtypeStruct((rows_i, width_i), f32),
        jax.ShapeDtypeStruct((rows_t, width_t), f32),
        jax.ShapeDtypeStruct((rows_i, width_i), f32),
        jax.ShapeDtypeStruct((2, 6, 2, 2, width_t // 8, rows_t), bf16),
        jax.ShapeDtypeStruct((2, 6, 2, 2, width_i // 8, rows_i), bf16),
        jax.ShapeDtypeStruct((13, mp, rows_t, TILE), bf16),
        jax.ShapeDtypeStruct((mp, rows_t, TILE), bf16),
        jax.ShapeDtypeStruct((10, mp, rows_i, TILE), bf16),
        jax.ShapeDtypeStruct((2 * params[0].shape[0], width_t), f32),
        jax.ShapeDtypeStruct((2 * params[0].shape[0], width_i), f32),
    ]
    fulls = []
    for array, kind in zip(weights, KINDS):
        shape = array.shape[:-1] + (mp * array.shape[-1],) if kind == "cols" else (mp * array.shape[0], array.shape[1])
        fulls.append(jax.ShapeDtypeStruct(shape, bf16))
    chunks = len(SEQUENCE)
    results = pl.pallas_call(
        functools.partial(layer_kernel, unit),
        out_shape=out_shape + fulls,
        in_specs=[pl.BlockSpec(memory_space=pltpu.SMEM)] * 2
        + [vmem] * 8
        + [pl.BlockSpec(memory_space=pl.ANY)] * len(weights),
        out_specs=[vmem] * len(out_shape) + [pl.BlockSpec(memory_space=pl.ANY)] * len(fulls),
        scratch_shapes=[
            pltpu.SemaphoreType.DMA((chunks, 12)),
            pltpu.SemaphoreType.DMA((chunks, 12)),
            pltpu.VMEM((3, 3 * width_i, inner), bf16),
            pltpu.SemaphoreType.DMA((15, 4 * mp)),
            pltpu.VMEM((rows_t, width_t), f32),
            pltpu.VMEM((rows_i, width_i), f32),
            pltpu.VMEM((3, rows_t, width_t), f32),
            pltpu.VMEM((3, rows_i, width_i), f32),
            pltpu.VMEM((3, rows_t, 128), f32),
            pltpu.VMEM((3, rows_i, 128), f32),
            pltpu.VMEM((text_tiles, rows_t, TILE), f32),
            pltpu.VMEM((mp, rows_i, TILE), f32),
            pltpu.VMEM((3, rows_t, inner), bf16),
            pltpu.VMEM((3, rows_i, inner), bf16),
            pltpu.VMEM((3, rows_t, inner), bf16),
            pltpu.VMEM((3, rows_i, inner), bf16),
            pltpu.VMEM((rows_t, rows_i), f32),
            pltpu.VMEM((rows_i, rows_t), f32),
            pltpu.VMEM((rows_t, rows_t), f32),
            pltpu.VMEM((rows_i, rows_i), f32),
            pltpu.VMEM((5, rows_t, width_t), bf16),
            pltpu.VMEM((5, rows_i, width_i), bf16),
        ],
        compiler_params=pltpu.CompilerParams(
            collective_id=0, has_side_effects=True, vmem_limit_bytes=67043328
        ),
        name="layer",
    )(lengths, counts, *rows, *params, *weights)
    return results[: len(out_shape)]


def shards(
    text_tokens, image_regions, lengths, region_counts, text_cross, image_cross, text_cross_out,
    image_cross_out, text_up, text_down, image_up, image_down, text_self, text_self_out, image_self,
    image_self_out, text_gains, text_shifts, image_gains, image_shifts, text_cotangent, image_cotangent,
):
    mp, dp = lax.axis_size("mp"), lax.axis_size("dp")
    more = dp // 8
    text_out_turned = text_self_out.T[None]
    text_four = jnp.concatenate([text_self, text_out_turned])
    spare = 256 - text_four.shape[-1]
    text_four = jnp.pad(text_four, ((0, 0), (0, 0), (0, spare)))
    weights = (
        text_cross, image_cross, text_cross_out, image_cross_out, text_up[None], text_down,
        image_up[None], image_down, text_four, image_self, image_self_out,
    )
    pairs, regions = image_regions.shape[0], image_regions.shape[1]
    padding = (-regions) % 16

    def pad_regions(array):
        return jnp.pad(array, ((0, 0), (0, padding), (0, 0))).reshape(-1, array.shape[-1])

    def flat(array):
        return array.reshape(-1, array.shape[-1])

    (
        text_result, image_result, text_input_grad, image_input_grad,
        text_left, image_left, text_right, text_extra, image_right, text_norms, image_norms,
    ) = layer(
        lengths, region_counts,
        (flat(text_tokens), pad_regions(image_regions), flat(text_cotangent), pad_regions(image_cotangent)),
        (text_gains, text_shifts, image_gains, image_shifts),
        weights, mp, more,
    )
    text_result, text_input_grad = [
        array.reshape(text_tokens.shape) for array in (text_result, text_input_grad)
    ]
    image_result, image_input_grad = [
        array.reshape(pairs, regions + padding, -1)[:, :regions]
        for array in (image_result, image_input_grad)
    ]
    norms = jnp.concatenate([text_norms.reshape(-1, 128), image_norms.reshape(-1, 128)])
    text_sums, image_sums, norm_sums = reduce_all(
        text_left, text_right, text_extra, image_left, image_right, norms, more
    )
    if more > 1:
        norm_sums = lax.psum(norm_sums, "dp") / 8
        text_sums, image_sums = outer_sum(text_sums, more), outer_sum(image_sums, more)

    def wide(sums, first, last):
        return jnp.concatenate([sums[n] for n in range(first, last)], -1)

    share, ups = text_self.shape[-1], text_up.shape[-1] // 256
    selfs = wide(text_sums, 4 + 2 * ups, text_sums.shape[0])
    text_parts = [text_sums[0:3], text_sums[3], wide(text_sums, 4, 4 + ups), wide(text_sums, 4 + ups, 4 + 2 * ups)]
    text_parts += [jnp.stack([selfs[:, n * share : (n + 1) * share] for n in range(3)]), selfs[:, 3 * share :]]
    image_parts = [image_sums[0:3], image_sums[3], image_sums[4], image_sums[5], image_sums[6:9], image_sums[9]]
    flat_norms = norm_sums.reshape(-1)
    text_size, image_size = text_gains.size, image_gains.size
    text_end = 2 * text_size
    return (
        text_result,
        image_result,
        text_input_grad,
        image_input_grad,
        text_parts[0],
        image_parts[0],
        text_parts[1].T,
        image_parts[1].T,
        text_parts[2],
        text_parts[3].T,
        image_parts[2],
        image_parts[3].T,
        text_parts[4],
        text_parts[5].T,
        image_parts[4],
        image_parts[5].T,
        flat_norms[:text_size].reshape(text_gains.shape),
        flat_norms[text_size:text_end].reshape(text_shifts.shape),
        flat_norms[text_end : text_end + image_size].reshape(image_gains.shape),
        flat_norms[text_end + image_size :].reshape(image_shifts.shape),
    )


def outer_sum(sums, more):
    chunks, rows, width = sums.shape
    apart = sums.reshape(chunks, 1, more, rows // more, width)
    low = lax.axis_index("dp") // more
    spread = jnp.zeros((chunks, 8, more, rows // more, width), sums.dtype)
    spread = lax.dynamic_update_slice(spread, apart, (0, low, 0, 0, 0))
    spread = spread.reshape(chunks, 8 * rows, width)
    return lax.psum_scatter(spread, "dp", scatter_dimension=1, tiled=True)


def solution(mesh):
    in_specs = (
        P(("dp", "mp"), None, None),
        P(("dp", "mp"), None, None),
        P(("dp", "mp")),
        P(("dp", "mp")),
        P(None, None, "mp"),
        P(None, None, "mp"),
        P("mp", None),
        P("mp", None),
        P(None, "mp"),
        P("mp", None),
        P(None, "mp"),
        P("mp", None),
        P(None, None, "mp"),
        P("mp", None),
        P(None, None, "mp"),
        P("mp", None),
        P(),
        P(),
        P(),
        P(),
        P(("dp", "mp"), None, None),
        P(("dp", "mp"), None, None),
    )
    out_specs = (
        P(("dp", "mp"), None, None),
        P(("dp", "mp"), None, None),
        P(("dp", "mp"), None, None),
        P(("dp", "mp"), None, None),
        P(None, "dp", "mp"),
        P(None, "dp", "mp"),
        P("mp", "dp"),
        P("mp", "dp"),
        P("dp", "mp"),
        P("mp", "dp"),
        P("dp", "mp"),
        P("mp", "dp"),
        P(None, "dp", "mp"),
        P("mp", "dp"),
        P(None, "dp", "mp"),
        P("mp", "dp"),
        P(),
        P(),
        P(),
        P(),
    )
    return jax.shard_map(shards, mesh=mesh, in_specs=in_specs, out_specs=out_specs, check_vma=False)
```
